32 devices in a mesh: gx: 4 (over y, core), gy: 8 (over z, x).
Axes of the slice: x: 2, y: 2, z: 4, core: 2. Of those that a mesh axis runs over, the one named last changes fastest.
Arguments:
- eps_field: bfloat16 [48, 256, 1024], P(None, 'gx', 'gy'), may hold values from 1 to 10
- charge: float32 [48, 256, 1024], P(None, 'gx', 'gy'), may hold values from -6 to 6
- potential_start: float32 [48, 256, 1024], P(None, 'gx', 'gy'), may hold values from -3 to 3
- colloid_vel: float32 [3, 1024], P(None, ('gx', 'gy')), may hold values from -0.3 to 0.3
- colloid_spin: float32 [3, 1024], P(None, ('gx', 'gy')), may hold values from -0.06 to 0.06
- link_dir: int32 [4, 8, 32768], P('gx', 'gy'), may hold values from 0 to 17
- link_colloid: int32 [4, 8, 32768], P('gx', 'gy'), may hold values from -1 to 1023, as said below
- link_site: int32 [4, 8, 32768], P('gx', 'gy'), may hold values from 0 to 8191
- link_depth: int32 [4, 8, 32768], P('gx', 'gy'), may hold values from 0 to 47
- link_pop: float32 [4, 8, 32768], P('gx', 'gy'), may hold values from -0.1 to 0.1
- link_rb: float32 [3, 4, 8, 32768], P(None, 'gx', 'gy'), may hold values from -9 to 9
Outputs:
- potential: float32 [48, 256, 1024], P(None, 'gx', 'gy')
- force_torque: float32 [6, 1024], P(None, ('gx', 'gy'))
- link_out: float32 [4, 8, 32768], P('gx', 'gy')
The draws below stay inside these ranges and needn't reach their ends.
Inputs may be any that keep to these rules, and one draw needn't show every extreme that they name: `link_colloid`: an empty slot holds -1 and the live slots of a tile come first; at least 16384 slots of every tile are live and every slot of at least one tile. The tile with index i along gx and j along gy owns the colloids (i n + j) * 32 up to (i n + j + 1) * 32 - 1, where n is the number of tiles along gy; a live slot names a colloid owned by its own tile or by one of the eight tiles beside it, wrapping around.
All inputs are finite; a program needn't handle non-finite values.
Results may differ from the reference program's by a relative error of at most 0.0003.
Values may be sent and summed in bfloat16 or wider, within the bound.
No kernel may reach another device: no remote copies, remote signals or barrier semaphores. Data moves between devices by JAX's collectives and lax.ppermute only.
A program may use at most 128 MiB of HBM per device.

```python
import math
import jax
import jax.numpy as jnp
import numpy as np
from jax import lax

NZ = 48
TX = 64
TY = 128
NC_DEV = 32
LINKS = 32768
SWEEPS = 6
RADIUS = 8
TILES_X = 4
TILES_Y = 8
NX = 256
NY = 1024
NC = 1024


def draw_link_colloid(key, part):
    base = jax.random.fold_in(key, 4711)
    key_live, key_full, key_stepx, key_stepy, key_slot = jax.random.split(base, 5)
    tile_count = TILES_X * TILES_Y
    live_count = jax.random.randint(key_live, (tile_count,), LINKS // 2, LINKS + 1)
    full_tile = jax.random.randint(key_full, (), 0, tile_count)
    tile_index = jnp.arange(tile_count, dtype=jnp.int32)
    live_count = jnp.where(tile_index == full_tile, LINKS, live_count)
    step_x = jax.random.randint(key_stepx, (tile_count, LINKS), -1, 2)
    step_y = jax.random.randint(key_stepy, (tile_count, LINKS), -1, 2)
    slot_index = jax.random.randint(key_slot, (tile_count, LINKS), 0, NC_DEV)
    home_x = (tile_index // TILES_Y)[:, None]
    home_y = (tile_index % TILES_Y)[:, None]
    owner = (home_x + step_x) % TILES_X * TILES_Y + (home_y + step_y) % TILES_Y
    colloid_ids = owner * NC_DEV + slot_index
    position = jnp.arange(LINKS, dtype=jnp.int32)[None, :]
    colloid_ids = jnp.where(position < live_count[:, None], colloid_ids, -1)
    return colloid_ids.reshape(TILES_X, TILES_Y, LINKS).astype(jnp.int32)


def with_ends(drawn, own_key, smallest, top_value):
    spot = [jax.random.randint(jax.random.fold_in(own_key, axis), (), 0, length) for axis, length in enumerate(drawn.shape)]
    widest = drawn.shape.index(max(drawn.shape))
    neighbour = spot[:widest] + [(spot[widest] + 1) % drawn.shape[widest]] + spot[widest + 1:]
    return drawn.at[tuple(spot)].set(smallest).at[tuple(neighbour)].set(top_value)


def level_of(rng, shape, pieces, low, top_value):
    def one(dim, blocks):
        heights = jax.random.uniform(jax.random.fold_in(jax.random.fold_in(rng, 6), dim), (blocks,), jnp.float32, low / len(pieces), top_value / len(pieces))
        return jnp.repeat(jnp.exp(heights), shape[dim] // blocks).reshape((-1,) + (1,) * (len(shape) - dim - 1))

    level = one(*pieces[0])
    for cut in pieces[1:]:
        level = level * one(*cut)
    return level


def normal_values(key, extent, width, reach, pieces=(), kind=jnp.bfloat16):
    level = level_of(key, extent, pieces, -0.22, 0.18) if pieces else 1.0
    result = jax.random.normal(key, extent, jnp.float32) * width * level
    return jnp.minimum(jnp.maximum(result, -reach), reach).astype(kind)


def setup_inputs(seed: int = 0) -> dict:
    arg_keys = jax.random.split(jax.random.key(seed), 12)
    return {
        "eps_field": jnp.clip(jnp.exp(math.log(10.0) - 2.3025851 * jax.random.uniform(arg_keys[0], (NZ, NX, NY), jnp.float32) ** level_of(arg_keys[0], (NZ, NX, NY), ((1, 4), (2, 8)), -0.2, 0.2)), 1.0, 10.0).astype(jnp.bfloat16),
        "charge": normal_values(arg_keys[1], (NZ, NX, NY), 1.0, 6.0, ((1, 4), (2, 8)), jnp.float32),
        "potential_start": normal_values(arg_keys[2], (NZ, NX, NY), 0.5, 3.0, ((1, 4), (2, 8)), jnp.float32),
        "colloid_vel": normal_values(arg_keys[3], (3, NC), 0.05, 0.3, ((1, 32),), jnp.float32),
        "colloid_spin": normal_values(arg_keys[4], (3, NC), 0.01, 0.06, ((1, 32),), jnp.float32),
        "link_dir": with_ends(jax.random.randint(arg_keys[5], (TILES_X, TILES_Y, LINKS), 0, 18), jax.random.fold_in(arg_keys[5], 1), 0, 17).astype(jnp.int32),
        "link_colloid": draw_link_colloid(jax.random.fold_in(arg_keys[11], 71), 0),
        "link_site": with_ends(jax.random.randint(arg_keys[7], (TILES_X, TILES_Y, LINKS), 0, TX * TY), jax.random.fold_in(arg_keys[7], 1), 0, (TX * TY) - 1).astype(jnp.int32),
        "link_depth": with_ends(jax.random.randint(arg_keys[8], (TILES_X, TILES_Y, LINKS), 0, NZ), jax.random.fold_in(arg_keys[8], 1), 0, NZ - 1).astype(jnp.int32),
        "link_pop": normal_values(arg_keys[9], (TILES_X, TILES_Y, LINKS), 0.015625, 0.1, ((0, 4), (1, 8)), jnp.float32),
        "link_rb": jnp.clip(jax.random.uniform(arg_keys[10], (3, TILES_X, TILES_Y, LINKS), jnp.float32, -9.0, 9.0) * level_of(arg_keys[10], (3, TILES_X, TILES_Y, LINKS), ((1, 4), (2, 8)), -0.4, 0.0), -9.0, 9.0),
    }


velocity_table = np.array([[1, 0, 0], [-1, 0, 0], [0, 1, 0], [0, -1, 0], [0, 0, 1], [0, 0, -1], [1, 1, 0], [1, -1, 0], [-1, 1, 0], [-1, -1, 0], [1, 0, 1], [1, 0, -1], [-1, 0, 1], [-1, 0, -1], [0, 1, 1], [0, 1, -1], [0, -1, 1], [0, -1, -1]], dtype=np.float32).T
weight_table = np.array([1.0 / 18.0] * 6 + [1.0 / 36.0] * 12, dtype=np.float32)
OVER_RELAX = 1.6


def lattice_lookup(directions):
    onehot = (directions[None, :] == jnp.arange(18, dtype=jnp.int32)[:, None]).astype(jnp.float32)
    velocity = jnp.dot(jnp.asarray(velocity_table).astype(jnp.float32), onehot, precision=lax.Precision.HIGHEST)
    weight = jnp.dot(jnp.asarray(weight_table).astype(jnp.float32)[None, :], onehot, precision=lax.Precision.HIGHEST)[0]
    return velocity, weight


def cross_product(first, second):
    return jnp.stack([first[1] * second[2] - first[2] * second[1], first[2] * second[0] - first[0] * second[2], first[0] * second[1] - first[1] * second[0]])


def link_terms(pops, velocity, weight, valid, offsets, at_links, pressure):
    boundary = at_links[0:3] + cross_product(at_links[3:6], offsets)
    along = jnp.sum(velocity * boundary, axis=0)
    transfer = (2.0 * pops - 6.0 * weight * along + weight * pressure) * valid
    force = velocity * transfer[None, :]
    torque = cross_product(offsets, force)
    return jnp.concatenate([force, torque], axis=0)


def reflected(pops, velocity, weight, valid, offsets, at_links):
    boundary = at_links[0:3] + cross_product(at_links[3:6], offsets)
    along = jnp.sum(velocity * boundary, axis=0)
    return pops - 6.0 * weight * along * valid


def owner_update(motion, sums):
    mass = 4.0 / 3.0 * math.pi * RADIUS ** 3
    inertia = 0.4 * mass * RADIUS ** 2
    new_motion = jnp.concatenate([motion[0:3] + sums[0:3] / mass, motion[3:6] + sums[3:6] / inertia], axis=0)
    report = jnp.concatenate([sums[0:3], sums[3:6] / RADIUS], axis=0)
    return new_motion, report


def relax_colour(phi_pad, eps_pad, charge, colour_mask):
    eps_slab = jnp.pad(eps_pad, ((1, 1), (0, 0), (0, 0)), mode="edge")
    padded = jnp.pad(phi_pad, ((1, 1), (0, 0), (0, 0)))
    eps_centre = eps_slab[1:-1, 1:-1, 1:-1]
    centre = padded[1:-1, 1:-1, 1:-1]
    eps_sides = [eps_slab[:-2, 1:-1, 1:-1], eps_slab[2:, 1:-1, 1:-1], eps_slab[1:-1, :-2, 1:-1], eps_slab[1:-1, 2:, 1:-1], eps_slab[1:-1, 1:-1, :-2], eps_slab[1:-1, 1:-1, 2:]]
    phi_sides = [padded[:-2, 1:-1, 1:-1], padded[2:, 1:-1, 1:-1], padded[1:-1, :-2, 1:-1], padded[1:-1, 2:, 1:-1], padded[1:-1, 1:-1, :-2], padded[1:-1, 1:-1, 2:]]
    numerator = charge
    denominator = jnp.zeros_like(charge)
    for eps_side, phi_side in zip(eps_sides, phi_sides):
        face = 0.5 * (eps_centre + eps_side)
        numerator = numerator + face * phi_side
        denominator = denominator + face
    target = numerator / denominator
    return jnp.where(colour_mask, centre + OVER_RELAX * (target - centre), centre)


def reference(eps_field, charge, potential_start, colloid_vel, colloid_spin, link_dir, link_colloid, link_site, link_depth, link_pop, link_rb):
    eps_whole = eps_field.astype(jnp.float32)
    eps_pad = jnp.pad(eps_whole, ((0, 0), (1, 1), (1, 1)), mode="wrap")
    shape = charge.shape
    parity = (lax.broadcasted_iota(jnp.int32, shape, 0) + lax.broadcasted_iota(jnp.int32, shape, 1) + lax.broadcasted_iota(jnp.int32, shape, 2)) % 2
    potential = potential_start
    for sweep_index in range(SWEEPS):
        for colour in (0, 1):
            phi_pad = jnp.pad(potential, ((0, 0), (1, 1), (1, 1)), mode="wrap")
            potential = relax_colour(phi_pad, eps_pad, charge, parity == colour)

    phi_flat = potential.reshape(-1)
    eps_flat = eps_whole.reshape(-1)
    motion = jnp.concatenate([colloid_vel, colloid_spin], axis=0)
    motion_rows = motion.T
    tile_count = TILES_X * TILES_Y
    dirs_all = link_dir.reshape(tile_count, LINKS)
    ids_all = link_colloid.reshape(tile_count, LINKS)
    sites_all = link_site.reshape(tile_count, LINKS)
    depths_all = link_depth.reshape(tile_count, LINKS)
    pops_all = link_pop.reshape(tile_count, LINKS)
    offsets_all = link_rb.reshape(3, tile_count, LINKS).transpose(1, 0, 2)
    tile_ids = jnp.arange(tile_count, dtype=jnp.int32)

    def tile_sum(total, inputs):
        tile, directions, colloid_ids, sites, depth, pops, offsets = inputs
        velocity, weight = lattice_lookup(directions)
        valid_mask = colloid_ids >= 0
        valid = valid_mask.astype(jnp.float32)
        row = sites // TY + (tile // TILES_Y) * TX
        column = sites % TY + (tile % TILES_Y) * TY
        place = ((depth * NX + row) * NY + column).astype(jnp.int32)
        phi_here = jnp.take(phi_flat, place)
        pressure = 0.5 * jnp.take(eps_flat, place) * phi_here * phi_here
        at_links = jnp.take(motion_rows, jnp.where(valid_mask, colloid_ids, 0), axis=0).T
        terms = link_terms(pops, velocity, weight, valid, offsets, at_links, pressure)
        target = jnp.where(valid_mask, colloid_ids, NC).astype(jnp.int32)
        partial_value = jax.ops.segment_sum(terms.T, target, num_segments=NC + 1)[:NC]
        return total + partial_value, jnp.zeros((), jnp.float32)

    sums_rows = lax.scan(tile_sum, jnp.zeros((NC, 6), jnp.float32), (tile_ids, dirs_all, ids_all, sites_all, depths_all, pops_all, offsets_all))[0]
    new_motion, report = owner_update(motion, sums_rows.T)
    moved_rows = new_motion.T

    def tile_out(inputs):
        directions, colloid_ids, pops, offsets = inputs
        velocity, weight = lattice_lookup(directions)
        valid_mask = colloid_ids >= 0
        valid = valid_mask.astype(jnp.float32)
        at_links = jnp.take(moved_rows, jnp.where(valid_mask, colloid_ids, 0), axis=0).T
        return reflected(pops, velocity, weight, valid, offsets, at_links)

    link_out = lax.map(tile_out, (dirs_all, ids_all, pops_all, offsets_all)).reshape(TILES_X, TILES_Y, LINKS)
    return potential, report, link_out
```

```python
import functools
import math

import jax
import jax.numpy as jnp
import numpy as np
from jax import lax
from jax.experimental import pallas as pl
from jax.experimental.pallas import tpu as pltpu
from jax.sharding import PartitionSpec as P

SWEEPS = 6
RADIUS = 8
OVER_RELAX = 1.6
HALO = 2 * SWEEPS
FIRST = 16
MARGIN = 8
GROUPS = 5
SLOT = 2 * HALO
KEY_BITS = 13
F32 = jnp.float32

VELOCITY = np.array(
    [
        [1, 0, 0], [-1, 0, 0], [0, 1, 0], [0, -1, 0], [0, 0, 1], [0, 0, -1],
        [1, 1, 0], [1, -1, 0], [-1, 1, 0], [-1, -1, 0], [1, 0, 1], [1, 0, -1],
        [-1, 0, 1], [-1, 0, -1], [0, 1, 1], [0, 1, -1], [0, -1, 1], [0, -1, -1],
    ],
    dtype=np.float32,
)
WEIGHT = np.array([1.0 / 18.0] * 6 + [1.0 / 36.0] * 12, dtype=np.float32)


def direction_table():
    table = np.zeros((4, 8, 128), np.float32)
    table[:3, :, :18] = VELOCITY.T[:, None, :]
    table[3, :, :18] = WEIGHT[None, :]
    return jnp.asarray(table)


PAIRS = [(a, b) for a in range(6) for b in range(a, 6)]


def lane_pick(table, index):
    return jnp.take_along_axis(table, index, axis=1, mode="promise_in_bounds")


def roll(value, shift):
    return pltpu.roll(value, shift % 128, 1)


def lanes_of(shape):
    return lax.broadcasted_iota(jnp.int32, shape, 1)


def parity_of(shape):
    rows = lax.broadcasted_iota(jnp.int32, shape, 0)
    return (rows + lanes_of(shape)) % 2 == 0


def pack_kernel(pot, charge, eps, low, high, split, to_right, to_left):
    depth, wide, _ = pot.shape
    layers = depth // 2
    last = FIRST + wide

    def build(k, carry):
        for f, field in enumerate((pot, charge, eps)):
            fill = 1.0 if f == 2 else 0.0
            parts = (
                (FIRST, field[2 * k].astype(F32), field[2 * k + 1].astype(F32)),
                (FIRST - HALO, low[f, 2 * k], low[f, 2 * k + 1]),
                (last, high[f, 2 * k], high[f, 2 * k + 1]),
            )
            for start, even, odd in parts:
                flat = parity_of(even.shape)
                count = even.shape[0]
                split[2 * f, k, start:start + count, :] = jnp.where(flat, even, odd)
                split[2 * f + 1, k, start:start + count, :] = jnp.where(flat, odd, even)
            spare = FIRST - HALO
            edge = jnp.full((spare, 128), fill, F32)
            for c in range(2):
                split[2 * f + c, k, 0:spare, :] = edge
                split[2 * f + c, k, last + HALO:last + HALO + spare, :] = edge
        return carry

    lax.fori_loop(0, layers, build, 0)
    for f in range(3):
        for c in range(2):
            split[2 * f + c, layers] = jnp.full(
                (split.shape[2], 128), 1.0 if f == 2 else 0.0, F32
            )

    rows = slice(FIRST - HALO, last + HALO)
    lane = lanes_of((wide + 2 * HALO, 128))

    def strips(n, carry):
        f = n // GROUPS
        i = n % GROUPS
        right = jnp.zeros((wide + 2 * HALO, 128), F32)
        left = jnp.zeros((wide + 2 * HALO, 128), F32)
        for g in range(GROUPS):
            red = split[2 * f, i + GROUPS * g, rows, :]
            black = split[2 * f + 1, i + GROUPS * g, rows, :]
            base = SLOT * g
            in_red = (lane >= base) & (lane < base + HALO)
            in_black = (lane >= base + HALO) & (lane < base + SLOT)
            right = jnp.where(in_red, roll(red, base + HALO), right)
            right = jnp.where(in_black, roll(black, base + SLOT), right)
            left = jnp.where(in_red, roll(red, base), left)
            left = jnp.where(in_black, roll(black, base + HALO), left)
        to_right[f, i] = right
        to_left[f, i] = left
        return carry

    lax.fori_loop(0, 3 * GROUPS, strips, 0)


def relax_kernel(split, from_left, from_right, pot_out, press_out, pa, ea, wa, pb, eb, cb, wb):
    layers = split.shape[1] - 1
    depth, wide, _ = pot_out.shape
    rows = split.shape[2]
    tiles = rows // 8
    top = MARGIN
    lane = lanes_of((8, 128))
    flat = parity_of((8, 128))
    at_0 = lane == 0
    at_127 = lane == 127
    in_slot = lane % SLOT
    in_left = in_slot < HALO
    slot_left = in_slot == HALO - 1
    slot_right = in_slot == HALO
    pick = [(lane == SLOT * g + HALO - 1) | (lane == SLOT * g + HALO) for g in range(GROUPS)]

    zero = jnp.zeros((rows + 2 * MARGIN, 128), F32)
    one = jnp.ones((rows + 2 * MARGIN, 128), F32)
    margin0 = jnp.zeros((MARGIN, 128), F32)
    margin1 = jnp.ones((MARGIN, 128), F32)
    for c in range(2):
        pa[c, 0] = zero
        ea[c, 0] = one
        ea[c, layers + 1] = one

    def load_core(k, carry):
        for c in range(2):
            pa[c, k + 1, 0:top, :] = margin0
            pa[c, k + 1, top:top + rows, :] = split[c, k]
            pa[c, k + 1, top + rows:, :] = margin0
            ea[c, k + 1, 0:top, :] = margin1
            ea[c, k + 1, top:top + rows, :] = split[4 + c, k]
            ea[c, k + 1, top + rows:, :] = margin1
        return carry

    lax.fori_loop(0, layers + 1, load_core, 0)
    for c in range(2):
        ea[c, 0, top:top + rows, :] = split[5 - c, 0]
        ea[c, layers + 1, top:top + rows, :] = split[5 - c, layers - 1]
        pa[c, layers + 2] = zero
        ea[c, layers + 2] = one

    first = FIRST - HALO
    high = wide + 2 * HALO
    wide_lane = lanes_of((high, 128))
    wide_left = wide_lane % SLOT < HALO
    wide_used = wide_lane < SLOT * GROUPS
    for c in range(2):
        for i in range(GROUPS + 2):
            pb[c, i] = zero
            eb[c, i] = one
        for i in range(GROUPS):
            cb[c, i] = jnp.zeros((rows, 128), F32)

    for f, target in enumerate((pb, cb, eb)):
        for i in range(GROUPS):
            west = from_left[f, i]
            east = from_right[f, i]
            red = jnp.where(wide_left, west, roll(east, HALO))
            black = jnp.where(wide_left, roll(west, -HALO), east)
            fill = 1.0 if f == 2 else 0.0
            red = jnp.where(wide_used, red, fill)
            black = jnp.where(wide_used, black, fill)
            if f == 1:
                target[0, i, first:first + high, :] = red
                target[1, i, first:first + high, :] = black
            else:
                target[0, i + 1, top + first:top + first + high, :] = red
                target[1, i + 1, top + first:top + first + high, :] = black

    all_lane = lanes_of((rows + 2 * MARGIN, 128))
    lead = all_lane < SLOT
    tail = all_lane >= SLOT * (GROUPS - 1)
    spare_slot = SLOT * (layers // GROUPS)
    in_spare = (all_lane >= spare_slot) & (all_lane < spare_slot + SLOT)

    def wrap_pot(c):
        pb[c, 0] = jnp.where(lead, 0.0, roll(pb[c, GROUPS], SLOT))
        pb[c, GROUPS + 1] = jnp.where(tail, 0.0, roll(pb[c, 1], -SLOT))

    spare_row = layers % GROUPS + 1
    for c in range(2):
        wrap_pot(c)
        eb[c, spare_row] = jnp.where(in_spare, eb[1 - c, spare_row - 1], eb[c, spare_row])
    for c in range(2):
        eb[c, 0] = jnp.where(lead, eb[1 - c, 1], roll(eb[c, GROUPS], SLOT))
        eb[c, GROUPS + 1] = jnp.where(tail, 1.0, roll(eb[c, 1], -SLOT))

    def around(src_a, src_b, other, color, i, t, body_a, body_b):
        r0 = top + 8 * t
        rs = slice(r0, r0 + 8)
        rm = slice(r0 - 1, r0 + 7)
        rp = slice(r0 + 1, r0 + 9)
        up = ~flat if color == 0 else flat
        side = src_b[other, i + 1, rs, :]
        edge = side
        for g in range(GROUPS):
            k = i + GROUPS * g
            here = src_a[other, k + 1, rs, :]
            halo = roll(side, -(SLOT * g + HALO))
            body_a(k, (
                here,
                jnp.where(up, src_a[other, k + 2, rs, :], src_a[other, k, rs, :]),
                src_a[other, k + 1, rm, :],
                src_a[other, k + 1, rp, :],
                roll(jnp.where(at_127, halo, here), 1),
                roll(jnp.where(at_0, halo, here), -1),
            ))
            if body_b is not None:
                edge = jnp.where(pick[g], roll(here, SLOT * g + HALO), edge)
        if body_b is not None:
            body_b((
                side,
                jnp.where(up, src_b[other, i + 2, rs, :], src_b[other, i, rs, :]),
                src_b[other, i + 1, rm, :],
                src_b[other, i + 1, rp, :],
                roll(jnp.where(slot_left, edge, side), 1),
                roll(jnp.where(slot_right, edge, side), -1),
            ))

    def coefficients(own, charge, sides):
        faces = [0.5 * (own + side) for side in sides]
        total = faces[0] + faces[1] + faces[2] + faces[3] + faces[4] + faces[5]
        scale = OVER_RELAX / total
        return [face * scale for face in faces] + [charge * scale]

    for c in range(2):
        def set_up(i, carry, c=c):
            for t in range(tiles):
                ts = slice(8 * t, 8 * t + 8)
                ps = slice(top + 8 * t, top + 8 * t + 8)

                def body_a(k, sides):
                    values = coefficients(ea[c, k + 1, ps, :], split[2 + c, k, ts, :], sides)
                    for n, value in enumerate(values):
                        wa[c, n, k, ts, :] = value

                def body_b(sides):
                    values = coefficients(eb[c, i + 1, ps, :], cb[c, i, ts, :], sides)
                    live = in_spare[0:8] & (i + 1 == spare_row)
                    for n, value in enumerate(values):
                        wb[c, n, i, ts, :] = jnp.where(live, 0.0, value)

                around(ea, eb, 1 - c, c, i, t, body_a, body_b)
            return carry

        lax.fori_loop(0, GROUPS, set_up, 0)
        for n in range(7):
            wa[c, n, layers] = jnp.zeros((rows, 128), F32)

    def combine(own, w, sides):
        left = w[0] * sides[0] + w[1] * sides[1]
        mid = w[2] * sides[2] + w[3] * sides[3]
        right = w[4] * sides[4] + w[5] * sides[5]
        return (w[6] - (OVER_RELAX - 1.0) * own) + (left + (mid + right))

    for step in range(2 * SWEEPS):
        c = step % 2
        reach = HALO - 1 - step
        t_low = (FIRST - reach) // 8
        t_high = -(-(FIRST + wide + reach) // 8)

        def half(i, carry, c=c, reach=reach, t_low=t_low, t_high=t_high):
            for t in range(t_low, t_high):
                ts = slice(8 * t, 8 * t + 8)
                ps = slice(top + 8 * t, top + 8 * t + 8)

                def body_a(k, sides):
                    w = [wa[c, n, k, ts, :] for n in range(7)]
                    pa[c, k + 1, ps, :] = combine(pa[c, k + 1, ps, :], w, sides)

                def body_b(sides):
                    w = [wb[c, n, i, ts, :] for n in range(7)]
                    pb[c, i + 1, ps, :] = combine(pb[c, i + 1, ps, :], w, sides)

                around(pa, pb, 1 - c, c, i, t, body_a, body_b if reach else None)
            return carry

        lax.fori_loop(0, GROUPS, half, 0)
        if reach:
            wrap_pot(c)

    core = slice(top + FIRST, top + FIRST + wide)
    core_flat = parity_of((wide, 128))

    def finish(k, carry):
        red, black = pa[0, k + 1, core, :], pa[1, k + 1, core, :]
        e_red, e_black = ea[0, k + 1, core, :], ea[1, k + 1, core, :]
        q_red = 0.5 * e_red * red * red
        q_black = 0.5 * e_black * black * black
        pot_out[2 * k] = jnp.where(core_flat, red, black)
        pot_out[2 * k + 1] = jnp.where(core_flat, black, red)
        press_out[2 * k] = jnp.where(core_flat, q_red, q_black)
        press_out[2 * k + 1] = jnp.where(core_flat, q_black, q_red)
        return carry

    lax.fori_loop(0, layers, finish, 0)


def geometry(direction, offsets, table):
    c0, c1, c2, w = [lane_pick(table[n], direction) for n in range(4)]
    r0, r1, r2 = offsets
    arms = [c0, c1, c2, r1 * c2 - r2 * c1, r2 * c0 - r0 * c2, r0 * c1 - r1 * c0]
    return arms, w


def store_split(stage, total, n, value):
    coarse = value.astype(jnp.bfloat16).astype(F32)
    stage[n] = coarse
    stage[total + n] = value - coarse


def add_by_slot(stage, slot, width):
    slots = lax.broadcasted_iota(jnp.int32, (width, 128), 0)
    hot, terms = [], []
    for s in range(8):
        row = jnp.broadcast_to(slot[s:s + 1, :], (width, 128))
        hot.append((row == slots).astype(F32).astype(jnp.bfloat16))
        terms.append(stage[:, s, :].astype(jnp.bfloat16))
    return lax.dot_general(
        jnp.concatenate(hot, axis=1),
        jnp.concatenate(terms, axis=1),
        (((1,), (1,)), ((), ())),
        preferred_element_type=F32,
    )


def fixed_kernel(slots, dirs, pops, rb, table, out, stage, acc, *, width):
    acc[...] = jnp.zeros_like(acc)
    total = stage.shape[0] // 2
    for n in range(6 + len(PAIRS), total):
        stage[n] = jnp.zeros((8, 128), F32)
        stage[total + n] = jnp.zeros((8, 128), F32)

    def block(b, carry):
        rs = pl.ds(pl.multiple_of(8 * b, 8), 8)
        arms, w = geometry(dirs[rs, :], [rb[n, rs, :] for n in range(3)], table)
        twice = 2.0 * pops[rs, :]
        weighted = [w * arm for arm in arms]
        for n in range(6):
            store_split(stage, total, n, twice * arms[n])
        for n, (a, d) in enumerate(PAIRS):
            store_split(stage, total, 6 + n, weighted[a] * arms[d])
        acc[...] += add_by_slot(stage, slots[rs, :], width)
        return carry

    lax.fori_loop(0, slots.shape[0] // 8, block, 0)
    out[...] = acc[:, 0:total] + acc[:, total:]


def press_kernel(low, high, keys, rb, table, press, out, stage, acc, *, width):
    acc[...] = jnp.zeros_like(acc)
    total = stage.shape[0] // 2
    for n in range(6, total):
        stage[n] = jnp.zeros((8, 128), F32)
        stage[total + n] = jnp.zeros((8, 128), F32)

    def block(b, carry):
        rs = pl.ds(pl.multiple_of(8 * b, 8), 8)
        key = keys[rs, :]
        place = (key >> KEY_BITS) + (1 << 18)
        code = key & ((1 << KEY_BITS) - 1)
        row = place >> 7
        column = place & 127
        slot = jnp.floor((code.astype(F32) + 0.5) * (1.0 / 18.0)).astype(jnp.int32)
        direction = code - 18 * slot

        def look(m, found):
            base = pl.multiple_of(8 * m, 8)
            ahead = row - base
            for s in range(8):
                line = jnp.broadcast_to(press[pl.ds(base + s, 1), :], (8, 128))
                found = jnp.where(ahead == s, lane_pick(line, column), found)
            return found

        q = lax.fori_loop(low[b], high[b] + 1, look, jnp.zeros((8, 128), F32))
        arms, w = geometry(direction, [rb[n][rs, :] for n in range(3)], table)
        wq = w * q
        for n in range(6):
            store_split(stage, total, n, wq * arms[n])
        acc[...] += add_by_slot(stage, slot, width)
        return carry

    lax.fori_loop(0, keys.shape[0] // 8, block, 0)
    out[...] = acc[:, 0:total] + acc[:, total:]


def press_entry(low, high, keys, rb0, rb1, rb2, table, press, out, stage, acc, *, width):
    press_kernel(low, high, keys, (rb0, rb1, rb2), table, press, out, stage, acc, width=width)


def reflect_kernel(slots, dirs, pops, rb, table, motion, out):
    def block(b, carry):
        rs = pl.ds(pl.multiple_of(8 * b, 8), 8)
        arms, w = geometry(dirs[rs, :], [rb[n, rs, :] for n in range(3)], table)
        slot = slots[rs, :]
        lane = slot & 127
        part = slot >> 7
        along = jnp.zeros((8, 128), F32)
        for n in range(6):
            value = jnp.zeros((8, 128), F32)
            for h in range(motion.shape[1]):
                line = jnp.broadcast_to(motion[n, h:h + 1, :], (8, 128))
                value = jnp.where(part == h, lane_pick(line, lane), value)
            along += arms[n] * value
        out[rs, :] = pops[rs, :] - jnp.where(slot >= 0, 6.0 * w * along, 0.0)
        return carry

    lax.fori_loop(0, slots.shape[0] // 8, block, 0)


def ring(axis):
    count = lax.axis_size(axis)
    forward = [(i, (i + 1) % count) for i in range(count)]
    return forward, [(b, a) for a, b in forward]


def vmem(n):
    return [pl.BlockSpec(memory_space=pltpu.VMEM)] * n


PARAMS = pltpu.CompilerParams(vmem_limit_bytes=60 * 1024 * 1024)


def shards(
    eps_field, charge, potential_start, colloid_vel, colloid_spin, link_dir, link_colloid,
    link_site, link_depth, link_pop, link_rb,
):
    depth, wide, long = charge.shape
    layers = depth // 2
    rows = wide + 2 * FIRST
    fx, bx = ring("gx")
    fy, by = ring("gy")

    def edge(part):
        return jnp.stack([potential_start[:, part], charge[:, part], eps_field[:, part].astype(F32)])

    low = lax.ppermute(edge(slice(wide - HALO, wide)), "gx", fx)
    high = lax.ppermute(edge(slice(0, HALO)), "gx", bx)

    per_tile = colloid_vel.shape[1]
    width = 9 * per_tile
    count = link_pop.shape[-1]
    lines = count // 128
    ids = link_colloid.reshape(lines, 128)
    dirs = link_dir.reshape(lines, 128)
    pops = link_pop.reshape(lines, 128)
    rb = link_rb.reshape(3, lines, 128)
    count_x, count_y = lax.axis_size("gx"), lax.axis_size("gy")
    owner = ids // per_tile
    near_x = (owner // count_y - lax.axis_index("gx") + 1) % count_x
    near_y = (owner % count_y - lax.axis_index("gy") + 1) % count_y
    live = ids >= 0
    slots = jnp.where(live, (near_x * 3 + near_y) * per_tile + ids % per_tile, -1)
    place = link_depth.reshape(lines, 128) * (wide * long) + link_site.reshape(lines, 128)
    key = jnp.where(
        live, (place - (1 << 18)) * (1 << KEY_BITS) + slots * 18 + dirs, np.int32(2**31 - 1)
    )
    keys, rb0, rb1, rb2 = lax.sort(
        (key.reshape(-1), rb[0].reshape(-1), rb[1].reshape(-1), rb[2].reshape(-1)),
        num_keys=1, is_stable=False,
    )
    keys = keys.reshape(lines, 128)
    table = direction_table()
    place_rows = (keys.reshape(-1, 1024)[:, ::1023] >> KEY_BITS) + (1 << 18)
    bounds = jnp.minimum(place_rows // 1024, depth * wide // 8 - 1)

    split, to_right, to_left = pl.pallas_call(
        pack_kernel,
        out_shape=(
            jax.ShapeDtypeStruct((6, layers + 1, rows, 128), F32),
            jax.ShapeDtypeStruct((3, GROUPS, wide + 2 * HALO, 128), F32),
            jax.ShapeDtypeStruct((3, GROUPS, wide + 2 * HALO, 128), F32),
        ),
        in_specs=vmem(5), out_specs=tuple(vmem(3)), compiler_params=PARAMS, name="pack",
    )(potential_start, charge, eps_field, low, high)
    from_left = lax.ppermute(to_right, "gy", fy)
    from_right = lax.ppermute(to_left, "gy", by)

    terms = 32
    fixed = pl.pallas_call(
        functools.partial(fixed_kernel, width=width),
        out_shape=jax.ShapeDtypeStruct((width, terms), F32),
        in_specs=vmem(5), out_specs=vmem(1)[0],
        scratch_shapes=[pltpu.VMEM((2 * terms, 8, 128), F32), pltpu.VMEM((width, 2 * terms), F32)],
        compiler_params=PARAMS, name="fixed",
        cost_estimate=pl.CostEstimate(flops=10**9, bytes_accessed=2 * 10**7, transcendentals=0),
    )(slots, dirs, pops, rb, table)

    tall = rows + 2 * MARGIN
    potential, press = pl.pallas_call(
        relax_kernel,
        out_shape=(jax.ShapeDtypeStruct(charge.shape, F32),) * 2,
        in_specs=vmem(3), out_specs=tuple(vmem(2)),
        scratch_shapes=[
            pltpu.VMEM((2, layers + 3, tall, 128), F32),
            pltpu.VMEM((2, layers + 3, tall, 128), F32),
            pltpu.VMEM((2, 7, layers + 1, rows, 128), F32),
            pltpu.VMEM((2, GROUPS + 2, tall, 128), F32),
            pltpu.VMEM((2, GROUPS + 2, tall, 128), F32),
            pltpu.VMEM((2, GROUPS, rows, 128), F32),
            pltpu.VMEM((2, 7, GROUPS, rows, 128), F32),
        ],
        compiler_params=PARAMS, name="relax",
    )(split, from_left, from_right)

    smem = pl.BlockSpec(memory_space=pltpu.SMEM)
    pressed = pl.pallas_call(
        functools.partial(press_entry, width=width),
        out_shape=jax.ShapeDtypeStruct((width, 8), F32),
        in_specs=[smem, smem] + vmem(6), out_specs=vmem(1)[0],
        scratch_shapes=[pltpu.VMEM((16, 8, 128), F32), pltpu.VMEM((width, 16), F32)],
        compiler_params=PARAMS, name="press",
    )(
        bounds[:, 0], bounds[:, 1], keys, rb0.reshape(lines, 128), rb1.reshape(lines, 128),
        rb2.reshape(lines, 128), table, press.reshape(depth * wide, 128),
    )

    sums = jnp.concatenate([fixed[:, 0:6] + pressed[:, 0:6], fixed[:, 6:27]], axis=1).T
    sums = sums.reshape(27, 3, 3, per_tile)
    mid = (
        sums[:, 1]
        + lax.ppermute(sums[:, 0], "gx", bx)
        + lax.ppermute(sums[:, 2], "gx", fx)
    )
    mine = mid[:, 1] + lax.ppermute(mid[:, 0], "gy", by) + lax.ppermute(mid[:, 2], "gy", fy)
    motion = jnp.concatenate([colloid_vel, colloid_spin], axis=0)
    drag = []
    for a in range(6):
        line = jnp.zeros_like(motion[0])
        for d in range(6):
            n = PAIRS.index((min(a, d), max(a, d)))
            line = line + mine[6 + n] * motion[d]
        drag.append(line)
    totals = mine[0:6] - 6.0 * jnp.stack(drag)
    mass = 4.0 / 3.0 * math.pi * RADIUS**3
    inertia = 0.4 * mass * RADIUS**2
    new_motion = jnp.concatenate(
        [motion[0:3] + totals[0:3] / mass, motion[3:6] + totals[3:6] / inertia], axis=0
    )
    report = jnp.concatenate([totals[0:3], totals[3:6] / RADIUS], axis=0)

    column = jnp.stack(
        [lax.ppermute(new_motion, "gy", fy), new_motion, lax.ppermute(new_motion, "gy", by)], axis=1
    )
    around = jnp.stack(
        [lax.ppermute(column, "gx", fx), column, lax.ppermute(column, "gx", bx)], axis=1
    ).reshape(6, width)
    groups = -(-width // 128)
    around = jnp.pad(around, ((0, 0), (0, groups * 128 - width))).reshape(6, groups, 128)
    link_out = pl.pallas_call(
        reflect_kernel,
        out_shape=jax.ShapeDtypeStruct((lines, 128), F32),
        in_specs=vmem(6), out_specs=vmem(1)[0], compiler_params=PARAMS, name="reflect",
    )(slots, dirs, pops, rb, table, around)
    return potential, report, link_out.reshape(link_pop.shape)


def solution(mesh):
    placed = (
        P(None, "gx", "gy"),
        P(None, "gx", "gy"),
        P(None, "gx", "gy"),
        P(None, ("gx", "gy")),
        P(None, ("gx", "gy")),
        P("gx", "gy", None),
        P("gx", "gy", None),
        P("gx", "gy", None),
        P("gx", "gy", None),
        P("gx", "gy", None),
        P(None, "gx", "gy", None),
    )
    return jax.shard_map(
        shards,
        mesh=mesh,
        in_specs=placed,
        out_specs=(P(None, "gx", "gy"), P(None, ("gx", "gy")), P("gx", "gy", None)),
        check_vma=False,
    )
```

```python
import functools
import math

import jax
import jax.numpy as jnp
import numpy as np
from jax import lax
from jax.experimental import pallas as pl
from jax.experimental.pallas import tpu as pltpu
from jax.sharding import PartitionSpec as P

SWEEPS = 6
RADIUS = 8
OVER_RELAX = 1.6
HALO = 2 * SWEEPS
FIRST = 16
MARGIN = 8
GROUPS = 5
SLOT = 2 * HALO
KEY_BITS = 13
F32 = jnp.float32

VELOCITY = np.array(
    [
        [1, 0, 0], [-1, 0, 0], [0, 1, 0], [0, -1, 0], [0, 0, 1], [0, 0, -1],
        [1, 1, 0], [1, -1, 0], [-1, 1, 0], [-1, -1, 0], [1, 0, 1], [1, 0, -1],
        [-1, 0, 1], [-1, 0, -1], [0, 1, 1], [0, 1, -1], [0, -1, 1], [0, -1, -1],
    ],
    dtype=np.float32,
)
WEIGHT = np.array([1.0 / 18.0] * 6 + [1.0 / 36.0] * 12, dtype=np.float32)


def direction_table():
    table = np.zeros((4, 8, 128), np.float32)
    table[:3, :, :18] = VELOCITY.T[:, None, :]
    table[3, :, :18] = WEIGHT[None, :]
    return jnp.asarray(table)


PAIRS = [(a, b) for a in range(6) for b in range(a, 6)]


def lane_pick(table, index):
    return jnp.take_along_axis(table, index, axis=1, mode="promise_in_bounds")


def roll(value, shift):
    return pltpu.roll(value, shift % 128, 1)


def lanes_of(shape):
    return lax.broadcasted_iota(jnp.int32, shape, 1)


def parity_of(shape):
    rows = lax.broadcasted_iota(jnp.int32, shape, 0)
    return (rows + lanes_of(shape)) % 2 == 0


def pack_kernel(pot, charge, eps, low, high, split, to_right, to_left, edges):
    depth, wide, _ = pot.shape
    layers = depth // 2
    last = FIRST + wide

    def build(k, carry):
        for f, field in enumerate((pot, charge, eps)):
            fill = 1.0 if f == 2 else 0.0
            parts = (
                (FIRST, field[2 * k].astype(F32), field[2 * k + 1].astype(F32)),
                (FIRST - HALO, low[f, 2 * k], low[f, 2 * k + 1]),
                (last, high[f, 2 * k], high[f, 2 * k + 1]),
            )
            for start, even, odd in parts:
                flat = parity_of(even.shape)
                count = even.shape[0]
                split[2 * f, k, start:start + count, :] = jnp.where(flat, even, odd)
                split[2 * f + 1, k, start:start + count, :] = jnp.where(flat, odd, even)
            spare = FIRST - HALO
            edge = jnp.full((spare, 128), fill, F32)
            for c in range(2):
                split[2 * f + c, k, 0:spare, :] = edge
                split[2 * f + c, k, last + HALO:last + HALO + spare, :] = edge
        return carry

    lax.fori_loop(0, layers, build, 0)
    for f in range(3):
        for c in range(2):
            split[2 * f + c, layers] = jnp.full(
                (split.shape[2], 128), 1.0 if f == 2 else 0.0, F32
            )

    rows = slice(FIRST - HALO, last + HALO)
    lane = lanes_of((wide + 2 * HALO, 128))
    early = lane % SLOT < HALO
    slot_of = [(lane >= SLOT * g) & (lane < SLOT * (g + 1)) for g in range(GROUPS)]

    def gather_edges(n, carry):
        f = n // GROUPS
        i = n % GROUPS
        for c in range(2):
            value = jnp.zeros((wide + 2 * HALO, 128), F32)
            for g in range(GROUPS):
                field = split[2 * f + c, i + GROUPS * g, rows, :]
                value = jnp.where(slot_of[g], roll(field, SLOT * g + HALO), value)
            edges[c, n] = value
        return carry

    lax.fori_loop(0, 3 * GROUPS, gather_edges, 0)

    middle = lane - 2 * (lane % SLOT) + SLOT - 1
    near, same, far = [jnp.clip(middle + n * HALO, 0, 127) for n in (-1, 0, 1)]

    def strips(n, carry):
        f = n // GROUPS
        i = n % GROUPS
        red, black = edges[0, n], edges[1, n]
        to_right[f, i] = jnp.where(early, lane_pick(red, near), lane_pick(black, same))
        to_left[f, i] = jnp.where(early, lane_pick(red, same), lane_pick(black, far))
        return carry

    lax.fori_loop(0, 3 * GROUPS, strips, 0)


def relax_kernel(split, from_left, from_right, pot_out, press_out, pa, ea, wa, pb, eb, cb, wb):
    layers = split.shape[1] - 1
    depth, wide, _ = pot_out.shape
    rows = split.shape[2]
    tiles = rows // 8
    top = MARGIN
    lane = lanes_of((8, 128))
    flat = parity_of((8, 128))
    at_0 = lane == 0
    at_127 = lane == 127
    in_slot = lane % SLOT
    slot_east = in_slot == HALO - 1
    slot_west = in_slot == HALO
    pick = [(lane == SLOT * g + HALO - 1) | (lane == SLOT * g + HALO) for g in range(GROUPS)]

    zero = jnp.zeros((rows + 2 * MARGIN, 128), F32)
    one = jnp.ones((rows + 2 * MARGIN, 128), F32)
    margin0 = jnp.zeros((MARGIN, 128), F32)
    margin1 = jnp.ones((MARGIN, 128), F32)
    for c in range(2):
        pa[c, 0] = zero
        ea[c, 0] = one
        ea[c, layers + 1] = one

    def load_core(k, carry):
        for c in range(2):
            pa[c, k + 1, 0:top, :] = margin0
            pa[c, k + 1, top:top + rows, :] = split[c, k]
            pa[c, k + 1, top + rows:, :] = margin0
            ea[c, k + 1, 0:top, :] = margin1
            ea[c, k + 1, top:top + rows, :] = split[4 + c, k]
            ea[c, k + 1, top + rows:, :] = margin1
        return carry

    lax.fori_loop(0, layers + 1, load_core, 0)
    for c in range(2):
        ea[c, 0, top:top + rows, :] = split[5 - c, 0]
        ea[c, layers + 1, top:top + rows, :] = split[5 - c, layers - 1]
        pa[c, layers + 2] = zero
        ea[c, layers + 2] = one

    first = FIRST - HALO
    high = wide + 2 * HALO
    wide_lane = lanes_of((high, 128))
    wide_first = wide_lane % SLOT < HALO
    wide_used = wide_lane < SLOT * GROUPS
    for c in range(2):
        for i in range(GROUPS + 2):
            pb[c, i] = zero
            eb[c, i] = one
        for i in range(GROUPS):
            cb[c, i] = jnp.zeros((rows, 128), F32)

    for f, target in enumerate((pb, cb, eb)):
        for i in range(GROUPS):
            west = from_left[f, i]
            east = from_right[f, i]
            red = jnp.where(wide_first, east, roll(west, HALO))
            black = jnp.where(wide_first, roll(east, -HALO), west)
            fill = 1.0 if f == 2 else 0.0
            red = jnp.where(wide_used, red, fill)
            black = jnp.where(wide_used, black, fill)
            if f == 1:
                target[0, i, first:first + high, :] = red
                target[1, i, first:first + high, :] = black
            else:
                target[0, i + 1, top + first:top + first + high, :] = red
                target[1, i + 1, top + first:top + first + high, :] = black

    all_lane = lanes_of((rows + 2 * MARGIN, 128))
    lead = all_lane < SLOT
    tail = all_lane >= SLOT * (GROUPS - 1)
    spare_slot = SLOT * (layers // GROUPS)
    in_spare = (all_lane >= spare_slot) & (all_lane < spare_slot + SLOT)

    def wrap_pot(c):
        pb[c, 0] = jnp.where(lead, 0.0, roll(pb[c, GROUPS], SLOT))
        pb[c, GROUPS + 1] = jnp.where(tail, 0.0, roll(pb[c, 1], -SLOT))

    spare_row = layers % GROUPS + 1
    for c in range(2):
        wrap_pot(c)
        eb[c, spare_row] = jnp.where(in_spare, eb[1 - c, spare_row - 1], eb[c, spare_row])
    for c in range(2):
        eb[c, 0] = jnp.where(lead, eb[1 - c, 1], roll(eb[c, GROUPS], SLOT))
        eb[c, GROUPS + 1] = jnp.where(tail, 1.0, roll(eb[c, 1], -SLOT))

    def around(src_a, src_b, other, color, i, t, body_a, body_b):
        r0 = top + 8 * t
        rs = slice(r0, r0 + 8)
        rm = slice(r0 - 1, r0 + 7)
        rp = slice(r0 + 1, r0 + 9)
        up = ~flat if color == 0 else flat
        side = src_b[other, i + 1, rs, :]
        edge = side
        for g in range(GROUPS):
            k = i + GROUPS * g
            here = src_a[other, k + 1, rs, :]
            halo = roll(side, -(SLOT * g + HALO))
            body_a(k, (
                here,
                jnp.where(up, src_a[other, k + 2, rs, :], src_a[other, k, rs, :]),
                src_a[other, k + 1, rm, :],
                src_a[other, k + 1, rp, :],
                jnp.where(at_0, halo, roll(here, 1)),
                jnp.where(at_127, halo, roll(here, -1)),
            ))
            if body_b is not None:
                edge = jnp.where(pick[g], roll(here, SLOT * g + HALO), edge)
        if body_b is not None:
            body_b((
                side,
                jnp.where(up, src_b[other, i, rs, :], src_b[other, i + 2, rs, :]),
                src_b[other, i + 1, rm, :],
                src_b[other, i + 1, rp, :],
                jnp.where(slot_east, edge, roll(side, -1)),
                jnp.where(slot_west, edge, roll(side, 1)),
            ))

    def coefficients(own, charge, sides):
        faces = [0.5 * (own + side) for side in sides]
        total = faces[0] + faces[1] + faces[2] + faces[3] + faces[4] + faces[5]
        scale = OVER_RELAX / total
        return [face * scale for face in faces] + [charge * scale]

    for c in range(2):
        def set_up(i, carry, c=c):
            for t in range(tiles):
                ts = slice(8 * t, 8 * t + 8)
                ps = slice(top + 8 * t, top + 8 * t + 8)

                def body_a(k, sides):
                    values = coefficients(ea[c, k + 1, ps, :], split[2 + c, k, ts, :], sides)
                    for n, value in enumerate(values):
                        wa[c, n, k, ts, :] = value

                def body_b(sides):
                    values = coefficients(eb[c, i + 1, ps, :], cb[c, i, ts, :], sides)
                    live = in_spare[0:8] & (i + 1 == spare_row)
                    for n, value in enumerate(values):
                        wb[c, n, i, ts, :] = jnp.where(live, 0.0, value)

                around(ea, eb, 1 - c, c, i, t, body_a, body_b)
            return carry

        lax.fori_loop(0, GROUPS, set_up, 0)
        for n in range(7):
            wa[c, n, layers] = jnp.zeros((rows, 128), F32)

    def combine(own, w, sides):
        left = w[0] * sides[0] + w[1] * sides[1]
        mid = w[2] * sides[2] + w[3] * sides[3]
        right = w[4] * sides[4] + w[5] * sides[5]
        return (w[6] - (OVER_RELAX - 1.0) * own) + (left + (mid + right))

    for step in range(2 * SWEEPS):
        c = step % 2
        reach = HALO - 1 - step
        t_low = (FIRST - reach) // 8
        t_high = -(-(FIRST + wide + reach) // 8)

        def half(i, carry, c=c, reach=reach, t_low=t_low, t_high=t_high):
            for t in range(t_low, t_high):
                ts = slice(8 * t, 8 * t + 8)
                ps = slice(top + 8 * t, top + 8 * t + 8)

                def body_a(k, sides):
                    w = [wa[c, n, k, ts, :] for n in range(7)]
                    pa[c, k + 1, ps, :] = combine(pa[c, k + 1, ps, :], w, sides)

                def body_b(sides):
                    w = [wb[c, n, i, ts, :] for n in range(7)]
                    pb[c, i + 1, ps, :] = combine(pb[c, i + 1, ps, :], w, sides)

                around(pa, pb, 1 - c, c, i, t, body_a, body_b if reach else None)
            return carry

        lax.fori_loop(0, GROUPS, half, 0)
        if reach:
            wrap_pot(c)

    core = slice(top + FIRST, top + FIRST + wide)
    core_flat = parity_of((wide, 128))

    def finish(k, carry):
        red, black = pa[0, k + 1, core, :], pa[1, k + 1, core, :]
        e_red, e_black = ea[0, k + 1, core, :], ea[1, k + 1, core, :]
        q_red = 0.5 * e_red * red * red
        q_black = 0.5 * e_black * black * black
        pot_out[2 * k] = jnp.where(core_flat, red, black)
        pot_out[2 * k + 1] = jnp.where(core_flat, black, red)
        press_out[2 * k] = jnp.where(core_flat, q_red, q_black)
        press_out[2 * k + 1] = jnp.where(core_flat, q_black, q_red)
        return carry

    lax.fori_loop(0, layers, finish, 0)


def geometry(direction, offsets, table):
    c0, c1, c2, w = [lane_pick(table[n], direction) for n in range(4)]
    r0, r1, r2 = offsets
    arms = [c0, c1, c2, r1 * c2 - r2 * c1, r2 * c0 - r0 * c2, r0 * c1 - r1 * c0]
    return arms, w


def store_term(stage, n, value):
    stage[8 * n:8 * n + 8, :] = value


def add_by_slot(stage, slot, width):
    total = stage.shape[0] // 8
    fine = slot & 15
    coarse = slot >> 4
    small = lax.broadcasted_iota(jnp.int32, (16, 128), 0)
    hot, terms = [], []
    for s in range(8):
        match = (jnp.broadcast_to(fine[s:s + 1, :], (16, 128)) == small).astype(F32)
        match = match.astype(jnp.bfloat16)
        part = jnp.broadcast_to(coarse[s:s + 1, :].astype(F32), (16, 128)).astype(jnp.bfloat16)
        none = jnp.zeros((16, 128), jnp.bfloat16)
        hot.append(jnp.concatenate(
            [jnp.where(part == m, match, none) for m in range(width // 16)], axis=0
        ))
        value = stage[pl.ds(s, total, stride=8), :]
        head = value.astype(jnp.bfloat16)
        terms.append(jnp.concatenate(
            [head.astype(F32), value - head.astype(F32)], axis=0
        ).astype(jnp.bfloat16))
    return lax.dot_general(
        jnp.concatenate(hot, axis=1),
        jnp.concatenate(terms, axis=1),
        (((1,), (1,)), ((), ())),
        preferred_element_type=F32,
    )


def fixed_kernel(slots, dirs, pops, rb, table, out, stage, acc, *, width):
    acc[...] = jnp.zeros_like(acc)
    total = stage.shape[0] // 8
    for n in range(6 + len(PAIRS), total):
        store_term(stage, n, jnp.zeros((8, 128), F32))

    def block(b, carry):
        rs = pl.ds(pl.multiple_of(8 * b, 8), 8)
        arms, w = geometry(dirs[rs, :], [rb[n, rs, :] for n in range(3)], table)
        twice = 2.0 * pops[rs, :]
        weighted = [w * arm for arm in arms]
        for n in range(6):
            store_term(stage, n, twice * arms[n])
        for n, (a, d) in enumerate(PAIRS):
            store_term(stage, 6 + n, weighted[a] * arms[d])
        acc[...] += add_by_slot(stage, slots[rs, :], width)
        return carry

    lax.fori_loop(0, slots.shape[0] // 8, block, 0)
    out[...] = acc[:, 0:total] + acc[:, total:]


BATCH = 4
AHEAD = 4


def press_kernel(low, passes, keys, rb0, rb1, rb2, table, press, out, stage, acc, *, width):
    acc[...] = jnp.zeros_like(acc)
    for n in range(6, stage.shape[0] // 8):
        store_term(stage, n, jnp.zeros((8, 128), F32))
    limit = press.shape[0] - 1
    line = lax.broadcasted_iota(jnp.int32, (8, 128), 0)

    def batch(b, carry):
        spots = [pl.ds(pl.multiple_of(8 * (BATCH * b + j), 8), 8) for j in range(BATCH)]
        columns, offsets, starts = [], [], []
        for j in range(BATCH):
            place = (keys[spots[j], :] >> KEY_BITS) + (1 << 18)
            start = [low[8 * (BATCH * b + j) + s] for s in range(8)]
            first = jnp.zeros((8, 128), jnp.int32)
            for s in range(8):
                first = jnp.where(line == s, start[s], first)
            columns.append(place & 127)
            offsets.append((place >> 7) - first)
            starts.append(start)

        def look(m, found):
            found = list(found)
            for j in range(BATCH):
                for t in range(AHEAD):
                    step = AHEAD * m + t
                    window = jnp.zeros((8, 128), F32)
                    for s in range(8):
                        row = press[pl.ds(jnp.minimum(starts[j][s] + step, limit), 1), :]
                        window = jnp.where(line == s, jnp.broadcast_to(row, (8, 128)), window)
                    value = lane_pick(window, columns[j])
                    found[j] = jnp.where(offsets[j] == step, value, found[j])
            return tuple(found)

        found = lax.fori_loop(
            0, passes[b], look, tuple(jnp.zeros((8, 128), F32) for _ in range(BATCH))
        )
        for j in range(BATCH):
            rs = spots[j]
            code = keys[rs, :] & ((1 << KEY_BITS) - 1)
            slot = jnp.floor((code.astype(F32) + 0.5) * (1.0 / 18.0)).astype(jnp.int32)
            direction = code - 18 * slot
            arms, w = geometry(direction, [rb0[rs, :], rb1[rs, :], rb2[rs, :]], table)
            wq = w * found[j]
            for n in range(6):
                store_term(stage, n, wq * arms[n])
            acc[...] += add_by_slot(stage, slot, width)
        return carry

    lax.fori_loop(0, keys.shape[0] // (8 * BATCH), batch, 0)
    total = stage.shape[0] // 8
    out[...] = acc[:, 0:total] + acc[:, total:]


def reflect_kernel(slots, dirs, pops, rb, table, motion, out):
    def block(b, carry):
        rs = pl.ds(pl.multiple_of(8 * b, 8), 8)
        arms, w = geometry(dirs[rs, :], [rb[n, rs, :] for n in range(3)], table)
        slot = slots[rs, :]
        lane = slot & 127
        part = slot >> 7
        along = jnp.zeros((8, 128), F32)
        for n in range(6):
            value = jnp.zeros((8, 128), F32)
            for h in range(motion.shape[1]):
                line = jnp.broadcast_to(motion[n, h:h + 1, :], (8, 128))
                value = jnp.where(part == h, lane_pick(line, lane), value)
            along += arms[n] * value
        out[rs, :] = pops[rs, :] - jnp.where(slot >= 0, 6.0 * w * along, 0.0)
        return carry

    lax.fori_loop(0, slots.shape[0] // 8, block, 0)


def ring(axis):
    count = lax.axis_size(axis)
    forward = [(i, (i + 1) % count) for i in range(count)]
    return forward, [(b, a) for a, b in forward]


def vmem(n):
    return [pl.BlockSpec(memory_space=pltpu.VMEM)] * n


PARAMS = pltpu.CompilerParams(vmem_limit_bytes=60 * 1024 * 1024)


def shards(
    eps_field, charge, potential_start, colloid_vel, colloid_spin, link_dir, link_colloid,
    link_site, link_depth, link_pop, link_rb,
):
    depth, wide, long = charge.shape
    layers = depth // 2
    rows = wide + 2 * FIRST
    fx, bx = ring("gx")
    fy, by = ring("gy")

    def edge(part):
        return jnp.stack([potential_start[:, part], charge[:, part], eps_field[:, part].astype(F32)])

    low = lax.ppermute(edge(slice(wide - HALO, wide)), "gx", fx)
    high = lax.ppermute(edge(slice(0, HALO)), "gx", bx)

    per_tile = colloid_vel.shape[1]
    width = 9 * per_tile
    count = link_pop.shape[-1]
    lines = count // 128
    ids = link_colloid.reshape(lines, 128)
    dirs = link_dir.reshape(lines, 128)
    pops = link_pop.reshape(lines, 128)
    rb = link_rb.reshape(3, lines, 128)
    count_x, count_y = lax.axis_size("gx"), lax.axis_size("gy")
    owner = ids // per_tile
    near_x = (owner // count_y - lax.axis_index("gx") + 1) % count_x
    near_y = (owner % count_y - lax.axis_index("gy") + 1) % count_y
    live = ids >= 0
    slots = jnp.where(live, (near_x * 3 + near_y) * per_tile + ids % per_tile, -1)
    place = link_depth.reshape(lines, 128) * (wide * long) + link_site.reshape(lines, 128)
    key = jnp.where(
        live, (place - (1 << 18)) * (1 << KEY_BITS) + slots * 18 + dirs, np.int32(2**31 - 1)
    )
    keys, rb0, rb1, rb2 = lax.sort(
        (key.reshape(-1), rb[0].reshape(-1), rb[1].reshape(-1), rb[2].reshape(-1)),
        num_keys=1, is_stable=False,
    )
    keys, rb0, rb1, rb2, low, high = lax.optimization_barrier((keys, rb0, rb1, rb2, low, high))
    keys = keys.reshape(lines, 128)
    table = direction_table()
    table_rows = ((keys >> KEY_BITS) + (1 << 18)) >> 7
    row_low = jnp.minimum(table_rows[:, 0], depth * wide - 1)
    row_high = jnp.max(jnp.where(table_rows < depth * wide, table_rows, 0), axis=1)
    span = jnp.max((row_high - row_low + 1).reshape(-1, 8 * BATCH), axis=1)
    passes = (jnp.maximum(span, 0) + AHEAD - 1) // AHEAD

    split, to_right, to_left = pl.pallas_call(
        pack_kernel,
        out_shape=(
            jax.ShapeDtypeStruct((6, layers + 1, rows, 128), F32),
            jax.ShapeDtypeStruct((3, GROUPS, wide + 2 * HALO, 128), F32),
            jax.ShapeDtypeStruct((3, GROUPS, wide + 2 * HALO, 128), F32),
        ),
        in_specs=vmem(5), out_specs=tuple(vmem(3)), compiler_params=PARAMS, name="pack",
        scratch_shapes=[pltpu.VMEM((2, 3 * GROUPS, wide + 2 * HALO, 128), F32)],
    )(potential_start, charge, eps_field, low, high)
    from_left = lax.ppermute(to_right, "gy", fy)
    from_right = lax.ppermute(to_left, "gy", by)

    terms = 32
    fixed = pl.pallas_call(
        functools.partial(fixed_kernel, width=width),
        out_shape=jax.ShapeDtypeStruct((width, terms), F32),
        in_specs=vmem(5), out_specs=vmem(1)[0],
        scratch_shapes=[pltpu.VMEM((8 * terms, 128), F32), pltpu.VMEM((width, 2 * terms), F32)],
        compiler_params=PARAMS, name="fixed",
        cost_estimate=pl.CostEstimate(flops=10**9, bytes_accessed=2 * 10**7, transcendentals=0),
    )(slots, dirs, pops, rb, table)

    tall = rows + 2 * MARGIN
    potential, press = pl.pallas_call(
        relax_kernel,
        out_shape=(jax.ShapeDtypeStruct(charge.shape, F32),) * 2,
        in_specs=vmem(3), out_specs=tuple(vmem(2)),
        scratch_shapes=[
            pltpu.VMEM((2, layers + 3, tall, 128), F32),
            pltpu.VMEM((2, layers + 3, tall, 128), F32),
            pltpu.VMEM((2, 7, layers + 1, rows, 128), F32),
            pltpu.VMEM((2, GROUPS + 2, tall, 128), F32),
            pltpu.VMEM((2, GROUPS + 2, tall, 128), F32),
            pltpu.VMEM((2, GROUPS, rows, 128), F32),
            pltpu.VMEM((2, 7, GROUPS, rows, 128), F32),
        ],
        compiler_params=PARAMS, name="relax",
    )(split, from_left, from_right)

    smem = pl.BlockSpec(memory_space=pltpu.SMEM)
    pressed = pl.pallas_call(
        functools.partial(press_kernel, width=width),
        out_shape=jax.ShapeDtypeStruct((width, 8), F32),
        in_specs=[smem, smem] + vmem(6), out_specs=vmem(1)[0],
        scratch_shapes=[pltpu.VMEM((64, 128), F32), pltpu.VMEM((width, 16), F32)],
        compiler_params=PARAMS, name="press",
    )(
        row_low, passes, keys, rb0.reshape(lines, 128), rb1.reshape(lines, 128),
        rb2.reshape(lines, 128), table, press.reshape(depth * wide, 128),
    )

    sums = jnp.concatenate([fixed[:, 0:6] + pressed[:, 0:6], fixed[:, 6:27]], axis=1).T
    sums = sums.reshape(27, 3, 3, per_tile)
    mid = (
        sums[:, 1]
        + lax.ppermute(sums[:, 0], "gx", bx)
        + lax.ppermute(sums[:, 2], "gx", fx)
    )
    mine = mid[:, 1] + lax.ppermute(mid[:, 0], "gy", by) + lax.ppermute(mid[:, 2], "gy", fy)
    motion = jnp.concatenate([colloid_vel, colloid_spin], axis=0)
    drag = []
    for a in range(6):
        line = jnp.zeros_like(motion[0])
        for d in range(6):
            n = PAIRS.index((min(a, d), max(a, d)))
            line = line + mine[6 + n] * motion[d]
        drag.append(line)
    totals = mine[0:6] - 6.0 * jnp.stack(drag)
    mass = 4.0 / 3.0 * math.pi * RADIUS**3
    inertia = 0.4 * mass * RADIUS**2
    new_motion = jnp.concatenate(
        [motion[0:3] + totals[0:3] / mass, motion[3:6] + totals[3:6] / inertia], axis=0
    )
    report = jnp.concatenate([totals[0:3], totals[3:6] / RADIUS], axis=0)

    column = jnp.stack(
        [lax.ppermute(new_motion, "gy", fy), new_motion, lax.ppermute(new_motion, "gy", by)], axis=1
    )
    around = jnp.stack(
        [lax.ppermute(column, "gx", fx), column, lax.ppermute(column, "gx", bx)], axis=1
    ).reshape(6, width)
    groups = -(-width // 128)
    around = jnp.pad(around, ((0, 0), (0, groups * 128 - width))).reshape(6, groups, 128)
    link_out = pl.pallas_call(
        reflect_kernel,
        out_shape=jax.ShapeDtypeStruct((lines, 128), F32),
        in_specs=vmem(6), out_specs=vmem(1)[0], compiler_params=PARAMS, name="reflect",
    )(slots, dirs, pops, rb, table, around)
    return potential, report, link_out.reshape(link_pop.shape)


def solution(mesh):
    placed = (
        P(None, "gx", "gy"),
        P(None, "gx", "gy"),
        P(None, "gx", "gy"),
        P(None, ("gx", "gy")),
        P(None, ("gx", "gy")),
        P("gx", "gy", None),
        P("gx", "gy", None),
        P("gx", "gy", None),
        P("gx", "gy", None),
        P("gx", "gy", None),
        P(None, "gx", "gy", None),
    )
    return jax.shard_map(
        shards,
        mesh=mesh,
        in_specs=placed,
        out_specs=(P(None, "gx", "gy"), P(None, ("gx", "gy")), P("gx", "gy", None)),
        check_vma=False,
    )
```

```python
import functools
import math

import jax
import jax.numpy as jnp
import numpy as np
from jax import lax
from jax.experimental import pallas as pl
from jax.experimental.pallas import tpu as pltpu
from jax.sharding import PartitionSpec as P

SWEEPS = 6
RADIUS = 8
OVER_RELAX = 1.6
HALO = 2 * SWEEPS
FIRST = 16
MARGIN = 8
GROUPS = 5
SLOT = 2 * HALO
KEY_BITS = 13
F32 = jnp.float32
HALF = jnp.float16
POT_SCALE = 2.0**14
CHARGE_SCALE = 2.0**13

VELOCITY = np.array(
    [
        [1, 0, 0], [-1, 0, 0], [0, 1, 0], [0, -1, 0], [0, 0, 1], [0, 0, -1],
        [1, 1, 0], [1, -1, 0], [-1, 1, 0], [-1, -1, 0], [1, 0, 1], [1, 0, -1],
        [-1, 0, 1], [-1, 0, -1], [0, 1, 1], [0, 1, -1], [0, -1, 1], [0, -1, -1],
    ],
    dtype=np.float32,
)
WEIGHT = np.array([1.0 / 18.0] * 6 + [1.0 / 36.0] * 12, dtype=np.float32)


def direction_table():
    table = np.zeros((4, 8, 128), np.float32)
    table[:3, :, :18] = VELOCITY.T[:, None, :]
    table[3, :, :18] = WEIGHT[None, :]
    return jnp.asarray(table)


PAIRS = [(a, b) for a in range(6) for b in range(a, 6)]


def lane_pick(table, index):
    return jnp.take_along_axis(table, index, axis=1, mode="promise_in_bounds")


def roll(value, shift):
    return pltpu.roll(value, shift % 128, 1)


def lanes_of(shape):
    return lax.broadcasted_iota(jnp.int32, shape, 1)


def parity_of(shape):
    rows = lax.broadcasted_iota(jnp.int32, shape, 0)
    return (rows + lanes_of(shape)) % 2 == 0


def pack_kernel(pot, charge, eps, low, high, split, to_right, to_left, edges):
    depth, wide, _ = pot.shape
    layers = depth // 2
    last = FIRST + wide

    def strip(source, f, z):
        return source[pl.ds(f * HALO * depth + z, HALO, stride=depth), :]

    def build(k, carry):
        for f, field in enumerate((pot, charge, eps)):
            fill = 1.0 if f == 2 else 0.0
            parts = (
                (FIRST, field[2 * k].astype(F32), field[2 * k + 1].astype(F32)),
                (FIRST - HALO, *(strip(low, f, 2 * k + n) for n in range(2))),
                (last, *(strip(high, f, 2 * k + n) for n in range(2))),
            )
            for start, even, odd in parts:
                flat = parity_of(even.shape)
                count = even.shape[0]
                split[2 * f, k, start:start + count, :] = jnp.where(flat, even, odd)
                split[2 * f + 1, k, start:start + count, :] = jnp.where(flat, odd, even)
            spare = FIRST - HALO
            edge = jnp.full((spare, 128), fill, F32)
            for c in range(2):
                split[2 * f + c, k, 0:spare, :] = edge
                split[2 * f + c, k, last + HALO:last + HALO + spare, :] = edge
        return carry

    lax.fori_loop(0, layers, build, 0)
    for f in range(3):
        for c in range(2):
            split[2 * f + c, layers] = jnp.full(
                (split.shape[2], 128), 1.0 if f == 2 else 0.0, F32
            )

    rows = slice(FIRST - HALO, last + HALO)
    lane = lanes_of((wide + 2 * HALO, 128))
    early = lane % SLOT < HALO
    slot_of = [(lane >= SLOT * g) & (lane < SLOT * (g + 1)) for g in range(GROUPS)]

    def gather_edges(n, carry):
        f = n // GROUPS
        i = n % GROUPS
        for c in range(2):
            value = jnp.zeros((wide + 2 * HALO, 128), F32)
            for g in range(GROUPS):
                field = split[2 * f + c, i + GROUPS * g, rows, :]
                value = jnp.where(slot_of[g], roll(field, SLOT * g + HALO), value)
            edges[c, n] = value
        return carry

    lax.fori_loop(0, 3 * GROUPS, gather_edges, 0)

    middle = lane - 2 * (lane % SLOT) + SLOT - 1
    near, same, far = [jnp.clip(middle + n * HALO, 0, 127) for n in (-1, 0, 1)]

    def strips(n, carry):
        f = n // GROUPS
        i = n % GROUPS
        red, black = edges[0, n], edges[1, n]
        to_right[f, i] = jnp.where(early, lane_pick(red, near), lane_pick(black, same))
        to_left[f, i] = jnp.where(early, lane_pick(red, same), lane_pick(black, far))
        return carry

    lax.fori_loop(0, 3 * GROUPS, strips, 0)


def relax_kernel(split, from_left, from_right, pot_out, press_out, pa, ea, wa, pb, eb, cb, wb):
    layers = split.shape[1] - 1
    depth, wide, _ = pot_out.shape
    rows = split.shape[2]
    tiles = rows // 8
    top = MARGIN
    lane = lanes_of((8, 128))
    flat = parity_of((8, 128))
    at_0 = lane == 0
    at_127 = lane == 127
    in_slot = lane % SLOT
    slot_east = in_slot == HALO - 1
    slot_west = in_slot == HALO
    pick = [(lane == SLOT * g + HALO - 1) | (lane == SLOT * g + HALO) for g in range(GROUPS)]

    zero = jnp.zeros((rows + 2 * MARGIN, 128), F32)
    one = jnp.ones((rows + 2 * MARGIN, 128), F32)
    margin0 = jnp.zeros((MARGIN, 128), F32)
    margin1 = jnp.ones((MARGIN, 128), F32)
    for c in range(2):
        pa[c, 0] = zero
        ea[c, 0] = one
        ea[c, layers + 1] = one

    def load_core(k, carry):
        for c in range(2):
            pa[c, k + 1, 0:top, :] = margin0
            pa[c, k + 1, top:top + rows, :] = split[c, k]
            pa[c, k + 1, top + rows:, :] = margin0
            ea[c, k + 1, 0:top, :] = margin1
            ea[c, k + 1, top:top + rows, :] = split[4 + c, k]
            ea[c, k + 1, top + rows:, :] = margin1
        return carry

    lax.fori_loop(0, layers + 1, load_core, 0)
    for c in range(2):
        ea[c, 0, top:top + rows, :] = split[5 - c, 0]
        ea[c, layers + 1, top:top + rows, :] = split[5 - c, layers - 1]
        pa[c, layers + 2] = zero
        ea[c, layers + 2] = one

    first = FIRST - HALO
    high = wide + 2 * HALO
    wide_lane = lanes_of((high, 128))
    wide_first = wide_lane % SLOT < HALO
    wide_used = wide_lane < SLOT * GROUPS
    for c in range(2):
        for i in range(GROUPS + 2):
            pb[c, i] = zero
            eb[c, i] = one
        for i in range(GROUPS):
            cb[c, i] = jnp.zeros((rows, 128), F32)

    for f, target in enumerate((pb, cb, eb)):
        for i in range(GROUPS):
            west = from_left[f, i]
            east = from_right[f, i]
            red = jnp.where(wide_first, east, roll(west, HALO))
            black = jnp.where(wide_first, roll(east, -HALO), west)
            fill = 1.0 if f == 2 else 0.0
            red = jnp.where(wide_used, red, fill)
            black = jnp.where(wide_used, black, fill)
            if f == 1:
                target[0, i, first:first + high, :] = red
                target[1, i, first:first + high, :] = black
            else:
                target[0, i + 1, top + first:top + first + high, :] = red
                target[1, i + 1, top + first:top + first + high, :] = black

    all_lane = lanes_of((rows + 2 * MARGIN, 128))
    lead = all_lane < SLOT
    tail = all_lane >= SLOT * (GROUPS - 1)
    spare_slot = SLOT * (layers // GROUPS)
    in_spare = (all_lane >= spare_slot) & (all_lane < spare_slot + SLOT)

    def wrap_pot(c):
        pb[c, 0] = jnp.where(lead, 0.0, roll(pb[c, GROUPS], SLOT))
        pb[c, GROUPS + 1] = jnp.where(tail, 0.0, roll(pb[c, 1], -SLOT))

    spare_row = layers % GROUPS + 1
    for c in range(2):
        wrap_pot(c)
        eb[c, spare_row] = jnp.where(in_spare, eb[1 - c, spare_row - 1], eb[c, spare_row])
    for c in range(2):
        eb[c, 0] = jnp.where(lead, eb[1 - c, 1], roll(eb[c, GROUPS], SLOT))
        eb[c, GROUPS + 1] = jnp.where(tail, 1.0, roll(eb[c, 1], -SLOT))

    def around(src_a, src_b, other, color, i, t, body_a, body_b):
        r0 = top + 8 * t
        rs = slice(r0, r0 + 8)
        rm = slice(r0 - 1, r0 + 7)
        rp = slice(r0 + 1, r0 + 9)
        up = ~flat if color == 0 else flat
        side = src_b[other, i + 1, rs, :]
        edge = side
        for g in range(GROUPS):
            k = i + GROUPS * g
            here = src_a[other, k + 1, rs, :]
            halo = roll(side, -(SLOT * g + HALO))
            body_a(k, (
                here,
                jnp.where(up, src_a[other, k + 2, rs, :], src_a[other, k, rs, :]),
                src_a[other, k + 1, rm, :],
                src_a[other, k + 1, rp, :],
                jnp.where(at_0, halo, roll(here, 1)),
                jnp.where(at_127, halo, roll(here, -1)),
            ))
            if body_b is not None:
                edge = jnp.where(pick[g], roll(here, SLOT * g + HALO), edge)
        if body_b is not None:
            body_b((
                side,
                jnp.where(up, src_b[other, i, rs, :], src_b[other, i + 2, rs, :]),
                src_b[other, i + 1, rm, :],
                src_b[other, i + 1, rp, :],
                jnp.where(slot_east, edge, roll(side, -1)),
                jnp.where(slot_west, edge, roll(side, 1)),
            ))

    def coefficients(own, charge, sides):
        faces = [0.5 * (own + side) for side in sides]
        total = faces[0] + faces[1] + faces[2] + faces[3] + faces[4] + faces[5]
        scale = OVER_RELAX / total
        return [face * scale for face in faces] + [charge * scale]

    for c in range(2):
        def set_up(i, carry, c=c):
            for t in range(tiles):
                ts = slice(8 * t, 8 * t + 8)
                ps = slice(top + 8 * t, top + 8 * t + 8)

                def body_a(k, sides):
                    values = coefficients(ea[c, k + 1, ps, :], split[2 + c, k, ts, :], sides)
                    for n, value in enumerate(values):
                        wa[c, n, k, ts, :] = value

                def body_b(sides):
                    values = coefficients(eb[c, i + 1, ps, :], cb[c, i, ts, :], sides)
                    live = in_spare[0:8] & (i + 1 == spare_row)
                    for n, value in enumerate(values):
                        wb[c, n, i, ts, :] = jnp.where(live, 0.0, value)

                around(ea, eb, 1 - c, c, i, t, body_a, body_b)
            return carry

        lax.fori_loop(0, GROUPS, set_up, 0)
        for n in range(7):
            wa[c, n, layers] = jnp.zeros((rows, 128), F32)

    def combine(own, w, sides):
        left = w[0] * sides[0] + w[1] * sides[1]
        mid = w[2] * sides[2] + w[3] * sides[3]
        right = w[4] * sides[4] + w[5] * sides[5]
        return (w[6] - (OVER_RELAX - 1.0) * own) + (left + (mid + right))

    for step in range(2 * SWEEPS):
        c = step % 2
        reach = HALO - 1 - step
        t_low = (FIRST - reach) // 8
        t_high = -(-(FIRST + wide + reach) // 8)

        def half(i, carry, c=c, reach=reach, t_low=t_low, t_high=t_high):
            for t in range(t_low, t_high):
                ts = slice(8 * t, 8 * t + 8)
                ps = slice(top + 8 * t, top + 8 * t + 8)

                def body_a(k, sides):
                    w = [wa[c, n, k, ts, :] for n in range(7)]
                    pa[c, k + 1, ps, :] = combine(pa[c, k + 1, ps, :], w, sides)

                def body_b(sides):
                    w = [wb[c, n, i, ts, :] for n in range(7)]
                    pb[c, i + 1, ps, :] = combine(pb[c, i + 1, ps, :], w, sides)

                around(pa, pb, 1 - c, c, i, t, body_a, body_b if reach else None)
            return carry

        lax.fori_loop(0, GROUPS, half, 0)
        if reach:
            wrap_pot(c)

    core = slice(top + FIRST, top + FIRST + wide)
    core_flat = parity_of((wide, 128))

    def finish(k, carry):
        red, black = pa[0, k + 1, core, :], pa[1, k + 1, core, :]
        e_red, e_black = ea[0, k + 1, core, :], ea[1, k + 1, core, :]
        q_red = 0.5 * e_red * red * red
        q_black = 0.5 * e_black * black * black
        pot_out[2 * k] = jnp.where(core_flat, red, black)
        pot_out[2 * k + 1] = jnp.where(core_flat, black, red)
        press_out[2 * k] = jnp.where(core_flat, q_red, q_black)
        press_out[2 * k + 1] = jnp.where(core_flat, q_black, q_red)
        return carry

    lax.fori_loop(0, layers, finish, 0)


def geometry(direction, offsets, table):
    c0, c1, c2, w = [lane_pick(table[n], direction) for n in range(4)]
    r0, r1, r2 = offsets
    arms = [c0, c1, c2, r1 * c2 - r2 * c1, r2 * c0 - r0 * c2, r0 * c1 - r1 * c0]
    return arms, w


def store_term(stage, n, value):
    stage[8 * n:8 * n + 8, :] = value


def add_by_slot(stage, slot, width):
    total = stage.shape[0] // 8
    fine = slot & 15
    coarse = slot >> 4
    small = lax.broadcasted_iota(jnp.int32, (16, 128), 0)
    hot, terms = [], []
    for s in range(8):
        match = (jnp.broadcast_to(fine[s:s + 1, :], (16, 128)) == small).astype(F32)
        match = match.astype(jnp.bfloat16)
        part = jnp.broadcast_to(coarse[s:s + 1, :].astype(F32), (16, 128)).astype(jnp.bfloat16)
        none = jnp.zeros((16, 128), jnp.bfloat16)
        hot.append(jnp.concatenate(
            [jnp.where(part == m, match, none) for m in range(width // 16)], axis=0
        ))
        value = stage[pl.ds(s, total, stride=8), :]
        head = value.astype(jnp.bfloat16)
        terms.append(jnp.concatenate(
            [head.astype(F32), value - head.astype(F32)], axis=0
        ).astype(jnp.bfloat16))
    return lax.dot_general(
        jnp.concatenate(terms, axis=1),
        jnp.concatenate(hot, axis=1),
        (((1,), (1,)), ((), ())),
        preferred_element_type=F32,
    )


def fixed_kernel(slots, dirs, pops, rb, table, out, reach, stage, acc, *, width):
    acc[...] = jnp.zeros_like(acc)
    total = stage.shape[0] // 8
    for n in range(6 + len(PAIRS), total):
        store_term(stage, n, jnp.zeros((8, 128), F32))

    def block(b, carry):
        rs = pl.ds(pl.multiple_of(8 * b, 8), 8)
        arms, w = geometry(dirs[rs, :], [rb[n, rs, :] for n in range(3)], table)
        twice = 2.0 * pops[rs, :]
        weighted = [w * arm for arm in arms]
        for n in range(6):
            reach[n, rs, :] = jnp.where(slots[rs, :] >= 0, 6.0 * weighted[n], 0.0)
        for n in range(6):
            store_term(stage, n, twice * arms[n])
        for n, (a, d) in enumerate(PAIRS):
            store_term(stage, 6 + n, weighted[a] * arms[d])
        acc[...] += add_by_slot(stage, slots[rs, :], width)
        return carry

    lax.fori_loop(0, slots.shape[0] // 8, block, 0)
    out[...] = acc[0:total, :] + acc[total:, :]


BATCH = 4
AHEAD = 4


def press_kernel(low, passes, keys, rb0, rb1, rb2, table, press, out, stage, acc, *, width):
    acc[...] = jnp.zeros_like(acc)
    for n in range(6, stage.shape[0] // 8):
        store_term(stage, n, jnp.zeros((8, 128), F32))
    limit = press.shape[0] - 1
    line = lax.broadcasted_iota(jnp.int32, (8, 128), 0)

    def batch(b, carry):
        spots = [pl.ds(pl.multiple_of(8 * (BATCH * b + j), 8), 8) for j in range(BATCH)]
        columns, offsets, starts = [], [], []
        for j in range(BATCH):
            place = (keys[spots[j], :] >> KEY_BITS) + (1 << 18)
            start = [low[8 * (BATCH * b + j) + s] for s in range(8)]
            first = jnp.zeros((8, 128), jnp.int32)
            for s in range(8):
                first = jnp.where(line == s, start[s], first)
            columns.append(place & 127)
            offsets.append((place >> 7) - first)
            starts.append(start)

        def look(m, found):
            found = list(found)
            for j in range(BATCH):
                for t in range(AHEAD):
                    step = AHEAD * m + t
                    window = jnp.zeros((8, 128), F32)
                    for s in range(8):
                        row = press[pl.ds(jnp.minimum(starts[j][s] + step, limit), 1), :]
                        window = jnp.where(line == s, jnp.broadcast_to(row, (8, 128)), window)
                    value = lane_pick(window, columns[j])
                    found[j] = jnp.where(offsets[j] == step, value, found[j])
            return tuple(found)

        found = lax.fori_loop(
            0, passes[b], look, tuple(jnp.zeros((8, 128), F32) for _ in range(BATCH))
        )
        for j in range(BATCH):
            rs = spots[j]
            code = keys[rs, :] & ((1 << KEY_BITS) - 1)
            slot = jnp.floor((code.astype(F32) + 0.5) * (1.0 / 18.0)).astype(jnp.int32)
            direction = code - 18 * slot
            arms, w = geometry(direction, [rb0[rs, :], rb1[rs, :], rb2[rs, :]], table)
            wq = w * found[j]
            for n in range(6):
                store_term(stage, n, wq * arms[n])
            acc[...] += add_by_slot(stage, slot, width)
        return carry

    lax.fori_loop(0, keys.shape[0] // (8 * BATCH), batch, 0)
    total = stage.shape[0] // 8
    out[...] = acc[0:total, :] + acc[total:, :]


def reflect_kernel(slots, reach, pops, motion, out):
    def block(b, carry):
        rs = pl.ds(pl.multiple_of(8 * b, 8), 8)
        slot = slots[rs, :]
        lane = slot & 127
        part = slot >> 7
        along = jnp.zeros((8, 128), F32)
        for n in range(6):
            value = jnp.zeros((8, 128), F32)
            for h in range(motion.shape[1]):
                line = jnp.broadcast_to(motion[n, h:h + 1, :], (8, 128))
                value = jnp.where(part == h, lane_pick(line, lane), value)
            along += reach[n, rs, :] * value
        out[rs, :] = pops[rs, :] - along
        return carry

    lax.fori_loop(0, slots.shape[0] // 8, block, 0)


def ring(axis):
    count = lax.axis_size(axis)
    forward = [(i, (i + 1) % count) for i in range(count)]
    return forward, [(b, a) for a, b in forward]


def scales():
    return jnp.array([POT_SCALE, CHARGE_SCALE, 1.0], F32).reshape(3, 1, 1, 1)


def to_half(strips):
    return (strips * scales()).astype(HALF)


def from_half(strips):
    return strips.astype(F32) * (1.0 / scales())


def vmem(n):
    return [pl.BlockSpec(memory_space=pltpu.VMEM)] * n


PARAMS = pltpu.CompilerParams(vmem_limit_bytes=60 * 1024 * 1024)


def shards(
    eps_field, charge, potential_start, colloid_vel, colloid_spin, link_dir, link_colloid,
    link_site, link_depth, link_pop, link_rb,
):
    depth, wide, long = charge.shape
    layers = depth // 2
    rows = wide + 2 * FIRST
    fx, bx = ring("gx")
    fy, by = ring("gy")

    def edge(part):
        strips = jnp.stack([
            potential_start[:, part] * POT_SCALE,
            charge[:, part] * CHARGE_SCALE,
            eps_field[:, part].astype(F32),
        ])
        return strips.transpose(0, 2, 1, 3).astype(HALF)

    low = lax.ppermute(edge(slice(wide - HALO, wide)), "gx", fx)
    high = lax.ppermute(edge(slice(0, HALO)), "gx", bx)

    per_tile = colloid_vel.shape[1]
    width = 9 * per_tile
    count = link_pop.shape[-1]
    lines = count // 128
    ids = link_colloid.reshape(lines, 128)
    dirs = link_dir.reshape(lines, 128)
    pops = link_pop.reshape(lines, 128)
    rb = link_rb.reshape(3, lines, 128)
    count_x, count_y = lax.axis_size("gx"), lax.axis_size("gy")
    owner = ids // per_tile
    near_x = (owner // count_y - lax.axis_index("gx") + 1) % count_x
    near_y = (owner % count_y - lax.axis_index("gy") + 1) % count_y
    live = ids >= 0
    slots = jnp.where(live, (near_x * 3 + near_y) * per_tile + ids % per_tile, -1)
    place = link_depth.reshape(lines, 128) * (wide * long) + link_site.reshape(lines, 128)
    key = jnp.where(
        live, (place - (1 << 18)) * (1 << KEY_BITS) + slots * 18 + dirs, np.int32(2**31 - 1)
    )
    keys, rb0, rb1, rb2 = lax.sort(
        (key.reshape(-1), rb[0].reshape(-1), rb[1].reshape(-1), rb[2].reshape(-1)),
        num_keys=1, is_stable=False,
    )
    keys, rb0, rb1, rb2, low, high = lax.optimization_barrier((keys, rb0, rb1, rb2, low, high))
    keys = keys.reshape(lines, 128)
    table = direction_table()
    table_rows = ((keys >> KEY_BITS) + (1 << 18)) >> 7
    row_low = jnp.minimum(table_rows[:, 0], depth * wide - 1)
    row_high = jnp.max(jnp.where(table_rows < depth * wide, table_rows, 0), axis=1)
    span = jnp.max((row_high - row_low + 1).reshape(-1, 8 * BATCH), axis=1)
    passes = (jnp.maximum(span, 0) + AHEAD - 1) // AHEAD

    split, to_right, to_left = pl.pallas_call(
        pack_kernel,
        out_shape=(
            jax.ShapeDtypeStruct((6, layers + 1, rows, 128), F32),
            jax.ShapeDtypeStruct((3, GROUPS, wide + 2 * HALO, 128), F32),
            jax.ShapeDtypeStruct((3, GROUPS, wide + 2 * HALO, 128), F32),
        ),
        in_specs=vmem(5), out_specs=tuple(vmem(3)), compiler_params=PARAMS, name="pack",
        scratch_shapes=[pltpu.VMEM((2, 3 * GROUPS, wide + 2 * HALO, 128), F32)],
    )(potential_start, charge, eps_field,
      from_half(low).reshape(-1, 128), from_half(high).reshape(-1, 128))
    from_left = lax.ppermute(to_half(to_right), "gy", fy)
    from_right = lax.ppermute(to_half(to_left), "gy", by)

    terms = 32
    dirs_late, split = lax.optimization_barrier((dirs, split))
    fixed, reach = pl.pallas_call(
        functools.partial(fixed_kernel, width=width),
        out_shape=(
            jax.ShapeDtypeStruct((terms, width), F32), jax.ShapeDtypeStruct((6, lines, 128), F32),
        ),
        in_specs=vmem(5), out_specs=tuple(vmem(2)),
        scratch_shapes=[pltpu.VMEM((8 * terms, 128), F32), pltpu.VMEM((2 * terms, width), F32)],
        compiler_params=PARAMS, name="fixed",
        cost_estimate=pl.CostEstimate(flops=10**9, bytes_accessed=2 * 10**7, transcendentals=0),
    )(slots, dirs_late, pops, rb, table)

    tall = rows + 2 * MARGIN
    potential, press = pl.pallas_call(
        relax_kernel,
        out_shape=(jax.ShapeDtypeStruct(charge.shape, F32),) * 2,
        in_specs=vmem(3), out_specs=tuple(vmem(2)),
        scratch_shapes=[
            pltpu.VMEM((2, layers + 3, tall, 128), F32),
            pltpu.VMEM((2, layers + 3, tall, 128), F32),
            pltpu.VMEM((2, 7, layers + 1, rows, 128), F32),
            pltpu.VMEM((2, GROUPS + 2, tall, 128), F32),
            pltpu.VMEM((2, GROUPS + 2, tall, 128), F32),
            pltpu.VMEM((2, GROUPS, rows, 128), F32),
            pltpu.VMEM((2, 7, GROUPS, rows, 128), F32),
        ],
        compiler_params=PARAMS, name="relax",
    )(split, from_half(from_left), from_half(from_right))

    smem = pl.BlockSpec(memory_space=pltpu.SMEM)
    pressed = pl.pallas_call(
        functools.partial(press_kernel, width=width),
        out_shape=jax.ShapeDtypeStruct((8, width), F32),
        in_specs=[smem, smem] + vmem(6), out_specs=vmem(1)[0],
        scratch_shapes=[pltpu.VMEM((64, 128), F32), pltpu.VMEM((16, width), F32)],
        compiler_params=PARAMS, name="press",
    )(
        row_low, passes, keys, rb0.reshape(lines, 128), rb1.reshape(lines, 128),
        rb2.reshape(lines, 128), table, press.reshape(depth * wide, 128),
    )

    sums = jnp.concatenate([fixed[0:6] + pressed[0:6], fixed[6:27]], axis=0)
    sums = sums.reshape(27, 3, 3, per_tile)
    mid = (
        sums[:, 1]
        + lax.ppermute(sums[:, 0], "gx", bx)
        + lax.ppermute(sums[:, 2], "gx", fx)
    )
    mine = mid[:, 1] + lax.ppermute(mid[:, 0], "gy", by) + lax.ppermute(mid[:, 2], "gy", fy)
    motion = jnp.concatenate([colloid_vel, colloid_spin], axis=0)
    drag = []
    for a in range(6):
        line = jnp.zeros_like(motion[0])
        for d in range(6):
            n = PAIRS.index((min(a, d), max(a, d)))
            line = line + mine[6 + n] * motion[d]
        drag.append(line)
    totals = mine[0:6] - 6.0 * jnp.stack(drag)
    mass = 4.0 / 3.0 * math.pi * RADIUS**3
    inertia = 0.4 * mass * RADIUS**2
    new_motion = jnp.concatenate(
        [motion[0:3] + totals[0:3] / mass, motion[3:6] + totals[3:6] / inertia], axis=0
    )
    report = jnp.concatenate([totals[0:3], totals[3:6] / RADIUS], axis=0)

    column = jnp.stack(
        [lax.ppermute(new_motion, "gy", fy), new_motion, lax.ppermute(new_motion, "gy", by)], axis=1
    )
    around = jnp.stack(
        [lax.ppermute(column, "gx", fx), column, lax.ppermute(column, "gx", bx)], axis=1
    ).reshape(6, width)
    groups = -(-width // 128)
    around = jnp.pad(around, ((0, 0), (0, groups * 128 - width))).reshape(6, groups, 128)
    link_out = pl.pallas_call(
        reflect_kernel,
        out_shape=jax.ShapeDtypeStruct((lines, 128), F32),
        in_specs=vmem(4), out_specs=vmem(1)[0], compiler_params=PARAMS, name="reflect",
    )(slots, reach, pops, around)
    return potential, report, link_out.reshape(link_pop.shape)


def solution(mesh):
    placed = (
        P(None, "gx", "gy"),
        P(None, "gx", "gy"),
        P(None, "gx", "gy"),
        P(None, ("gx", "gy")),
        P(None, ("gx", "gy")),
        P("gx", "gy", None),
        P("gx", "gy", None),
        P("gx", "gy", None),
        P("gx", "gy", None),
        P("gx", "gy", None),
        P(None, "gx", "gy", None),
    )
    return jax.shard_map(
        shards,
        mesh=mesh,
        in_specs=placed,
        out_specs=(P(None, "gx", "gy"), P(None, ("gx", "gy")), P("gx", "gy", None)),
        check_vma=False,
    )
```

```python
import functools
import math

import jax
import jax.numpy as jnp
import numpy as np
from jax import lax
from jax.experimental import pallas as pl
from jax.experimental.pallas import tpu as pltpu
from jax.sharding import PartitionSpec as P

SWEEPS = 6
RADIUS = 8
OVER_RELAX = 1.6
HALO = 2 * SWEEPS
FIRST = 16
MARGIN = 8
GROUPS = 5
SLOT = 2 * HALO
KEY_BITS = 13
F32 = jnp.float32
HALF = jnp.float16
POT_SCALE = 2.0**14
CHARGE_SCALE = 2.0**13

VELOCITY = np.array(
    [
        [1, 0, 0], [-1, 0, 0], [0, 1, 0], [0, -1, 0], [0, 0, 1], [0, 0, -1],
        [1, 1, 0], [1, -1, 0], [-1, 1, 0], [-1, -1, 0], [1, 0, 1], [1, 0, -1],
        [-1, 0, 1], [-1, 0, -1], [0, 1, 1], [0, 1, -1], [0, -1, 1], [0, -1, -1],
    ],
    dtype=np.float32,
)
WEIGHT = np.array([1.0 / 18.0] * 6 + [1.0 / 36.0] * 12, dtype=np.float32)


def direction_table():
    table = np.zeros((4, 8, 128), np.float32)
    table[:3, :, :18] = VELOCITY.T[:, None, :]
    table[3, :, :18] = WEIGHT[None, :]
    return jnp.asarray(table)


PAIRS = [(a, b) for a in range(6) for b in range(a, 6)]


def lane_pick(table, index):
    return jnp.take_along_axis(table, index, axis=1, mode="promise_in_bounds")


def roll(value, shift):
    return pltpu.roll(value, shift % 128, 1)


def lanes_of(shape):
    return lax.broadcasted_iota(jnp.int32, shape, 1)


def parity_of(shape):
    rows = lax.broadcasted_iota(jnp.int32, shape, 0)
    return (rows + lanes_of(shape)) % 2 == 0


def pack_kernel(pot, charge, eps, low, high, split, to_right, to_left, edges):
    depth, wide, _ = pot.shape
    layers = depth // 2
    last = FIRST + wide

    def strip(source, f, z):
        return source[pl.ds(f * HALO * depth + z, HALO, stride=depth), :]

    def build(k, carry):
        for f, field in enumerate((pot, charge, eps)):
            fill = 1.0 if f == 2 else 0.0
            parts = (
                (FIRST, field[2 * k].astype(F32), field[2 * k + 1].astype(F32)),
                (FIRST - HALO, *(strip(low, f, 2 * k + n) for n in range(2))),
                (last, *(strip(high, f, 2 * k + n) for n in range(2))),
            )
            for start, even, odd in parts:
                flat = parity_of(even.shape)
                count = even.shape[0]
                split[2 * f, k, start:start + count, :] = jnp.where(flat, even, odd)
                split[2 * f + 1, k, start:start + count, :] = jnp.where(flat, odd, even)
            spare = FIRST - HALO
            edge = jnp.full((spare, 128), fill, F32)
            for c in range(2):
                split[2 * f + c, k, 0:spare, :] = edge
                split[2 * f + c, k, last + HALO:last + HALO + spare, :] = edge
        return carry

    lax.fori_loop(0, layers, build, 0)
    for f in range(3):
        for c in range(2):
            split[2 * f + c, layers] = jnp.full(
                (split.shape[2], 128), 1.0 if f == 2 else 0.0, F32
            )

    rows = slice(FIRST - HALO, last + HALO)
    lane = lanes_of((wide + 2 * HALO, 128))
    early = lane % SLOT < HALO
    slot_of = [(lane >= SLOT * g) & (lane < SLOT * (g + 1)) for g in range(GROUPS)]

    def gather_edges(n, carry):
        f = n // GROUPS
        i = n % GROUPS
        for c in range(2):
            value = jnp.zeros((wide + 2 * HALO, 128), F32)
            for g in range(GROUPS):
                field = split[2 * f + c, i + GROUPS * g, rows, :]
                value = jnp.where(slot_of[g], roll(field, SLOT * g + HALO), value)
            edges[c, n] = value
        return carry

    lax.fori_loop(0, 3 * GROUPS, gather_edges, 0)

    middle = lane - 2 * (lane % SLOT) + SLOT - 1
    near, same, far = [jnp.clip(middle + n * HALO, 0, 127) for n in (-1, 0, 1)]

    def strips(n, carry):
        f = n // GROUPS
        i = n % GROUPS
        red, black = edges[0, n], edges[1, n]
        to_right[f, i] = jnp.where(early, lane_pick(red, near), lane_pick(black, same))
        to_left[f, i] = jnp.where(early, lane_pick(red, same), lane_pick(black, far))
        return carry

    lax.fori_loop(0, 3 * GROUPS, strips, 0)


def relax_kernel(split, from_left, from_right, pot_out, press_out, pa, ea, wa, pb, eb, cb, wb):
    layers = split.shape[1] - 1
    depth, wide, _ = pot_out.shape
    rows = split.shape[2]
    tiles = rows // 8
    top = MARGIN
    lane = lanes_of((8, 128))
    flat = parity_of((8, 128))
    at_0 = lane == 0
    at_127 = lane == 127
    in_slot = lane % SLOT
    slot_east = in_slot == HALO - 1
    slot_west = in_slot == HALO
    pick = [(lane == SLOT * g + HALO - 1) | (lane == SLOT * g + HALO) for g in range(GROUPS)]

    zero = jnp.zeros((rows + 2 * MARGIN, 128), F32)
    one = jnp.ones((rows + 2 * MARGIN, 128), F32)
    margin0 = jnp.zeros((MARGIN, 128), F32)
    margin1 = jnp.ones((MARGIN, 128), F32)
    for c in range(2):
        pa[c, 0] = zero
        ea[c, 0] = one
        ea[c, layers + 1] = one

    def load_core(k, carry):
        for c in range(2):
            pa[c, k + 1, 0:top, :] = margin0
            pa[c, k + 1, top:top + rows, :] = split[c, k]
            pa[c, k + 1, top + rows:, :] = margin0
            ea[c, k + 1, 0:top, :] = margin1
            ea[c, k + 1, top:top + rows, :] = split[4 + c, k]
            ea[c, k + 1, top + rows:, :] = margin1
        return carry

    lax.fori_loop(0, layers + 1, load_core, 0)
    for c in range(2):
        ea[c, 0, top:top + rows, :] = split[5 - c, 0]
        ea[c, layers + 1, top:top + rows, :] = split[5 - c, layers - 1]
        pa[c, layers + 2] = zero
        ea[c, layers + 2] = one

    first = FIRST - HALO
    high = wide + 2 * HALO
    wide_lane = lanes_of((high, 128))
    wide_first = wide_lane % SLOT < HALO
    wide_used = wide_lane < SLOT * GROUPS
    for c in range(2):
        for i in range(GROUPS + 2):
            pb[c, i] = zero
            eb[c, i] = one
        for i in range(GROUPS):
            cb[c, i] = jnp.zeros((rows, 128), F32)

    for f, target in enumerate((pb, cb, eb)):
        for i in range(GROUPS):
            west = from_left[f, i]
            east = from_right[f, i]
            red = jnp.where(wide_first, east, roll(west, HALO))
            black = jnp.where(wide_first, roll(east, -HALO), west)
            fill = 1.0 if f == 2 else 0.0
            red = jnp.where(wide_used, red, fill)
            black = jnp.where(wide_used, black, fill)
            if f == 1:
                target[0, i, first:first + high, :] = red
                target[1, i, first:first + high, :] = black
            else:
                target[0, i + 1, top + first:top + first + high, :] = red
                target[1, i + 1, top + first:top + first + high, :] = black

    all_lane = lanes_of((rows + 2 * MARGIN, 128))
    lead = all_lane < SLOT
    tail = all_lane >= SLOT * (GROUPS - 1)
    spare_slot = SLOT * (layers // GROUPS)
    in_spare = (all_lane >= spare_slot) & (all_lane < spare_slot + SLOT)

    def wrap_pot(c):
        pb[c, 0] = jnp.where(lead, 0.0, roll(pb[c, GROUPS], SLOT))
        pb[c, GROUPS + 1] = jnp.where(tail, 0.0, roll(pb[c, 1], -SLOT))

    spare_row = layers % GROUPS + 1
    for c in range(2):
        wrap_pot(c)
        eb[c, spare_row] = jnp.where(in_spare, eb[1 - c, spare_row - 1], eb[c, spare_row])
    for c in range(2):
        eb[c, 0] = jnp.where(lead, eb[1 - c, 1], roll(eb[c, GROUPS], SLOT))
        eb[c, GROUPS + 1] = jnp.where(tail, 1.0, roll(eb[c, 1], -SLOT))

    def around(src_a, src_b, other, color, i, t, body_a, body_b):
        r0 = top + 8 * t
        rs = slice(r0, r0 + 8)
        rm = slice(r0 - 1, r0 + 7)
        rp = slice(r0 + 1, r0 + 9)
        up = ~flat if color == 0 else flat
        side = src_b[other, i + 1, rs, :]
        edge = side
        for g in range(GROUPS):
            k = i + GROUPS * g
            here = src_a[other, k + 1, rs, :]
            halo = roll(side, -(SLOT * g + HALO))
            body_a(k, (
                here,
                jnp.where(up, src_a[other, k + 2, rs, :], src_a[other, k, rs, :]),
                src_a[other, k + 1, rm, :],
                src_a[other, k + 1, rp, :],
                jnp.where(at_0, halo, roll(here, 1)),
                jnp.where(at_127, halo, roll(here, -1)),
            ))
            if body_b is not None:
                edge = jnp.where(pick[g], roll(here, SLOT * g + HALO), edge)
        if body_b is not None:
            body_b((
                side,
                jnp.where(up, src_b[other, i, rs, :], src_b[other, i + 2, rs, :]),
                src_b[other, i + 1, rm, :],
                src_b[other, i + 1, rp, :],
                jnp.where(slot_east, edge, roll(side, -1)),
                jnp.where(slot_west, edge, roll(side, 1)),
            ))

    def coefficients(own, charge, sides):
        faces = [0.5 * (own + side) for side in sides]
        total = faces[0] + faces[1] + faces[2] + faces[3] + faces[4] + faces[5]
        scale = OVER_RELAX / total
        return [face * scale for face in faces] + [charge * scale]

    for c in range(2):
        def set_up(i, carry, c=c):
            for t in range(tiles):
                ts = slice(8 * t, 8 * t + 8)
                ps = slice(top + 8 * t, top + 8 * t + 8)

                def body_a(k, sides):
                    values = coefficients(ea[c, k + 1, ps, :], split[2 + c, k, ts, :], sides)
                    for n, value in enumerate(values):
                        wa[c, n, k, ts, :] = value

                def body_b(sides):
                    values = coefficients(eb[c, i + 1, ps, :], cb[c, i, ts, :], sides)
                    live = in_spare[0:8] & (i + 1 == spare_row)
                    for n, value in enumerate(values):
                        wb[c, n, i, ts, :] = jnp.where(live, 0.0, value)

                around(ea, eb, 1 - c, c, i, t, body_a, body_b)
            return carry

        lax.fori_loop(0, GROUPS, set_up, 0)
        for n in range(7):
            wa[c, n, layers] = jnp.zeros((rows, 128), F32)

    def combine(own, w, sides):
        left = w[0] * sides[0] + w[1] * sides[1]
        mid = w[2] * sides[2] + w[3] * sides[3]
        right = w[4] * sides[4] + w[5] * sides[5]
        return (w[6] - (OVER_RELAX - 1.0) * own) + (left + (mid + right))

    for step in range(2 * SWEEPS):
        c = step % 2
        reach = HALO - 1 - step
        t_low = (FIRST - reach) // 8
        t_high = -(-(FIRST + wide + reach) // 8)

        def half(i, carry, c=c, reach=reach, t_low=t_low, t_high=t_high):
            for t in range(t_low, t_high):
                ts = slice(8 * t, 8 * t + 8)
                ps = slice(top + 8 * t, top + 8 * t + 8)

                def body_a(k, sides):
                    w = [wa[c, n, k, ts, :] for n in range(7)]
                    pa[c, k + 1, ps, :] = combine(pa[c, k + 1, ps, :], w, sides)

                def body_b(sides):
                    w = [wb[c, n, i, ts, :] for n in range(7)]
                    pb[c, i + 1, ps, :] = combine(pb[c, i + 1, ps, :], w, sides)

                around(pa, pb, 1 - c, c, i, t, body_a, body_b if reach else None)
            return carry

        lax.fori_loop(0, GROUPS, half, 0)
        if reach:
            wrap_pot(c)

    press_out[depth] = jnp.zeros((wide, 128), F32)
    core = slice(top + FIRST, top + FIRST + wide)
    core_flat = parity_of((wide, 128))

    def finish(k, carry):
        red, black = pa[0, k + 1, core, :], pa[1, k + 1, core, :]
        e_red, e_black = ea[0, k + 1, core, :], ea[1, k + 1, core, :]
        q_red = 0.5 * e_red * red * red
        q_black = 0.5 * e_black * black * black
        pot_out[2 * k] = jnp.where(core_flat, red, black)
        pot_out[2 * k + 1] = jnp.where(core_flat, black, red)
        press_out[2 * k] = jnp.where(core_flat, q_red, q_black)
        press_out[2 * k + 1] = jnp.where(core_flat, q_black, q_red)
        return carry

    lax.fori_loop(0, layers, finish, 0)


def geometry(direction, offsets, table):
    c0, c1, c2, w = [lane_pick(table[n], direction) for n in range(4)]
    r0, r1, r2 = offsets
    arms = [c0, c1, c2, r1 * c2 - r2 * c1, r2 * c0 - r0 * c2, r0 * c1 - r1 * c0]
    return arms, w


def store_term(stage, n, value):
    stage[8 * n:8 * n + 8, :] = value


def add_by_slot(stage, slot, width):
    total = stage.shape[0] // 8
    fine = slot & 15
    coarse = slot >> 4
    small = lax.broadcasted_iota(jnp.int32, (16, 128), 0)
    hot, terms = [], []
    for s in range(8):
        match = (jnp.broadcast_to(fine[s:s + 1, :], (16, 128)) == small).astype(F32)
        match = match.astype(jnp.bfloat16)
        part = jnp.broadcast_to(coarse[s:s + 1, :].astype(F32), (16, 128)).astype(jnp.bfloat16)
        none = jnp.zeros((16, 128), jnp.bfloat16)
        hot.append(jnp.concatenate(
            [jnp.where(part == m, match, none) for m in range(width // 16)], axis=0
        ))
        value = stage[pl.ds(s, total, stride=8), :]
        head = value.astype(jnp.bfloat16)
        terms.append(jnp.concatenate(
            [head.astype(F32), value - head.astype(F32)], axis=0
        ).astype(jnp.bfloat16))
    return lax.dot_general(
        jnp.concatenate(terms, axis=1),
        jnp.concatenate(hot, axis=1),
        (((1,), (1,)), ((), ())),
        preferred_element_type=F32,
    )


def add_by_tile(stage, slot, per_tile):
    total = stage.shape[0] // 8
    shift = per_tile.bit_length() - 1
    tile = (slot >> shift).astype(F32)
    fine = (slot & (per_tile - 1)).astype(F32)
    small = lax.broadcasted_iota(jnp.int32, (per_tile, 128), 0).astype(F32).astype(jnp.bfloat16)
    one = jnp.ones((per_tile, 128), jnp.bfloat16)
    none = jnp.zeros((2 * total, 128), jnp.bfloat16)
    hot, terms = [], []
    for s in range(8):
        place = jnp.broadcast_to(fine[s:s + 1, :], (per_tile, 128)).astype(jnp.bfloat16)
        hot.append(jnp.where(place == small, one, jnp.zeros_like(one)))
        owner = jnp.broadcast_to(tile[s:s + 1, :], (2 * total, 128)).astype(jnp.bfloat16)
        value = stage[pl.ds(s, total, stride=8), :]
        head = value.astype(jnp.bfloat16)
        both = jnp.concatenate([head.astype(F32), value - head.astype(F32)], axis=0)
        both = both.astype(jnp.bfloat16)
        terms.append(jnp.concatenate([jnp.where(owner == t, both, none) for t in range(9)], axis=0))
    return lax.dot_general(
        jnp.concatenate(terms, axis=1),
        jnp.concatenate(hot, axis=1),
        (((1,), (1,)), ((), ())),
        preferred_element_type=F32,
    )


def write_sums(acc, out):
    total = out.shape[1]
    for t in range(9):
        base = 2 * total * t
        out[t] = acc[base:base + total, :] + acc[base + total:base + 2 * total, :]


def fixed_kernel(slots, dirs, pops, rb, table, out, reach, stage, acc, *, width):
    acc[...] = jnp.zeros_like(acc)
    total = stage.shape[0] // 8
    for n in range(6 + len(PAIRS), total):
        store_term(stage, n, jnp.zeros((8, 128), F32))

    def block(b, carry):
        rs = pl.ds(pl.multiple_of(8 * b, 8), 8)
        arms, w = geometry(dirs[rs, :], [rb[n, rs, :] for n in range(3)], table)
        twice = 2.0 * pops[rs, :]
        weighted = [w * arm for arm in arms]
        for n in range(6):
            reach[n, rs, :] = jnp.where(slots[rs, :] >= 0, 6.0 * weighted[n], 0.0)
        for n in range(6):
            store_term(stage, n, twice * arms[n])
        for n, (a, d) in enumerate(PAIRS):
            store_term(stage, 6 + n, weighted[a] * arms[d])
        acc[...] += add_by_slot(stage, slots[rs, :], width)
        return carry

    lax.fori_loop(0, slots.shape[0] // 8, block, 0)
    out[...] = acc[0:total, :] + acc[total:, :]


BATCH = 8
AHEAD = 4


def press_kernel(low, passes, keys, rb0, rb1, rb2, table, press, out, stage, acc, *, per_tile):
    acc[...] = jnp.zeros_like(acc)
    for n in range(6, stage.shape[0] // 8):
        store_term(stage, n, jnp.zeros((8, 128), F32))
    limit = press.shape[0] - AHEAD
    line = lax.broadcasted_iota(jnp.int32, (8, 128), 0)

    def batch(b, carry):
        spots = [pl.ds(pl.multiple_of(8 * (BATCH * b + j), 8), 8) for j in range(BATCH)]
        columns, offsets, starts = [], [], []
        for j in range(BATCH):
            place = (keys[spots[j], :] >> KEY_BITS) + (1 << 18)
            start = [low[8 * (BATCH * b + j) + s] for s in range(8)]
            first = jnp.zeros((8, 128), jnp.int32)
            for s in range(8):
                first = jnp.where(line == s, start[s], first)
            columns.append(place & 127)
            offsets.append((place >> 7) - first)
            starts.append(start)

        def look(m, found):
            found = list(found)
            for j in range(BATCH):
                bases = [jnp.minimum(starts[j][s] + AHEAD * m, limit) for s in range(8)]
                for t in range(AHEAD):
                    window = jnp.zeros((8, 128), F32)
                    for s in range(8):
                        row = press[pl.ds(bases[s] + t, 1), :]
                        window = jnp.where(line == s, jnp.broadcast_to(row, (8, 128)), window)
                    value = lane_pick(window, columns[j])
                    found[j] = jnp.where(offsets[j] == AHEAD * m + t, value, found[j])
            return tuple(found)

        found = lax.fori_loop(
            0, passes[b], look, tuple(jnp.zeros((8, 128), F32) for _ in range(BATCH))
        )
        for j in range(BATCH):
            rs = spots[j]
            code = keys[rs, :] & ((1 << KEY_BITS) - 1)
            slot = jnp.floor((code.astype(F32) + 0.5) * (1.0 / 18.0)).astype(jnp.int32)
            direction = code - 18 * slot
            arms, w = geometry(direction, [rb0[rs, :], rb1[rs, :], rb2[rs, :]], table)
            wq = w * found[j]
            for n in range(6):
                store_term(stage, n, wq * arms[n])
            acc[...] += add_by_tile(stage, slot, per_tile)
        return carry

    lax.fori_loop(0, keys.shape[0] // (8 * BATCH), batch, 0)
    write_sums(acc, out)


TOGETHER = 4


def reflect_kernel(slots, reach, pops, motion, out):
    def batch(b, carry):
        for j in range(TOGETHER):
            rs = pl.ds(pl.multiple_of(8 * (TOGETHER * b + j), 8), 8)
            slot = slots[rs, :]
            lane = slot & 127
            part = slot >> 7
            along = jnp.zeros((8, 128), F32)
            for n in range(6):
                value = jnp.zeros((8, 128), F32)
                for h in range(motion.shape[1]):
                    line = jnp.broadcast_to(motion[n, h:h + 1, :], (8, 128))
                    value = jnp.where(part == h, lane_pick(line, lane), value)
                along += reach[n, rs, :] * value
            out[rs, :] = pops[rs, :] - along
        return carry

    lax.fori_loop(0, slots.shape[0] // (8 * TOGETHER), batch, 0)


def ring(axis):
    count = lax.axis_size(axis)
    forward = [(i, (i + 1) % count) for i in range(count)]
    return forward, [(b, a) for a, b in forward]


def scales():
    return jnp.array([POT_SCALE, CHARGE_SCALE, 1.0], F32).reshape(3, 1, 1, 1)


def to_half(strips):
    return (strips * scales()).astype(HALF)


def from_half(strips):
    return strips.astype(F32) * (1.0 / scales())


def vmem(n):
    return [pl.BlockSpec(memory_space=pltpu.VMEM)] * n


def grant(mib):
    return pltpu.CompilerParams(vmem_limit_bytes=mib * 1024 * 1024)


def shards(
    eps_field, charge, potential_start, colloid_vel, colloid_spin, link_dir, link_colloid,
    link_site, link_depth, link_pop, link_rb,
):
    depth, wide, long = charge.shape
    layers = depth // 2
    rows = wide + 2 * FIRST
    fx, bx = ring("gx")
    fy, by = ring("gy")

    def edge(part):
        strips = jnp.stack([
            potential_start[:, part] * POT_SCALE,
            charge[:, part] * CHARGE_SCALE,
            eps_field[:, part].astype(F32),
        ])
        return strips.transpose(0, 2, 1, 3).astype(HALF)

    low = lax.ppermute(edge(slice(wide - HALO, wide)), "gx", fx)
    high = lax.ppermute(edge(slice(0, HALO)), "gx", bx)

    per_tile = colloid_vel.shape[1]
    width = 9 * per_tile
    count = link_pop.shape[-1]
    lines = count // 128
    ids = link_colloid.reshape(lines, 128)
    dirs = link_dir.reshape(lines, 128)
    pops = link_pop.reshape(lines, 128)
    rb = link_rb.reshape(3, lines, 128)
    count_x, count_y = lax.axis_size("gx"), lax.axis_size("gy")
    owner = ids // per_tile
    near_x = (owner // count_y - lax.axis_index("gx") + 1) % count_x
    near_y = (owner % count_y - lax.axis_index("gy") + 1) % count_y
    live = ids >= 0
    slots = jnp.where(live, (near_x * 3 + near_y) * per_tile + ids % per_tile, -1)
    place = link_depth.reshape(lines, 128) * (wide * long) + link_site.reshape(lines, 128)
    key = jnp.where(
        live, (place - (1 << 18)) * (1 << KEY_BITS) + slots * 18 + dirs, np.int32(2**31 - 1)
    )
    keys, rb0, rb1, rb2 = lax.sort(
        (key.reshape(-1), rb[0].reshape(-1), rb[1].reshape(-1), rb[2].reshape(-1)),
        num_keys=1, is_stable=False,
    )
    keys, rb0, rb1, rb2, low, high = lax.optimization_barrier((keys, rb0, rb1, rb2, low, high))
    keys = keys.reshape(lines, 128)
    table = direction_table()
    table_rows = ((keys >> KEY_BITS) + (1 << 18)) >> 7
    row_low = jnp.minimum(table_rows[:, 0], depth * wide - 1)
    row_high = jnp.max(jnp.where(table_rows < depth * wide, table_rows, 0), axis=1)
    span = jnp.max((row_high - row_low + 1).reshape(-1, 8 * BATCH), axis=1)
    passes = (jnp.maximum(span, 0) + AHEAD - 1) // AHEAD

    split, to_right, to_left = pl.pallas_call(
        pack_kernel,
        out_shape=(
            jax.ShapeDtypeStruct((6, layers + 1, rows, 128), F32),
            jax.ShapeDtypeStruct((3, GROUPS, wide + 2 * HALO, 128), F32),
            jax.ShapeDtypeStruct((3, GROUPS, wide + 2 * HALO, 128), F32),
        ),
        in_specs=vmem(5), out_specs=tuple(vmem(3)), compiler_params=grant(24), name="pack",
        scratch_shapes=[pltpu.VMEM((2, 3 * GROUPS, wide + 2 * HALO, 128), F32)],
    )(potential_start, charge, eps_field,
      from_half(low).reshape(-1, 128), from_half(high).reshape(-1, 128))
    from_left = lax.ppermute(to_half(to_right), "gy", fy)
    from_right = lax.ppermute(to_half(to_left), "gy", by)

    terms = 32
    dirs_late, split = lax.optimization_barrier((dirs, split))
    fixed, reach = pl.pallas_call(
        functools.partial(fixed_kernel, width=width),
        out_shape=(
            jax.ShapeDtypeStruct((terms, width), F32), jax.ShapeDtypeStruct((6, lines, 128), F32),
        ),
        in_specs=vmem(5), out_specs=tuple(vmem(2)),
        scratch_shapes=[pltpu.VMEM((8 * terms, 128), F32), pltpu.VMEM((2 * terms, width), F32)],
        compiler_params=grant(8), name="fixed",
        cost_estimate=pl.CostEstimate(flops=10**9, bytes_accessed=2 * 10**7, transcendentals=0),
    )(slots, dirs_late, pops, rb, table)

    tall = rows + 2 * MARGIN
    potential, press = pl.pallas_call(
        relax_kernel,
        out_shape=(
            jax.ShapeDtypeStruct((depth, wide, 128), F32),
            jax.ShapeDtypeStruct((depth + 1, wide, 128), F32),
        ),
        in_specs=vmem(3), out_specs=tuple(vmem(2)),
        scratch_shapes=[
            pltpu.VMEM((2, layers + 3, tall, 128), F32),
            pltpu.VMEM((2, layers + 3, tall, 128), F32),
            pltpu.VMEM((2, 7, layers + 1, rows, 128), F32),
            pltpu.VMEM((2, GROUPS + 2, tall, 128), F32),
            pltpu.VMEM((2, GROUPS + 2, tall, 128), F32),
            pltpu.VMEM((2, GROUPS, rows, 128), F32),
            pltpu.VMEM((2, 7, GROUPS, rows, 128), F32),
        ],
        compiler_params=grant(44), name="relax",
    )(split, from_half(from_left), from_half(from_right))

    smem = pl.BlockSpec(memory_space=pltpu.SMEM)
    pressed = pl.pallas_call(
        functools.partial(press_kernel, per_tile=per_tile),
        out_shape=jax.ShapeDtypeStruct((9, 8, per_tile), F32),
        in_specs=[smem, smem] + vmem(6), out_specs=vmem(1)[0],
        scratch_shapes=[pltpu.VMEM((64, 128), F32), pltpu.VMEM((9 * 16, per_tile), F32)],
        compiler_params=grant(8), name="press",
    )(
        row_low, passes, keys, rb0.reshape(lines, 128), rb1.reshape(lines, 128),
        rb2.reshape(lines, 128), table, press.reshape(-1, 128),
    )

    fixed = fixed.reshape(terms, 9, per_tile).transpose(1, 0, 2)
    sums = jnp.concatenate([fixed[:, 0:6] + pressed[:, 0:6], fixed[:, 6:27]], axis=1)
    sums = sums.reshape(3, 3, 27, per_tile)
    mid = sums[1] + lax.ppermute(sums[0], "gx", bx) + lax.ppermute(sums[2], "gx", fx)
    mine = mid[1] + lax.ppermute(mid[0], "gy", by) + lax.ppermute(mid[2], "gy", fy)
    motion = jnp.concatenate([colloid_vel, colloid_spin], axis=0)
    drag = []
    for a in range(6):
        line = jnp.zeros_like(motion[0])
        for d in range(6):
            n = PAIRS.index((min(a, d), max(a, d)))
            line = line + mine[6 + n] * motion[d]
        drag.append(line)
    totals = mine[0:6] - 6.0 * jnp.stack(drag)
    mass = 4.0 / 3.0 * math.pi * RADIUS**3
    inertia = 0.4 * mass * RADIUS**2
    new_motion = jnp.concatenate(
        [motion[0:3] + totals[0:3] / mass, motion[3:6] + totals[3:6] / inertia], axis=0
    )
    report = jnp.concatenate([totals[0:3], totals[3:6] / RADIUS], axis=0)

    column = jnp.stack(
        [lax.ppermute(new_motion, "gy", fy), new_motion, lax.ppermute(new_motion, "gy", by)], axis=1
    )
    around = jnp.stack(
        [lax.ppermute(column, "gx", fx), column, lax.ppermute(column, "gx", bx)], axis=1
    ).reshape(6, width)
    groups = -(-width // 128)
    around = jnp.pad(around, ((0, 0), (0, groups * 128 - width))).reshape(6, groups, 128)
    link_out = pl.pallas_call(
        reflect_kernel,
        out_shape=jax.ShapeDtypeStruct((lines, 128), F32),
        in_specs=vmem(4), out_specs=vmem(1)[0], compiler_params=grant(6), name="reflect",
    )(slots, reach, pops, around)
    return potential, report, link_out.reshape(link_pop.shape)


def solution(mesh):
    placed = (
        P(None, "gx", "gy"),
        P(None, "gx", "gy"),
        P(None, "gx", "gy"),
        P(None, ("gx", "gy")),
        P(None, ("gx", "gy")),
        P("gx", "gy", None),
        P("gx", "gy", None),
        P("gx", "gy", None),
        P("gx", "gy", None),
        P("gx", "gy", None),
        P(None, "gx", "gy", None),
    )
    return jax.shard_map(
        shards,
        mesh=mesh,
        in_specs=placed,
        out_specs=(P(None, "gx", "gy"), P(None, ("gx", "gy")), P("gx", "gy", None)),
        check_vma=False,
    )
```

```python
import functools
import math

import jax
import jax.numpy as jnp
import numpy as np
from jax import lax
from jax.experimental import pallas as pl
from jax.experimental.pallas import tpu as pltpu
from jax.sharding import PartitionSpec as P

SWEEPS = 6
RADIUS = 8
OVER_RELAX = 1.6
HALO = 2 * SWEEPS
FIRST = 16
MARGIN = 8
GROUPS = 5
SLOT = 2 * HALO
KEY_BITS = 13
F32 = jnp.float32
HALF = jnp.float16
POT_SCALE = 2.0**14
CHARGE_SCALE = 2.0**13

VELOCITY = np.array(
    [
        [1, 0, 0], [-1, 0, 0], [0, 1, 0], [0, -1, 0], [0, 0, 1], [0, 0, -1],
        [1, 1, 0], [1, -1, 0], [-1, 1, 0], [-1, -1, 0], [1, 0, 1], [1, 0, -1],
        [-1, 0, 1], [-1, 0, -1], [0, 1, 1], [0, 1, -1], [0, -1, 1], [0, -1, -1],
    ],
    dtype=np.float32,
)
WEIGHT = np.array([1.0 / 18.0] * 6 + [1.0 / 36.0] * 12, dtype=np.float32)


def direction_table():
    table = np.zeros((4, 8, 128), np.float32)
    table[:3, :, :18] = VELOCITY.T[:, None, :]
    table[3, :, :18] = WEIGHT[None, :]
    return jnp.asarray(table)


PAIRS = [(a, b) for a in range(6) for b in range(a, 6)]


def lane_pick(table, index):
    return jnp.take_along_axis(table, index, axis=1, mode="promise_in_bounds")


def roll(value, shift):
    return pltpu.roll(value, shift % 128, 1)


def lanes_of(shape):
    return lax.broadcasted_iota(jnp.int32, shape, 1)


def parity_of(shape):
    rows = lax.broadcasted_iota(jnp.int32, shape, 0)
    return (rows + lanes_of(shape)) % 2 == 0


def pack_kernel(pot, charge, eps, low, high, kept, to_right, to_left, split, edges, sem):
    depth, wide, _ = pot.shape
    layers = depth // 2
    last = FIRST + wide

    def strip(source, f, z):
        return source[pl.ds(f * HALO * depth + z, HALO, stride=depth), :]

    def build(k, carry):
        for f, field in enumerate((pot, charge, eps)):
            fill = 1.0 if f == 2 else 0.0
            parts = (
                (FIRST, field[2 * k].astype(F32), field[2 * k + 1].astype(F32)),
                (FIRST - HALO, *(strip(low, f, 2 * k + n) for n in range(2))),
                (last, *(strip(high, f, 2 * k + n) for n in range(2))),
            )
            for start, even, odd in parts:
                flat = parity_of(even.shape)
                count = even.shape[0]
                split[2 * f, k, start:start + count, :] = jnp.where(flat, even, odd)
                split[2 * f + 1, k, start:start + count, :] = jnp.where(flat, odd, even)
            spare = FIRST - HALO
            edge = jnp.full((spare, 128), fill, F32)
            for c in range(2):
                split[2 * f + c, k, 0:spare, :] = edge
                split[2 * f + c, k, last + HALO:last + HALO + spare, :] = edge
        return carry

    lax.fori_loop(0, layers, build, 0)
    for f in range(3):
        for c in range(2):
            split[2 * f + c, layers] = jnp.full(
                (split.shape[2], 128), 1.0 if f == 2 else 0.0, F32
            )

    keep = pltpu.make_async_copy(split, kept, sem)
    keep.start()

    rows = slice(FIRST - HALO, last + HALO)
    lane = lanes_of((wide + 2 * HALO, 128))
    early = lane % SLOT < HALO
    slot_of = [(lane >= SLOT * g) & (lane < SLOT * (g + 1)) for g in range(GROUPS)]

    def gather_edges(n, carry):
        f = n // GROUPS
        i = n % GROUPS
        for c in range(2):
            value = jnp.zeros((wide + 2 * HALO, 128), F32)
            for g in range(GROUPS):
                field = split[2 * f + c, i + GROUPS * g, rows, :]
                value = jnp.where(slot_of[g], roll(field, SLOT * g + HALO), value)
            edges[c, n] = value
        return carry

    lax.fori_loop(0, 3 * GROUPS, gather_edges, 0)

    middle = lane - 2 * (lane % SLOT) + SLOT - 1
    near, same, far = [jnp.clip(middle + n * HALO, 0, 127) for n in (-1, 0, 1)]

    def strips(n, carry):
        f = n // GROUPS
        i = n % GROUPS
        red, black = edges[0, n], edges[1, n]
        to_right[f, i] = jnp.where(early, lane_pick(red, near), lane_pick(black, same))
        to_left[f, i] = jnp.where(early, lane_pick(red, same), lane_pick(black, far))
        return carry

    lax.fori_loop(0, 3 * GROUPS, strips, 0)
    keep.wait()


def relax_kernel(
    kept, from_left, from_right, pot_out, press_out, pa, ea, ca, wa, pb, eb, cb, wb, sems
):
    layers = kept.shape[1] - 1
    depth, wide, _ = pot_out.shape
    rows = kept.shape[2]
    tiles = rows // 8
    top = MARGIN
    lane = lanes_of((8, 128))
    flat = parity_of((8, 128))
    at_0 = lane == 0
    at_127 = lane == 127
    in_slot = lane % SLOT
    slot_east = in_slot == HALO - 1
    slot_west = in_slot == HALO
    pick = [(lane == SLOT * g + HALO - 1) | (lane == SLOT * g + HALO) for g in range(GROUPS)]

    zero = jnp.zeros((rows + 2 * MARGIN, 128), F32)
    one = jnp.ones((rows + 2 * MARGIN, 128), F32)
    margin0 = jnp.zeros((MARGIN, 128), F32)
    margin1 = jnp.ones((MARGIN, 128), F32)
    body = pl.ds(top, rows)
    middle = pl.ds(1, layers + 1)
    loads = []
    for c in range(2):
        loads.append(pltpu.make_async_copy(kept.at[4 + c], ea.at[c, middle, body], sems.at[c]))
        loads.append(pltpu.make_async_copy(kept.at[2 + c], ca.at[c], sems.at[2 + c]))
        loads.append(pltpu.make_async_copy(kept.at[c], pa.at[c, middle, body], sems.at[4 + c]))
        for load in loads[-3:]:
            load.start()

    def set_margins(k, carry):
        for c in range(2):
            for start in (0, top + rows):
                pa[c, k + 1, start:start + MARGIN, :] = margin0
                ea[c, k + 1, start:start + MARGIN, :] = margin1
        return carry

    lax.fori_loop(0, layers + 1, set_margins, 0)
    for c in range(2):
        pa[c, 0] = zero
        pa[c, layers + 2] = zero
        for start in (0, top + rows):
            ea[c, 0, start:start + MARGIN, :] = margin1
        ea[c, layers + 2] = one

    first = FIRST - HALO
    high = wide + 2 * HALO
    wide_lane = lanes_of((high, 128))
    wide_first = wide_lane % SLOT < HALO
    wide_used = wide_lane < SLOT * GROUPS
    for c in range(2):
        for i in range(GROUPS + 2):
            pb[c, i] = zero
            eb[c, i] = one
        for i in range(GROUPS):
            cb[c, i] = jnp.zeros((rows, 128), F32)

    for f, target in enumerate((pb, cb, eb)):
        for i in range(GROUPS):
            west = from_left[f, i]
            east = from_right[f, i]
            red = jnp.where(wide_first, east, roll(west, HALO))
            black = jnp.where(wide_first, roll(east, -HALO), west)
            fill = 1.0 if f == 2 else 0.0
            red = jnp.where(wide_used, red, fill)
            black = jnp.where(wide_used, black, fill)
            if f == 1:
                target[0, i, first:first + high, :] = red
                target[1, i, first:first + high, :] = black
            else:
                target[0, i + 1, top + first:top + first + high, :] = red
                target[1, i + 1, top + first:top + first + high, :] = black

    all_lane = lanes_of((rows + 2 * MARGIN, 128))
    lead = all_lane < SLOT
    tail = all_lane >= SLOT * (GROUPS - 1)
    spare_slot = SLOT * (layers // GROUPS)
    in_spare = (all_lane >= spare_slot) & (all_lane < spare_slot + SLOT)

    def wrap_pot(c):
        pb[c, 0] = jnp.where(lead, 0.0, roll(pb[c, GROUPS], SLOT))
        pb[c, GROUPS + 1] = jnp.where(tail, 0.0, roll(pb[c, 1], -SLOT))

    spare_row = layers % GROUPS + 1
    for c in range(2):
        wrap_pot(c)
        eb[c, spare_row] = jnp.where(in_spare, eb[1 - c, spare_row - 1], eb[c, spare_row])
    for c in range(2):
        eb[c, 0] = jnp.where(lead, eb[1 - c, 1], roll(eb[c, GROUPS], SLOT))
        eb[c, GROUPS + 1] = jnp.where(tail, 1.0, roll(eb[c, 1], -SLOT))

    for load in loads:
        load.wait()
    for c in range(2):
        ea[c, 0, top:top + rows, :] = ea[1 - c, 1, top:top + rows, :]
        ea[c, layers + 1, top:top + rows, :] = ea[1 - c, layers, top:top + rows, :]

    def around(src_a, src_b, other, color, i, t, body_a, body_b):
        r0 = top + 8 * t
        rs = slice(r0, r0 + 8)
        rm = slice(r0 - 1, r0 + 7)
        rp = slice(r0 + 1, r0 + 9)
        up = ~flat if color == 0 else flat
        side = src_b[other, i + 1, rs, :]
        edge = side
        for g in range(GROUPS):
            k = i + GROUPS * g
            here = src_a[other, k + 1, rs, :]
            halo = roll(side, -(SLOT * g + HALO))
            body_a(k, (
                here,
                jnp.where(up, src_a[other, k + 2, rs, :], src_a[other, k, rs, :]),
                src_a[other, k + 1, rm, :],
                src_a[other, k + 1, rp, :],
                jnp.where(at_0, halo, roll(here, 1)),
                jnp.where(at_127, halo, roll(here, -1)),
            ))
            if body_b is not None:
                edge = jnp.where(pick[g], roll(here, SLOT * g + HALO), edge)
        if body_b is not None:
            body_b((
                side,
                jnp.where(up, src_b[other, i, rs, :], src_b[other, i + 2, rs, :]),
                src_b[other, i + 1, rm, :],
                src_b[other, i + 1, rp, :],
                jnp.where(slot_east, edge, roll(side, -1)),
                jnp.where(slot_west, edge, roll(side, 1)),
            ))

    def coefficients(own, charge, sides):
        faces = [0.5 * (own + side) for side in sides]
        total = faces[0] + faces[1] + faces[2] + faces[3] + faces[4] + faces[5]
        scale = OVER_RELAX / total
        return [face * scale for face in faces] + [charge * scale]

    for c in range(2):
        def set_up(i, carry, c=c):
            for t in range(tiles):
                ts = slice(8 * t, 8 * t + 8)
                ps = slice(top + 8 * t, top + 8 * t + 8)

                def body_a(k, sides):
                    values = coefficients(ea[c, k + 1, ps, :], ca[c, k, ts, :], sides)
                    for n, value in enumerate(values):
                        wa[c, n, k, ts, :] = value

                def body_b(sides):
                    values = coefficients(eb[c, i + 1, ps, :], cb[c, i, ts, :], sides)
                    live = in_spare[0:8] & (i + 1 == spare_row)
                    for n, value in enumerate(values):
                        wb[c, n, i, ts, :] = jnp.where(live, 0.0, value)

                around(ea, eb, 1 - c, c, i, t, body_a, body_b)
            return carry

        lax.fori_loop(0, GROUPS, set_up, 0)
        for n in range(7):
            wa[c, n, layers] = jnp.zeros((rows, 128), F32)

    def combine(own, w, sides):
        left = w[0] * sides[0] + w[1] * sides[1]
        mid = w[2] * sides[2] + w[3] * sides[3]
        right = w[4] * sides[4] + w[5] * sides[5]
        return (w[6] - (OVER_RELAX - 1.0) * own) + (left + (mid + right))

    for step in range(2 * SWEEPS):
        c = step % 2
        reach = HALO - 1 - step
        t_low = (FIRST - reach) // 8
        t_high = -(-(FIRST + wide + reach) // 8)

        def half(i, carry, c=c, reach=reach, t_low=t_low, t_high=t_high):
            for t in range(t_low, t_high):
                ts = slice(8 * t, 8 * t + 8)
                ps = slice(top + 8 * t, top + 8 * t + 8)

                def body_a(k, sides):
                    w = [wa[c, n, k, ts, :] for n in range(7)]
                    pa[c, k + 1, ps, :] = combine(pa[c, k + 1, ps, :], w, sides)

                def body_b(sides):
                    w = [wb[c, n, i, ts, :] for n in range(7)]
                    pb[c, i + 1, ps, :] = combine(pb[c, i + 1, ps, :], w, sides)

                around(pa, pb, 1 - c, c, i, t, body_a, body_b if reach else None)
            return carry

        lax.fori_loop(0, GROUPS, half, 0)
        if reach:
            wrap_pot(c)

    press_out[depth] = jnp.zeros((wide, 128), F32)
    core = slice(top + FIRST, top + FIRST + wide)
    core_flat = parity_of((wide, 128))

    def finish(k, carry):
        red, black = pa[0, k + 1, core, :], pa[1, k + 1, core, :]
        e_red, e_black = ea[0, k + 1, core, :], ea[1, k + 1, core, :]
        q_red = 0.5 * e_red * red * red
        q_black = 0.5 * e_black * black * black
        pot_out[2 * k] = jnp.where(core_flat, red, black)
        pot_out[2 * k + 1] = jnp.where(core_flat, black, red)
        press_out[2 * k] = jnp.where(core_flat, q_red, q_black)
        press_out[2 * k + 1] = jnp.where(core_flat, q_black, q_red)
        return carry

    lax.fori_loop(0, layers, finish, 0)


def geometry(direction, offsets, table):
    c0, c1, c2, w = [lane_pick(table[n], direction) for n in range(4)]
    r0, r1, r2 = offsets
    arms = [c0, c1, c2, r1 * c2 - r2 * c1, r2 * c0 - r0 * c2, r0 * c1 - r1 * c0]
    return arms, w


ARM_REACH = 9.0
ARM_BITS = 21
ARM_STEP = 2.0 * ARM_REACH / (2**ARM_BITS - 1)
SPARE_BITS = 32 - ARM_BITS


def pack_arms(rb):
    a, b, c = [jnp.round((rb[n] + ARM_REACH) * (1.0 / ARM_STEP)).astype(jnp.int32) for n in range(3)]
    low = c & ((1 << SPARE_BITS) - 1)
    return (a << SPARE_BITS) | low, (b << SPARE_BITS) | (c >> SPARE_BITS)


def unpack_arms(first, second):
    low = (1 << SPARE_BITS) - 1
    whole = (1 << ARM_BITS) - 1
    a = (first >> SPARE_BITS) & whole
    b = (second >> SPARE_BITS) & whole
    c = ((second & low) << SPARE_BITS) | (first & low)
    return [part.astype(F32) * ARM_STEP - ARM_REACH for part in (a, b, c)]


def store_term(stage, n, value):
    stage[8 * n:8 * n + 8, :] = value


def add_by_slot(stage, slot, width):
    total = stage.shape[0] // 8
    fine = slot & 15
    coarse = slot >> 4
    small = lax.broadcasted_iota(jnp.int32, (16, 128), 0)
    hot, terms = [], []
    for s in range(8):
        match = (jnp.broadcast_to(fine[s:s + 1, :], (16, 128)) == small).astype(F32)
        match = match.astype(jnp.bfloat16)
        part = jnp.broadcast_to(coarse[s:s + 1, :].astype(F32), (16, 128)).astype(jnp.bfloat16)
        none = jnp.zeros((16, 128), jnp.bfloat16)
        hot.append(jnp.concatenate(
            [jnp.where(part == m, match, none) for m in range(width // 16)], axis=0
        ))
        value = stage[pl.ds(s, total, stride=8), :]
        head = value.astype(jnp.bfloat16)
        terms.append(jnp.concatenate(
            [head.astype(F32), value - head.astype(F32)], axis=0
        ).astype(jnp.bfloat16))
    return lax.dot_general(
        jnp.concatenate(terms, axis=1),
        jnp.concatenate(hot, axis=1),
        (((1,), (1,)), ((), ())),
        preferred_element_type=F32,
    )


def add_by_tile(stage, slot, per_tile):
    total = stage.shape[0] // 8
    shift = per_tile.bit_length() - 1
    tile = (slot >> shift).astype(F32)
    fine = (slot & (per_tile - 1)).astype(F32)
    small = lax.broadcasted_iota(jnp.int32, (per_tile, 128), 0).astype(F32).astype(jnp.bfloat16)
    one = jnp.ones((per_tile, 128), jnp.bfloat16)
    none = jnp.zeros((2 * total, 128), jnp.bfloat16)
    hot, terms = [], []
    for s in range(8):
        place = jnp.broadcast_to(fine[s:s + 1, :], (per_tile, 128)).astype(jnp.bfloat16)
        hot.append(jnp.where(place == small, one, jnp.zeros_like(one)))
        owner = jnp.broadcast_to(tile[s:s + 1, :], (2 * total, 128)).astype(jnp.bfloat16)
        value = stage[pl.ds(s, total, stride=8), :]
        head = value.astype(jnp.bfloat16)
        both = jnp.concatenate([head.astype(F32), value - head.astype(F32)], axis=0)
        both = both.astype(jnp.bfloat16)
        terms.append(jnp.concatenate([jnp.where(owner == t, both, none) for t in range(9)], axis=0))
    return lax.dot_general(
        jnp.concatenate(terms, axis=1),
        jnp.concatenate(hot, axis=1),
        (((1,), (1,)), ((), ())),
        preferred_element_type=F32,
    )


def write_sums(acc, out):
    total = out.shape[1]
    for t in range(9):
        base = 2 * total * t
        out[t] = acc[base:base + total, :] + acc[base + total:base + 2 * total, :]


def fixed_kernel(slots, dirs, pops, rb, table, out, reach, stage, acc, *, width):
    acc[...] = jnp.zeros_like(acc)
    total = stage.shape[0] // 8
    for n in range(6 + len(PAIRS), total):
        store_term(stage, n, jnp.zeros((8, 128), F32))

    def block(b, carry):
        rs = pl.ds(pl.multiple_of(8 * b, 8), 8)
        arms, w = geometry(dirs[rs, :], [rb[n, rs, :] for n in range(3)], table)
        twice = 2.0 * pops[rs, :]
        weighted = [w * arm for arm in arms]
        for n in range(6):
            reach[n, rs, :] = jnp.where(slots[rs, :] >= 0, 6.0 * weighted[n], 0.0)
        for n in range(6):
            store_term(stage, n, twice * arms[n])
        for n, (a, d) in enumerate(PAIRS):
            store_term(stage, 6 + n, weighted[a] * arms[d])
        acc[...] += add_by_slot(stage, slots[rs, :], width)
        return carry

    lax.fori_loop(0, slots.shape[0] // 8, block, 0)
    out[...] = acc[0:total, :] + acc[total:, :]


BATCH = 8
AHEAD = 4


def press_kernel(low, passes, keys, arm0, arm1, table, press, out, stage, acc, *, per_tile):
    acc[...] = jnp.zeros_like(acc)
    for n in range(6, stage.shape[0] // 8):
        store_term(stage, n, jnp.zeros((8, 128), F32))
    limit = press.shape[0] - AHEAD
    line = lax.broadcasted_iota(jnp.int32, (8, 128), 0)

    def batch(b, carry):
        spots = [pl.ds(pl.multiple_of(8 * (BATCH * b + j), 8), 8) for j in range(BATCH)]
        columns, offsets, starts = [], [], []
        for j in range(BATCH):
            place = (keys[spots[j], :] >> KEY_BITS) + (1 << 18)
            start = [low[8 * (BATCH * b + j) + s] for s in range(8)]
            first = jnp.zeros((8, 128), jnp.int32)
            for s in range(8):
                first = jnp.where(line == s, start[s], first)
            columns.append(place & 127)
            offsets.append((place >> 7) - first)
            starts.append(start)

        def look(m, found):
            found = list(found)
            for j in range(BATCH):
                bases = [jnp.minimum(starts[j][s] + AHEAD * m, limit) for s in range(8)]
                for t in range(AHEAD):
                    window = jnp.zeros((8, 128), F32)
                    for s in range(8):
                        row = press[pl.ds(bases[s] + t, 1), :]
                        window = jnp.where(line == s, jnp.broadcast_to(row, (8, 128)), window)
                    value = lane_pick(window, columns[j])
                    found[j] = jnp.where(offsets[j] == AHEAD * m + t, value, found[j])
            return tuple(found)

        found = lax.fori_loop(
            0, passes[b], look, tuple(jnp.zeros((8, 128), F32) for _ in range(BATCH))
        )
        for j in range(BATCH):
            rs = spots[j]
            code = keys[rs, :] & ((1 << KEY_BITS) - 1)
            slot = jnp.floor((code.astype(F32) + 0.5) * (1.0 / 18.0)).astype(jnp.int32)
            direction = code - 18 * slot
            arms, w = geometry(direction, unpack_arms(arm0[rs, :], arm1[rs, :]), table)
            wq = w * found[j]
            for n in range(6):
                store_term(stage, n, wq * arms[n])
            acc[...] += add_by_tile(stage, slot, per_tile)
        return carry

    lax.fori_loop(0, keys.shape[0] // (8 * BATCH), batch, 0)
    write_sums(acc, out)


TOGETHER = 4


def reflect_kernel(slots, reach, pops, motion, out):
    def batch(b, carry):
        for j in range(TOGETHER):
            rs = pl.ds(pl.multiple_of(8 * (TOGETHER * b + j), 8), 8)
            slot = slots[rs, :]
            lane = slot & 127
            part = slot >> 7
            along = jnp.zeros((8, 128), F32)
            for n in range(6):
                value = jnp.zeros((8, 128), F32)
                for h in range(motion.shape[1]):
                    line = jnp.broadcast_to(motion[n, h:h + 1, :], (8, 128))
                    value = jnp.where(part == h, lane_pick(line, lane), value)
                along += reach[n, rs, :] * value
            out[rs, :] = pops[rs, :] - along
        return carry

    lax.fori_loop(0, slots.shape[0] // (8 * TOGETHER), batch, 0)


def ring(axis):
    count = lax.axis_size(axis)
    forward = [(i, (i + 1) % count) for i in range(count)]
    return forward, [(b, a) for a, b in forward]


def scales():
    return jnp.array([POT_SCALE, CHARGE_SCALE, 1.0], F32).reshape(3, 1, 1, 1)


def to_half(strips):
    return (strips * scales()).astype(HALF)


def from_half(strips):
    return strips.astype(F32) * (1.0 / scales())


def vmem(n):
    return [pl.BlockSpec(memory_space=pltpu.VMEM)] * n


def grant(mib):
    return pltpu.CompilerParams(vmem_limit_bytes=mib * 1024 * 1024)


def shards(
    eps_field, charge, potential_start, colloid_vel, colloid_spin, link_dir, link_colloid,
    link_site, link_depth, link_pop, link_rb,
):
    depth, wide, long = charge.shape
    layers = depth // 2
    rows = wide + 2 * FIRST
    fx, bx = ring("gx")
    fy, by = ring("gy")

    def edge(part):
        strips = jnp.stack([
            potential_start[:, part] * POT_SCALE,
            charge[:, part] * CHARGE_SCALE,
            eps_field[:, part].astype(F32),
        ])
        return strips.transpose(0, 2, 1, 3).astype(HALF)

    low = lax.ppermute(edge(slice(wide - HALO, wide)), "gx", fx)
    high = lax.ppermute(edge(slice(0, HALO)), "gx", bx)

    per_tile = colloid_vel.shape[1]
    width = 9 * per_tile
    count = link_pop.shape[-1]
    lines = count // 128
    ids = link_colloid.reshape(lines, 128)
    dirs = link_dir.reshape(lines, 128)
    pops = link_pop.reshape(lines, 128)
    rb = link_rb.reshape(3, lines, 128)
    count_x, count_y = lax.axis_size("gx"), lax.axis_size("gy")
    owner = ids // per_tile
    near_x = (owner // count_y - lax.axis_index("gx") + 1) % count_x
    near_y = (owner % count_y - lax.axis_index("gy") + 1) % count_y
    live = ids >= 0
    slots = jnp.where(live, (near_x * 3 + near_y) * per_tile + ids % per_tile, -1)
    place = link_depth.reshape(lines, 128) * (wide * long) + link_site.reshape(lines, 128)
    key = jnp.where(
        live, (place - (1 << 18)) * (1 << KEY_BITS) + slots * 18 + dirs, np.int32(2**31 - 1)
    )
    keys, arm0, arm1 = lax.sort(
        (key.reshape(-1), *(part.reshape(-1) for part in pack_arms(rb))),
        num_keys=1, is_stable=False,
    )
    keys, arm0, arm1, low, high = lax.optimization_barrier((keys, arm0, arm1, low, high))
    keys = keys.reshape(lines, 128)
    table = direction_table()
    table_rows = ((keys >> KEY_BITS) + (1 << 18)) >> 7
    row_low = jnp.minimum(table_rows[:, 0], depth * wide - 1)
    row_high = jnp.max(jnp.where(table_rows < depth * wide, table_rows, 0), axis=1)
    span = jnp.max((row_high - row_low + 1).reshape(-1, 8 * BATCH), axis=1)
    passes = (jnp.maximum(span, 0) + AHEAD - 1) // AHEAD

    split, to_right, to_left = pl.pallas_call(
        pack_kernel,
        out_shape=(
            jax.ShapeDtypeStruct((6, layers + 1, rows, 128), F32),
            jax.ShapeDtypeStruct((3, GROUPS, wide + 2 * HALO, 128), F32),
            jax.ShapeDtypeStruct((3, GROUPS, wide + 2 * HALO, 128), F32),
        ),
        in_specs=vmem(5), out_specs=(pl.BlockSpec(memory_space=pltpu.HBM), *vmem(2)),
        compiler_params=grant(52), name="pack",
        scratch_shapes=[
            pltpu.VMEM((6, layers + 1, rows, 128), F32),
            pltpu.VMEM((2, 3 * GROUPS, wide + 2 * HALO, 128), F32),
            pltpu.SemaphoreType.DMA,
        ],
    )(potential_start, charge, eps_field,
      from_half(low).reshape(-1, 128), from_half(high).reshape(-1, 128))
    to_right, dirs_late = lax.optimization_barrier((to_half(to_right), dirs))
    from_left = lax.ppermute(to_right, "gy", fy)
    from_right = lax.ppermute(to_half(to_left), "gy", by)

    terms = 32
    fixed, reach = pl.pallas_call(
        functools.partial(fixed_kernel, width=width),
        out_shape=(
            jax.ShapeDtypeStruct((terms, width), F32), jax.ShapeDtypeStruct((6, lines, 128), F32),
        ),
        in_specs=vmem(5), out_specs=tuple(vmem(2)),
        scratch_shapes=[pltpu.VMEM((8 * terms, 128), F32), pltpu.VMEM((2 * terms, width), F32)],
        compiler_params=grant(8), name="fixed",
        cost_estimate=pl.CostEstimate(flops=10**9, bytes_accessed=2 * 10**7, transcendentals=0),
    )(slots, dirs_late, pops, rb, table)

    tall = rows + 2 * MARGIN
    potential, press = pl.pallas_call(
        relax_kernel,
        out_shape=(
            jax.ShapeDtypeStruct((depth, wide, 128), F32),
            jax.ShapeDtypeStruct((depth + 1, wide, 128), F32),
        ),
        in_specs=[pl.BlockSpec(memory_space=pltpu.HBM)] + vmem(2), out_specs=tuple(vmem(2)),
        scratch_shapes=[
            pltpu.VMEM((2, layers + 3, tall, 128), F32),
            pltpu.VMEM((2, layers + 3, tall, 128), F32),
            pltpu.VMEM((2, layers + 1, rows, 128), F32),
            pltpu.VMEM((2, 7, layers + 1, rows, 128), F32),
            pltpu.VMEM((2, GROUPS + 2, tall, 128), F32),
            pltpu.VMEM((2, GROUPS + 2, tall, 128), F32),
            pltpu.VMEM((2, GROUPS, rows, 128), F32),
            pltpu.VMEM((2, 7, GROUPS, rows, 128), F32),
            pltpu.SemaphoreType.DMA((6,)),
        ],
        compiler_params=grant(48), name="relax",
    )(split, from_half(from_left), from_half(from_right))

    smem = pl.BlockSpec(memory_space=pltpu.SMEM)
    pressed = pl.pallas_call(
        functools.partial(press_kernel, per_tile=per_tile),
        out_shape=jax.ShapeDtypeStruct((9, 8, per_tile), F32),
        in_specs=[smem, smem] + vmem(5), out_specs=vmem(1)[0],
        scratch_shapes=[pltpu.VMEM((64, 128), F32), pltpu.VMEM((9 * 16, per_tile), F32)],
        compiler_params=grant(8), name="press",
    )(
        row_low, passes, keys, arm0.reshape(lines, 128), arm1.reshape(lines, 128),
        table, press.reshape(-1, 128),
    )

    fixed = fixed.reshape(terms, 9, per_tile).transpose(1, 0, 2)
    sums = jnp.concatenate([fixed[:, 0:6] + pressed[:, 0:6], fixed[:, 6:27]], axis=1)
    sums = sums.reshape(3, 3, 27, per_tile)
    mid = sums[1] + lax.ppermute(sums[0], "gx", bx) + lax.ppermute(sums[2], "gx", fx)
    mine = mid[1] + lax.ppermute(mid[0], "gy", by) + lax.ppermute(mid[2], "gy", fy)
    motion = jnp.concatenate([colloid_vel, colloid_spin], axis=0)
    drag = []
    for a in range(6):
        line = jnp.zeros_like(motion[0])
        for d in range(6):
            n = PAIRS.index((min(a, d), max(a, d)))
            line = line + mine[6 + n] * motion[d]
        drag.append(line)
    totals = mine[0:6] - 6.0 * jnp.stack(drag)
    mass = 4.0 / 3.0 * math.pi * RADIUS**3
    inertia = 0.4 * mass * RADIUS**2
    new_motion = jnp.concatenate(
        [motion[0:3] + totals[0:3] / mass, motion[3:6] + totals[3:6] / inertia], axis=0
    )
    report = jnp.concatenate([totals[0:3], totals[3:6] / RADIUS], axis=0)

    column = jnp.stack(
        [lax.ppermute(new_motion, "gy", fy), new_motion, lax.ppermute(new_motion, "gy", by)], axis=1
    )
    around = jnp.stack(
        [lax.ppermute(column, "gx", fx), column, lax.ppermute(column, "gx", bx)], axis=1
    ).reshape(6, width)
    groups = -(-width // 128)
    around = jnp.pad(around, ((0, 0), (0, groups * 128 - width))).reshape(6, groups, 128)
    link_out = pl.pallas_call(
        reflect_kernel,
        out_shape=jax.ShapeDtypeStruct((lines, 128), F32),
        in_specs=vmem(4), out_specs=vmem(1)[0], compiler_params=grant(6), name="reflect",
    )(slots, reach, pops, around)
    return potential, report, link_out.reshape(link_pop.shape)


def solution(mesh):
    placed = (
        P(None, "gx", "gy"),
        P(None, "gx", "gy"),
        P(None, "gx", "gy"),
        P(None, ("gx", "gy")),
        P(None, ("gx", "gy")),
        P("gx", "gy", None),
        P("gx", "gy", None),
        P("gx", "gy", None),
        P("gx", "gy", None),
        P("gx", "gy", None),
        P(None, "gx", "gy", None),
    )
    return jax.shard_map(
        shards,
        mesh=mesh,
        in_specs=placed,
        out_specs=(P(None, "gx", "gy"), P(None, ("gx", "gy")), P("gx", "gy", None)),
        check_vma=False,
    )
```

```python
import functools
import math

import jax
import jax.numpy as jnp
import numpy as np
from jax import lax
from jax.experimental import pallas as pl
from jax.experimental.pallas import tpu as pltpu
from jax.sharding import PartitionSpec as P

SWEEPS = 6
RADIUS = 8
OVER_RELAX = 1.6
HALO = 2 * SWEEPS
FIRST = 16
MARGIN = 8
GROUPS = 5
SLOT = 2 * HALO
KEY_BITS = 13
F32 = jnp.float32
HALF = jnp.float16
POT_SCALE = 2.0**14
CHARGE_SCALE = 2.0**13

VELOCITY = np.array(
    [
        [1, 0, 0], [-1, 0, 0], [0, 1, 0], [0, -1, 0], [0, 0, 1], [0, 0, -1],
        [1, 1, 0], [1, -1, 0], [-1, 1, 0], [-1, -1, 0], [1, 0, 1], [1, 0, -1],
        [-1, 0, 1], [-1, 0, -1], [0, 1, 1], [0, 1, -1], [0, -1, 1], [0, -1, -1],
    ],
    dtype=np.float32,
)
WEIGHT = np.array([1.0 / 18.0] * 6 + [1.0 / 36.0] * 12, dtype=np.float32)


def direction_table():
    table = np.zeros((4, 8, 128), np.float32)
    table[:3, :, :18] = VELOCITY.T[:, None, :]
    table[3, :, :18] = WEIGHT[None, :]
    return jnp.asarray(table)


PAIRS = [(a, b) for a in range(6) for b in range(a, 6)]


def lane_pick(table, index):
    return jnp.take_along_axis(table, index, axis=1, mode="promise_in_bounds")


def roll(value, shift):
    return pltpu.roll(value, shift % 128, 1)


def lanes_of(shape):
    return lax.broadcasted_iota(jnp.int32, shape, 1)


def parity_of(shape):
    rows = lax.broadcasted_iota(jnp.int32, shape, 0)
    return (rows + lanes_of(shape)) % 2 == 0


def pack_kernel(pot, charge, eps, low, high, kept, to_right, to_left, split, edges, sem):
    depth, wide, _ = pot.shape
    layers = depth // 2
    last = FIRST + wide

    def strip(source, f, z):
        return source[pl.ds(f * HALO * depth + z, HALO, stride=depth), :]

    def build(k, carry):
        for f, field in enumerate((pot, charge, eps)):
            fill = 1.0 if f == 2 else 0.0
            parts = (
                (FIRST, field[2 * k].astype(F32), field[2 * k + 1].astype(F32)),
                (FIRST - HALO, *(strip(low, f, 2 * k + n) for n in range(2))),
                (last, *(strip(high, f, 2 * k + n) for n in range(2))),
            )
            for start, even, odd in parts:
                flat = parity_of(even.shape)
                count = even.shape[0]
                split[2 * f, k, start:start + count, :] = jnp.where(flat, even, odd)
                split[2 * f + 1, k, start:start + count, :] = jnp.where(flat, odd, even)
            spare = FIRST - HALO
            edge = jnp.full((spare, 128), fill, F32)
            for c in range(2):
                split[2 * f + c, k, 0:spare, :] = edge
                split[2 * f + c, k, last + HALO:last + HALO + spare, :] = edge
        return carry

    lax.fori_loop(0, layers, build, 0)
    for f in range(3):
        for c in range(2):
            split[2 * f + c, layers] = jnp.full(
                (split.shape[2], 128), 1.0 if f == 2 else 0.0, F32
            )

    keep = pltpu.make_async_copy(split, kept, sem)
    keep.start()

    rows = slice(FIRST - HALO, last + HALO)
    lane = lanes_of((wide + 2 * HALO, 128))
    early = lane % SLOT < HALO
    slot_of = [(lane >= SLOT * g) & (lane < SLOT * (g + 1)) for g in range(GROUPS)]

    def gather_edges(n, carry):
        f = n // GROUPS
        i = n % GROUPS
        for c in range(2):
            value = jnp.zeros((wide + 2 * HALO, 128), F32)
            for g in range(GROUPS):
                field = split[2 * f + c, i + GROUPS * g, rows, :]
                value = jnp.where(slot_of[g], roll(field, SLOT * g + HALO), value)
            edges[c, n] = value
        return carry

    lax.fori_loop(0, 3 * GROUPS, gather_edges, 0)

    middle = lane - 2 * (lane % SLOT) + SLOT - 1
    near, same, far = [jnp.clip(middle + n * HALO, 0, 127) for n in (-1, 0, 1)]

    def strips(n, carry):
        f = n // GROUPS
        i = n % GROUPS
        red, black = edges[0, n], edges[1, n]
        to_right[f, i] = jnp.where(early, lane_pick(red, near), lane_pick(black, same))
        to_left[f, i] = jnp.where(early, lane_pick(red, same), lane_pick(black, far))
        return carry

    lax.fori_loop(0, 3 * GROUPS, strips, 0)
    keep.wait()


def relax_kernel(
    kept, from_left, from_right, pot_out, press_out, pa, ea, ca, wa, pb, eb, cb, wb, sems
):
    layers = kept.shape[1] - 1
    depth, wide, _ = pot_out.shape
    rows = kept.shape[2]
    tiles = rows // 8
    top = MARGIN
    lane = lanes_of((8, 128))
    flat = parity_of((8, 128))
    at_0 = lane == 0
    at_127 = lane == 127
    in_slot = lane % SLOT
    slot_east = in_slot == HALO - 1
    slot_west = in_slot == HALO
    pick = [(lane == SLOT * g + HALO - 1) | (lane == SLOT * g + HALO) for g in range(GROUPS)]

    zero = jnp.zeros((rows + 2 * MARGIN, 128), F32)
    one = jnp.ones((rows + 2 * MARGIN, 128), F32)
    margin0 = jnp.zeros((MARGIN, 128), F32)
    margin1 = jnp.ones((MARGIN, 128), F32)
    body = pl.ds(top, rows)
    middle = pl.ds(1, layers + 1)
    loads = []
    for c in range(2):
        loads.append(pltpu.make_async_copy(kept.at[4 + c], ea.at[c, middle, body], sems.at[c]))
        loads.append(pltpu.make_async_copy(kept.at[2 + c], ca.at[c], sems.at[2 + c]))
        loads.append(pltpu.make_async_copy(kept.at[c], pa.at[c, middle, body], sems.at[4 + c]))
        for load in loads[-3:]:
            load.start()

    def set_margins(k, carry):
        for c in range(2):
            for start in (0, top + rows):
                pa[c, k + 1, start:start + MARGIN, :] = margin0
                ea[c, k + 1, start:start + MARGIN, :] = margin1
        return carry

    lax.fori_loop(0, layers + 1, set_margins, 0)
    for c in range(2):
        pa[c, 0] = zero
        pa[c, layers + 2] = zero
        for start in (0, top + rows):
            ea[c, 0, start:start + MARGIN, :] = margin1
        ea[c, layers + 2] = one

    first = FIRST - HALO
    high = wide + 2 * HALO
    wide_lane = lanes_of((high, 128))
    wide_first = wide_lane % SLOT < HALO
    wide_used = wide_lane < SLOT * GROUPS
    for c in range(2):
        for i in range(GROUPS + 2):
            pb[c, i] = zero
            eb[c, i] = one
        for i in range(GROUPS):
            cb[c, i] = jnp.zeros((rows, 128), F32)

    for f, target in enumerate((pb, cb, eb)):
        for i in range(GROUPS):
            west = from_left[f, i]
            east = from_right[f, i]
            red = jnp.where(wide_first, east, roll(west, HALO))
            black = jnp.where(wide_first, roll(east, -HALO), west)
            fill = 1.0 if f == 2 else 0.0
            red = jnp.where(wide_used, red, fill)
            black = jnp.where(wide_used, black, fill)
            if f == 1:
                target[0, i, first:first + high, :] = red
                target[1, i, first:first + high, :] = black
            else:
                target[0, i + 1, top + first:top + first + high, :] = red
                target[1, i + 1, top + first:top + first + high, :] = black

    all_lane = lanes_of((rows + 2 * MARGIN, 128))
    lead = all_lane < SLOT
    tail = all_lane >= SLOT * (GROUPS - 1)
    spare_slot = SLOT * (layers // GROUPS)
    in_spare = (all_lane >= spare_slot) & (all_lane < spare_slot + SLOT)

    def wrap_pot(c):
        pb[c, 0] = jnp.where(lead, 0.0, roll(pb[c, GROUPS], SLOT))
        pb[c, GROUPS + 1] = jnp.where(tail, 0.0, roll(pb[c, 1], -SLOT))

    spare_row = layers % GROUPS + 1
    for c in range(2):
        wrap_pot(c)
        eb[c, spare_row] = jnp.where(in_spare, eb[1 - c, spare_row - 1], eb[c, spare_row])
    for c in range(2):
        eb[c, 0] = jnp.where(lead, eb[1 - c, 1], roll(eb[c, GROUPS], SLOT))
        eb[c, GROUPS + 1] = jnp.where(tail, 1.0, roll(eb[c, 1], -SLOT))

    for load in loads:
        load.wait()
    for c in range(2):
        ea[c, 0, top:top + rows, :] = ea[1 - c, 1, top:top + rows, :]
        ea[c, layers + 1, top:top + rows, :] = ea[1 - c, layers, top:top + rows, :]

    def around(src_a, src_b, other, color, i, t, body_a, body_b):
        r0 = top + 8 * t
        rs = slice(r0, r0 + 8)
        rm = slice(r0 - 1, r0 + 7)
        rp = slice(r0 + 1, r0 + 9)
        up = ~flat if color == 0 else flat
        side = src_b[other, i + 1, rs, :]
        edge = side
        for g in range(GROUPS):
            k = i + GROUPS * g
            here = src_a[other, k + 1, rs, :]
            halo = roll(side, -(SLOT * g + HALO))
            body_a(k, (
                here,
                jnp.where(up, src_a[other, k + 2, rs, :], src_a[other, k, rs, :]),
                src_a[other, k + 1, rm, :],
                src_a[other, k + 1, rp, :],
                jnp.where(at_0, halo, roll(here, 1)),
                jnp.where(at_127, halo, roll(here, -1)),
            ))
            if body_b is not None:
                edge = jnp.where(pick[g], roll(here, SLOT * g + HALO), edge)
        if body_b is not None:
            body_b((
                side,
                jnp.where(up, src_b[other, i, rs, :], src_b[other, i + 2, rs, :]),
                src_b[other, i + 1, rm, :],
                src_b[other, i + 1, rp, :],
                jnp.where(slot_east, edge, roll(side, -1)),
                jnp.where(slot_west, edge, roll(side, 1)),
            ))

    def coefficients(own, charge, sides):
        faces = [0.5 * (own + side) for side in sides]
        total = faces[0] + faces[1] + faces[2] + faces[3] + faces[4] + faces[5]
        scale = OVER_RELAX / total
        return [face * scale for face in faces] + [charge * scale]

    for c in range(2):
        def set_up(i, carry, c=c):
            for t in range(tiles):
                ts = slice(8 * t, 8 * t + 8)
                ps = slice(top + 8 * t, top + 8 * t + 8)

                def body_a(k, sides):
                    values = coefficients(ea[c, k + 1, ps, :], ca[c, k, ts, :], sides)
                    for n, value in enumerate(values):
                        wa[c, n, k, ts, :] = value

                def body_b(sides):
                    values = coefficients(eb[c, i + 1, ps, :], cb[c, i, ts, :], sides)
                    live = in_spare[0:8] & (i + 1 == spare_row)
                    for n, value in enumerate(values):
                        wb[c, n, i, ts, :] = jnp.where(live, 0.0, value)

                around(ea, eb, 1 - c, c, i, t, body_a, body_b)
            return carry

        lax.fori_loop(0, GROUPS, set_up, 0)
        for n in range(7):
            wa[c, n, layers] = jnp.zeros((rows, 128), F32)

    def combine(own, w, sides):
        left = w[0] * sides[0] + w[1] * sides[1]
        mid = w[2] * sides[2] + w[3] * sides[3]
        right = w[4] * sides[4] + w[5] * sides[5]
        return (w[6] - (OVER_RELAX - 1.0) * own) + (left + (mid + right))

    for step in range(2 * SWEEPS):
        c = step % 2
        reach = HALO - 1 - step
        t_low = (FIRST - reach) // 8
        t_high = -(-(FIRST + wide + reach) // 8)

        def half(i, carry, c=c, reach=reach, t_low=t_low, t_high=t_high):
            for t in range(t_low, t_high):
                ts = slice(8 * t, 8 * t + 8)
                ps = slice(top + 8 * t, top + 8 * t + 8)

                def body_a(k, sides):
                    w = [wa[c, n, k, ts, :] for n in range(7)]
                    pa[c, k + 1, ps, :] = combine(pa[c, k + 1, ps, :], w, sides)

                def body_b(sides):
                    w = [wb[c, n, i, ts, :] for n in range(7)]
                    pb[c, i + 1, ps, :] = combine(pb[c, i + 1, ps, :], w, sides)

                around(pa, pb, 1 - c, c, i, t, body_a, body_b if reach else None)
            return carry

        lax.fori_loop(0, GROUPS, half, 0)
        if reach:
            wrap_pot(c)

    press_out[depth] = jnp.zeros((wide, 128), F32)
    core = slice(top + FIRST, top + FIRST + wide)
    core_flat = parity_of((wide, 128))

    def finish(k, carry):
        red, black = pa[0, k + 1, core, :], pa[1, k + 1, core, :]
        e_red, e_black = ea[0, k + 1, core, :], ea[1, k + 1, core, :]
        q_red = 0.5 * e_red * red * red
        q_black = 0.5 * e_black * black * black
        pot_out[2 * k] = jnp.where(core_flat, red, black)
        pot_out[2 * k + 1] = jnp.where(core_flat, black, red)
        press_out[2 * k] = jnp.where(core_flat, q_red, q_black)
        press_out[2 * k + 1] = jnp.where(core_flat, q_black, q_red)
        return carry

    lax.fori_loop(0, layers, finish, 0)


def geometry(direction, offsets, table):
    c0, c1, c2, w = [lane_pick(table[n], direction) for n in range(4)]
    r0, r1, r2 = offsets
    arms = [c0, c1, c2, r1 * c2 - r2 * c1, r2 * c0 - r0 * c2, r0 * c1 - r1 * c0]
    return arms, w


ARM_REACH = 9.0
ARM_BITS = 21
ARM_STEP = 2.0 * ARM_REACH / (2**ARM_BITS - 1)
SPARE_BITS = 32 - ARM_BITS


def pack_arms(rb):
    a, b, c = [jnp.round((rb[n] + ARM_REACH) * (1.0 / ARM_STEP)).astype(jnp.int32) for n in range(3)]
    low = c & ((1 << SPARE_BITS) - 1)
    return (a << SPARE_BITS) | low, (b << SPARE_BITS) | (c >> SPARE_BITS)


def unpack_arms(first, second):
    low = (1 << SPARE_BITS) - 1
    whole = (1 << ARM_BITS) - 1
    a = (first >> SPARE_BITS) & whole
    b = (second >> SPARE_BITS) & whole
    c = ((second & low) << SPARE_BITS) | (first & low)
    return [part.astype(F32) * ARM_STEP - ARM_REACH for part in (a, b, c)]


def store_term(stage, n, value):
    stage[8 * n:8 * n + 8, :] = value


def add_by_slot(stage, slot, width):
    total = stage.shape[0] // 8
    fine = slot & 15
    coarse = slot >> 4
    small = lax.broadcasted_iota(jnp.int32, (16, 128), 0)
    hot, terms = [], []
    for s in range(8):
        match = (jnp.broadcast_to(fine[s:s + 1, :], (16, 128)) == small).astype(F32)
        match = match.astype(jnp.bfloat16)
        part = jnp.broadcast_to(coarse[s:s + 1, :].astype(F32), (16, 128)).astype(jnp.bfloat16)
        none = jnp.zeros((16, 128), jnp.bfloat16)
        hot.append(jnp.concatenate(
            [jnp.where(part == m, match, none) for m in range(width // 16)], axis=0
        ))
        value = stage[pl.ds(s, total, stride=8), :]
        head = value.astype(jnp.bfloat16)
        terms.append(jnp.concatenate(
            [head.astype(F32), value - head.astype(F32)], axis=0
        ).astype(jnp.bfloat16))
    return lax.dot_general(
        jnp.concatenate(terms, axis=1),
        jnp.concatenate(hot, axis=1),
        (((1,), (1,)), ((), ())),
        preferred_element_type=F32,
    )


def add_by_tile(stage, slot, per_tile):
    total = stage.shape[0] // 8
    shift = per_tile.bit_length() - 1
    tile = (slot >> shift).astype(F32)
    fine = (slot & (per_tile - 1)).astype(F32)
    small = lax.broadcasted_iota(jnp.int32, (per_tile, 128), 0).astype(F32).astype(jnp.bfloat16)
    one = jnp.ones((per_tile, 128), jnp.bfloat16)
    none = jnp.zeros((2 * total, 128), jnp.bfloat16)
    hot, terms = [], []
    for s in range(8):
        place = jnp.broadcast_to(fine[s:s + 1, :], (per_tile, 128)).astype(jnp.bfloat16)
        hot.append(jnp.where(place == small, one, jnp.zeros_like(one)))
        owner = jnp.broadcast_to(tile[s:s + 1, :], (2 * total, 128)).astype(jnp.bfloat16)
        value = stage[pl.ds(s, total, stride=8), :]
        head = value.astype(jnp.bfloat16)
        both = jnp.concatenate([head.astype(F32), value - head.astype(F32)], axis=0)
        both = both.astype(jnp.bfloat16)
        terms.append(jnp.concatenate([jnp.where(owner == t, both, none) for t in range(9)], axis=0))
    return lax.dot_general(
        jnp.concatenate(terms, axis=1),
        jnp.concatenate(hot, axis=1),
        (((1,), (1,)), ((), ())),
        preferred_element_type=F32,
    )


def write_sums(acc, out):
    total = out.shape[1]
    for t in range(9):
        base = 2 * total * t
        out[t] = acc[base:base + total, :] + acc[base + total:base + 2 * total, :]


def fixed_kernel(slots, dirs, pops, rb, table, out, reach, stage, acc, *, width):
    acc[...] = jnp.zeros_like(acc)
    total = stage.shape[0] // 8
    for n in range(6 + len(PAIRS), total):
        store_term(stage, n, jnp.zeros((8, 128), F32))

    def block(b, carry):
        rs = pl.ds(pl.multiple_of(8 * b, 8), 8)
        arms, w = geometry(dirs[rs, :], [rb[n, rs, :] for n in range(3)], table)
        twice = 2.0 * pops[rs, :]
        weighted = [w * arm for arm in arms]
        for n in range(6):
            reach[n, rs, :] = jnp.where(slots[rs, :] >= 0, 6.0 * weighted[n], 0.0)
        for n in range(6):
            store_term(stage, n, twice * arms[n])
        for n, (a, d) in enumerate(PAIRS):
            store_term(stage, 6 + n, weighted[a] * arms[d])
        acc[...] += add_by_slot(stage, slots[rs, :], width)
        return carry

    lax.fori_loop(0, slots.shape[0] // 8, block, 0)
    out[...] = acc[0:total, :] + acc[total:, :]


BATCH = 8
AHEAD = 4


def press_kernel(low, passes, keys, arm0, arm1, table, press, out, stage, acc, *, per_tile):
    acc[...] = jnp.zeros_like(acc)
    for n in range(6, stage.shape[0] // 8):
        store_term(stage, n, jnp.zeros((8, 128), F32))
    limit = press.shape[0] - AHEAD
    line = lax.broadcasted_iota(jnp.int32, (8, 128), 0)

    def batch(b, carry):
        spots = [pl.ds(pl.multiple_of(8 * (BATCH * b + j), 8), 8) for j in range(BATCH)]
        columns, offsets, starts = [], [], []
        for j in range(BATCH):
            place = (keys[spots[j], :] >> KEY_BITS) + (1 << 18)
            start = [low[8 * (BATCH * b + j) + s] for s in range(8)]
            first = jnp.zeros((8, 128), jnp.int32)
            for s in range(8):
                first = jnp.where(line == s, start[s], first)
            columns.append(place & 127)
            offsets.append((place >> 7) - first)
            starts.append(start)

        def look(m, found):
            found = list(found)
            for j in range(BATCH):
                bases = [jnp.minimum(starts[j][s] + AHEAD * m, limit) for s in range(8)]
                for t in range(AHEAD):
                    window = jnp.zeros((8, 128), F32)
                    for s in range(8):
                        row = press[pl.ds(bases[s] + t, 1), :]
                        window = jnp.where(line == s, jnp.broadcast_to(row, (8, 128)), window)
                    value = lane_pick(window, columns[j])
                    found[j] = jnp.where(offsets[j] == AHEAD * m + t, value, found[j])
            return tuple(found)

        found = lax.fori_loop(
            0, passes[b], look, tuple(jnp.zeros((8, 128), F32) for _ in range(BATCH))
        )
        for j in range(BATCH):
            rs = spots[j]
            code = keys[rs, :] & ((1 << KEY_BITS) - 1)
            slot = jnp.floor((code.astype(F32) + 0.5) * (1.0 / 18.0)).astype(jnp.int32)
            direction = code - 18 * slot
            arms, w = geometry(direction, unpack_arms(arm0[rs, :], arm1[rs, :]), table)
            wq = w * found[j]
            for n in range(6):
                store_term(stage, n, wq * arms[n])
            acc[...] += add_by_tile(stage, slot, per_tile)
        return carry

    lax.fori_loop(0, keys.shape[0] // (8 * BATCH), batch, 0)
    write_sums(acc, out)


TOGETHER = 4
AROUND = [(ox, oy) for ox in range(-2, 3) for oy in range(-2, 3)]


def reflect_kernel(
    home, partial_sums, slots, reach, pops, motion, report, out, *, per_tile, counts
):
    lanes = motion.shape[1]
    slot_of_lane = lax.broadcasted_iota(jnp.int32, (8, lanes), 1) // per_tile
    tile_x = slot_of_lane // 3 - 1
    tile_y = slot_of_lane % 3 - 1
    totals = jnp.zeros((8, lanes), F32)
    for ox, oy in AROUND:
        near = (abs(tile_x - ox) <= 1) & (abs(tile_y - oy) <= 1) & (slot_of_lane < 9)
        shift = per_tile * (3 * ox + oy)
        peer_x = lax.rem(home[0] + ox + 2 * counts[0], counts[0])
        peer_y = lax.rem(home[1] + oy + 2 * counts[1], counts[1])
        peer = peer_x * counts[1] + peer_y
        moved = pltpu.roll(partial_sums[peer], shift % lanes, 1)
        totals = totals + jnp.where(near, moved, 0.0)
    mass = 4.0 / 3.0 * math.pi * RADIUS**3
    inertia = 0.4 * mass * RADIUS**2
    is_force = lax.broadcasted_iota(jnp.int32, (8, lanes), 0) < 3
    moved = motion[...] + totals * jnp.where(is_force, 1.0 / mass, 1.0 / inertia)
    stated = totals * jnp.where(is_force, 1.0, 1.0 / RADIUS)
    report[...] = stated[0:6, 4 * per_tile:5 * per_tile]

    table = [
        [jnp.broadcast_to(moved[n:n + 1, 128 * h:128 * h + 128], (8, 128)) for h in range(lanes // 128)]
        for n in range(6)
    ]

    def batch(b, carry):
        for j in range(TOGETHER):
            rs = pl.ds(pl.multiple_of(8 * (TOGETHER * b + j), 8), 8)
            slot = slots[rs, :]
            lane = slot & 127
            part = slot >> 7
            along = jnp.zeros((8, 128), F32)
            for n in range(6):
                value = jnp.zeros((8, 128), F32)
                for h in range(lanes // 128):
                    value = jnp.where(part == h, lane_pick(table[n][h], lane), value)
                along += reach[n, rs, :] * value
            out[rs, :] = pops[rs, :] - along
        return carry

    lax.fori_loop(0, slots.shape[0] // (8 * TOGETHER), batch, 0)


def ring(axis):
    count = lax.axis_size(axis)
    forward = [(i, (i + 1) % count) for i in range(count)]
    return forward, [(b, a) for a, b in forward]


def scales():
    return jnp.array([POT_SCALE, CHARGE_SCALE, 1.0], F32).reshape(3, 1, 1, 1)


def to_half(strips):
    return (strips * scales()).astype(HALF)


def from_half(strips):
    return strips.astype(F32) * (1.0 / scales())


MOTION_SCALE = 2.0**10
REST_SCALE = 2.0**12


def motion_plane(motions, rows):
    value = motions.reshape(-1, motions.shape[-1]) * MOTION_SCALE
    head = lax.reduce_precision(value, 8, 10)
    both = jnp.concatenate([head, (value - head) * REST_SCALE], axis=0).astype(HALF)
    return jnp.pad(both, ((0, rows - both.shape[0]), (0, 128 - both.shape[1])))[None]


def motion_of(plane, shape):
    count = math.prod(shape[:-1])
    both = plane[:2 * count, :shape[-1]].astype(F32)
    value = both[:count] + both[count:] * (1.0 / REST_SCALE)
    return (value * (1.0 / MOTION_SCALE)).reshape(shape)


def vmem(n):
    return [pl.BlockSpec(memory_space=pltpu.VMEM)] * n


def grant(mib):
    return pltpu.CompilerParams(vmem_limit_bytes=mib * 1024 * 1024)


def shards(
    eps_field, charge, potential_start, colloid_vel, colloid_spin, link_dir, link_colloid,
    link_site, link_depth, link_pop, link_rb,
):
    depth, wide, long = charge.shape
    layers = depth // 2
    rows = wide + 2 * FIRST
    fx, bx = ring("gx")
    fy, by = ring("gy")

    per_tile = colloid_vel.shape[1]
    motion = jnp.concatenate([colloid_vel, colloid_spin], axis=0)
    def edge(part):
        strips = jnp.stack([
            potential_start[:, part] * POT_SCALE,
            charge[:, part] * CHARGE_SCALE,
            eps_field[:, part].astype(F32),
        ])
        strips = strips.transpose(0, 2, 1, 3).astype(HALF).reshape(3 * HALO, depth, 128)
        return jnp.concatenate([strips, motion_plane(motion, depth)], axis=0)

    low = lax.ppermute(edge(slice(wide - HALO, wide)), "gx", fx)
    high = lax.ppermute(edge(slice(0, HALO)), "gx", bx)

    width = 9 * per_tile
    count = link_pop.shape[-1]
    lines = count // 128
    ids = link_colloid.reshape(lines, 128)
    dirs = link_dir.reshape(lines, 128)
    pops = link_pop.reshape(lines, 128)
    rb = link_rb.reshape(3, lines, 128)
    count_x, count_y = lax.axis_size("gx"), lax.axis_size("gy")
    owner = ids // per_tile
    near_x = (owner // count_y - lax.axis_index("gx") + 1) % count_x
    near_y = (owner % count_y - lax.axis_index("gy") + 1) % count_y
    live = ids >= 0
    slots = jnp.where(live, (near_x * 3 + near_y) * per_tile + ids % per_tile, -1)
    place = link_depth.reshape(lines, 128) * (wide * long) + link_site.reshape(lines, 128)
    key = jnp.where(
        live, (place - (1 << 18)) * (1 << KEY_BITS) + slots * 18 + dirs, np.int32(2**31 - 1)
    )
    keys, arm0, arm1 = lax.sort(
        (key.reshape(-1), *(part.reshape(-1) for part in pack_arms(rb))),
        num_keys=1, is_stable=False,
    )
    keys, arm0, arm1, low, high = lax.optimization_barrier((keys, arm0, arm1, low, high))
    keys = keys.reshape(lines, 128)
    table = direction_table()
    table_rows = ((keys >> KEY_BITS) + (1 << 18)) >> 7
    row_low = jnp.minimum(table_rows[:, 0], depth * wide - 1)
    row_high = jnp.max(jnp.where(table_rows < depth * wide, table_rows, 0), axis=1)
    span = jnp.max((row_high - row_low + 1).reshape(-1, 8 * BATCH), axis=1)
    passes = (jnp.maximum(span, 0) + AHEAD - 1) // AHEAD

    split, to_right, to_left = pl.pallas_call(
        pack_kernel,
        out_shape=(
            jax.ShapeDtypeStruct((6, layers + 1, rows, 128), F32),
            jax.ShapeDtypeStruct((3, GROUPS, wide + 2 * HALO, 128), F32),
            jax.ShapeDtypeStruct((3, GROUPS, wide + 2 * HALO, 128), F32),
        ),
        in_specs=vmem(5), out_specs=(pl.BlockSpec(memory_space=pltpu.HBM), *vmem(2)),
        compiler_params=grant(52), name="pack",
        scratch_shapes=[
            pltpu.VMEM((6, layers + 1, rows, 128), F32),
            pltpu.VMEM((2, 3 * GROUPS, wide + 2 * HALO, 128), F32),
            pltpu.SemaphoreType.DMA,
        ],
    )(potential_start, charge, eps_field,
      *(from_half(part[:-1].reshape(3, HALO, depth, 128)).reshape(-1, 128) for part in (low, high)))
    row = jnp.stack([
        motion_of(low[-1], motion.shape), motion, motion_of(high[-1], motion.shape)
    ])
    plane = motion_plane(row, wide + 2 * HALO)

    def strip(part):
        return jnp.concatenate([to_half(part).reshape(-1, *part.shape[2:]), plane], axis=0)

    to_right, dirs_late = lax.optimization_barrier((strip(to_right), dirs))
    from_left = lax.ppermute(to_right, "gy", fy)
    from_right = lax.ppermute(strip(to_left), "gy", by)
    shape = (3, GROUPS, wide + 2 * HALO, 128)
    west, east = [from_half(part[:-1].reshape(shape)) for part in (from_left, from_right)]
    near_motion = jnp.stack(
        [motion_of(from_left[-1], row.shape), row, motion_of(from_right[-1], row.shape)], axis=1
    )
    near_motion = near_motion.transpose(2, 0, 1, 3).reshape(6, width)

    terms = 32
    fixed, reach = pl.pallas_call(
        functools.partial(fixed_kernel, width=width),
        out_shape=(
            jax.ShapeDtypeStruct((terms, width), F32), jax.ShapeDtypeStruct((6, lines, 128), F32),
        ),
        in_specs=vmem(5), out_specs=tuple(vmem(2)),
        scratch_shapes=[pltpu.VMEM((8 * terms, 128), F32), pltpu.VMEM((2 * terms, width), F32)],
        compiler_params=grant(8), name="fixed",
        cost_estimate=pl.CostEstimate(flops=10**9, bytes_accessed=2 * 10**7, transcendentals=0),
    )(slots, dirs_late, pops, rb, table)

    tall = rows + 2 * MARGIN
    potential, press = pl.pallas_call(
        relax_kernel,
        out_shape=(
            jax.ShapeDtypeStruct((depth, wide, 128), F32),
            jax.ShapeDtypeStruct((depth + 1, wide, 128), F32),
        ),
        in_specs=[pl.BlockSpec(memory_space=pltpu.HBM)] + vmem(2), out_specs=tuple(vmem(2)),
        scratch_shapes=[
            pltpu.VMEM((2, layers + 3, tall, 128), F32),
            pltpu.VMEM((2, layers + 3, tall, 128), F32),
            pltpu.VMEM((2, layers + 1, rows, 128), F32),
            pltpu.VMEM((2, 7, layers + 1, rows, 128), F32),
            pltpu.VMEM((2, GROUPS + 2, tall, 128), F32),
            pltpu.VMEM((2, GROUPS + 2, tall, 128), F32),
            pltpu.VMEM((2, GROUPS, rows, 128), F32),
            pltpu.VMEM((2, 7, GROUPS, rows, 128), F32),
            pltpu.SemaphoreType.DMA((6,)),
        ],
        compiler_params=grant(48), name="relax",
    )(split, west, east)

    smem = pl.BlockSpec(memory_space=pltpu.SMEM)
    pressed = pl.pallas_call(
        functools.partial(press_kernel, per_tile=per_tile),
        out_shape=jax.ShapeDtypeStruct((9, 8, per_tile), F32),
        in_specs=[smem, smem] + vmem(5), out_specs=vmem(1)[0],
        scratch_shapes=[pltpu.VMEM((64, 128), F32), pltpu.VMEM((9 * 16, per_tile), F32)],
        compiler_params=grant(8), name="press",
    )(
        row_low, passes, keys, arm0.reshape(lines, 128), arm1.reshape(lines, 128),
        table, press.reshape(-1, 128),
    )

    drag = []
    for a in range(6):
        line = jnp.zeros((width,), F32)
        for d in range(6):
            n = PAIRS.index((min(a, d), max(a, d)))
            line = line + fixed[6 + n] * near_motion[d]
        drag.append(line)
    settled = fixed[0:6] - 6.0 * jnp.stack(drag)
    lanes = -(-width // 128) * 128
    partial = settled + pressed.transpose(1, 0, 2)[0:6].reshape(6, width)
    partial = jnp.pad(partial, ((0, 2), (0, lanes - width)))
    devices = count_x * count_y
    partials = lax.all_to_all(
        jnp.broadcast_to(partial, (devices, 8, lanes)), ("gx", "gy"), 0, 0
    )
    home = jnp.stack([lax.axis_index("gx"), lax.axis_index("gy")])
    report, link_out = pl.pallas_call(
        functools.partial(reflect_kernel, per_tile=per_tile, counts=(count_x, count_y)),
        out_shape=(
            jax.ShapeDtypeStruct((6, per_tile), F32), jax.ShapeDtypeStruct((lines, 128), F32),
        ),
        in_specs=[smem] + vmem(5), out_specs=tuple(vmem(2)), compiler_params=grant(6),
        name="reflect",
    )(home, partials, slots, reach, pops, jnp.pad(near_motion, ((0, 2), (0, lanes - width))))
    return potential, report, link_out.reshape(link_pop.shape)


def solution(mesh):
    placed = (
        P(None, "gx", "gy"),
        P(None, "gx", "gy"),
        P(None, "gx", "gy"),
        P(None, ("gx", "gy")),
        P(None, ("gx", "gy")),
        P("gx", "gy", None),
        P("gx", "gy", None),
        P("gx", "gy", None),
        P("gx", "gy", None),
        P("gx", "gy", None),
        P(None, "gx", "gy", None),
    )
    return jax.shard_map(
        shards,
        mesh=mesh,
        in_specs=placed,
        out_specs=(P(None, "gx", "gy"), P(None, ("gx", "gy")), P("gx", "gy", None)),
        check_vma=False,
    )
```

```python
import functools
import math

import jax
import jax.numpy as jnp
import numpy as np
from jax import lax
from jax.experimental import pallas as pl
from jax.experimental.pallas import tpu as pltpu
from jax.sharding import PartitionSpec as P

SWEEPS = 6
RADIUS = 8
OVER_RELAX = 1.6
HALO = 2 * SWEEPS
FIRST = 16
MARGIN = 8
GROUPS = 5
SLOT = 2 * HALO
KEY_BITS = 13
F32 = jnp.float32
HALF = jnp.float16
POT_SCALE = 2.0**14
CHARGE_SCALE = 2.0**13

VELOCITY = np.array(
    [
        [1, 0, 0], [-1, 0, 0], [0, 1, 0], [0, -1, 0], [0, 0, 1], [0, 0, -1],
        [1, 1, 0], [1, -1, 0], [-1, 1, 0], [-1, -1, 0], [1, 0, 1], [1, 0, -1],
        [-1, 0, 1], [-1, 0, -1], [0, 1, 1], [0, 1, -1], [0, -1, 1], [0, -1, -1],
    ],
    dtype=np.float32,
)
WEIGHT = np.array([1.0 / 18.0] * 6 + [1.0 / 36.0] * 12, dtype=np.float32)


def direction_table():
    table = np.zeros((4, 8, 128), np.float32)
    table[:3, :, :18] = VELOCITY.T[:, None, :]
    table[3, :, :18] = WEIGHT[None, :]
    return jnp.asarray(table)


PAIRS = [(a, b) for a in range(6) for b in range(a, 6)]


def lane_pick(table, index):
    return jnp.take_along_axis(table, index, axis=1, mode="promise_in_bounds")


def roll(value, shift):
    return pltpu.roll(value, shift % 128, 1)


def lanes_of(shape):
    return lax.broadcasted_iota(jnp.int32, shape, 1)


def parity_of(shape):
    rows = lax.broadcasted_iota(jnp.int32, shape, 0)
    return (rows + lanes_of(shape)) % 2 == 0


def pack_kernel(pot, charge, eps, low, high, kept, to_right, to_left, split, edges, sem):
    depth, wide, _ = pot.shape
    layers = depth // 2
    last = FIRST + wide

    def strip(source, f, z):
        return source[pl.ds(f * HALO * depth + z, HALO, stride=depth), :]

    def build(k, carry):
        for f, field in enumerate((pot, charge, eps)):
            fill = 1.0 if f == 2 else 0.0
            parts = (
                (FIRST, field[2 * k].astype(F32), field[2 * k + 1].astype(F32)),
                (FIRST - HALO, *(strip(low, f, 2 * k + n) for n in range(2))),
                (last, *(strip(high, f, 2 * k + n) for n in range(2))),
            )
            for start, even, odd in parts:
                flat = parity_of(even.shape)
                count = even.shape[0]
                split[2 * f, k, start:start + count, :] = jnp.where(flat, even, odd)
                split[2 * f + 1, k, start:start + count, :] = jnp.where(flat, odd, even)
            spare = FIRST - HALO
            edge = jnp.full((spare, 128), fill, F32)
            for c in range(2):
                split[2 * f + c, k, 0:spare, :] = edge
                split[2 * f + c, k, last + HALO:last + HALO + spare, :] = edge
        return carry

    lax.fori_loop(0, layers, build, 0)
    for f in range(3):
        for c in range(2):
            split[2 * f + c, layers] = jnp.full(
                (split.shape[2], 128), 1.0 if f == 2 else 0.0, F32
            )

    keep = pltpu.make_async_copy(split, kept, sem)
    keep.start()

    rows = slice(FIRST - HALO, last + HALO)
    lane = lanes_of((wide + 2 * HALO, 128))
    early = lane % SLOT < HALO
    slot_of = [(lane >= SLOT * g) & (lane < SLOT * (g + 1)) for g in range(GROUPS)]

    def gather_edges(n, carry):
        f = n // GROUPS
        i = n % GROUPS
        for c in range(2):
            value = jnp.zeros((wide + 2 * HALO, 128), F32)
            for g in range(GROUPS):
                field = split[2 * f + c, i + GROUPS * g, rows, :]
                value = jnp.where(slot_of[g], roll(field, SLOT * g + HALO), value)
            edges[c, n] = value
        return carry

    lax.fori_loop(0, 3 * GROUPS, gather_edges, 0)

    middle = lane - 2 * (lane % SLOT) + SLOT - 1
    near, same, far = [jnp.clip(middle + n * HALO, 0, 127) for n in (-1, 0, 1)]

    def strips(n, carry):
        f = n // GROUPS
        i = n % GROUPS
        red, black = edges[0, n], edges[1, n]
        to_right[f, i] = jnp.where(early, lane_pick(red, near), lane_pick(black, same))
        to_left[f, i] = jnp.where(early, lane_pick(red, same), lane_pick(black, far))
        return carry

    lax.fori_loop(0, 3 * GROUPS, strips, 0)
    keep.wait()


def relax_kernel(
    kept, from_left, from_right, pot_out, press_out, pa, ea, ca, wa, pb, eb, cb, wb, sems
):
    layers = kept.shape[1] - 1
    depth, wide, _ = pot_out.shape
    rows = kept.shape[2]
    tiles = rows // 8
    top = MARGIN
    lane = lanes_of((8, 128))
    flat = parity_of((8, 128))
    at_0 = lane == 0
    at_127 = lane == 127
    in_slot = lane % SLOT
    slot_east = in_slot == HALO - 1
    slot_west = in_slot == HALO
    pick = [(lane == SLOT * g + HALO - 1) | (lane == SLOT * g + HALO) for g in range(GROUPS)]

    zero = jnp.zeros((rows + 2 * MARGIN, 128), F32)
    one = jnp.ones((rows + 2 * MARGIN, 128), F32)
    margin0 = jnp.zeros((MARGIN, 128), F32)
    margin1 = jnp.ones((MARGIN, 128), F32)
    body = pl.ds(top, rows)
    middle = pl.ds(1, layers + 1)
    loads = []
    for c in range(2):
        loads.append(pltpu.make_async_copy(kept.at[4 + c], ea.at[c, middle, body], sems.at[c]))
        loads.append(pltpu.make_async_copy(kept.at[2 + c], ca.at[c], sems.at[2 + c]))
        loads.append(pltpu.make_async_copy(kept.at[c], pa.at[c, middle, body], sems.at[4 + c]))
        for load in loads[-3:]:
            load.start()

    def set_margins(k, carry):
        for c in range(2):
            for start in (0, top + rows):
                pa[c, k + 1, start:start + MARGIN, :] = margin0
                ea[c, k + 1, start:start + MARGIN, :] = margin1
        return carry

    lax.fori_loop(0, layers + 1, set_margins, 0)
    for c in range(2):
        pa[c, 0] = zero
        pa[c, layers + 2] = zero
        for start in (0, top + rows):
            ea[c, 0, start:start + MARGIN, :] = margin1
        ea[c, layers + 2] = one

    first = FIRST - HALO
    high = wide + 2 * HALO
    wide_lane = lanes_of((high, 128))
    wide_first = wide_lane % SLOT < HALO
    wide_used = wide_lane < SLOT * GROUPS
    for c in range(2):
        for i in range(GROUPS + 2):
            pb[c, i] = zero
            eb[c, i] = one
        for i in range(GROUPS):
            cb[c, i] = jnp.zeros((rows, 128), F32)

    for f, target in enumerate((pb, cb, eb)):
        for i in range(GROUPS):
            west = from_left[GROUPS * f + i]
            east = from_right[GROUPS * f + i]
            red = jnp.where(wide_first, east, roll(west, HALO))
            black = jnp.where(wide_first, roll(east, -HALO), west)
            fill = 1.0 if f == 2 else 0.0
            red = jnp.where(wide_used, red, fill)
            black = jnp.where(wide_used, black, fill)
            if f == 1:
                target[0, i, first:first + high, :] = red
                target[1, i, first:first + high, :] = black
            else:
                target[0, i + 1, top + first:top + first + high, :] = red
                target[1, i + 1, top + first:top + first + high, :] = black

    all_lane = lanes_of((rows + 2 * MARGIN, 128))
    lead = all_lane < SLOT
    tail = all_lane >= SLOT * (GROUPS - 1)
    spare_slot = SLOT * (layers // GROUPS)
    in_spare = (all_lane >= spare_slot) & (all_lane < spare_slot + SLOT)

    def wrap_pot(c):
        pb[c, 0] = jnp.where(lead, 0.0, roll(pb[c, GROUPS], SLOT))
        pb[c, GROUPS + 1] = jnp.where(tail, 0.0, roll(pb[c, 1], -SLOT))

    spare_row = layers % GROUPS + 1
    for c in range(2):
        wrap_pot(c)
        eb[c, spare_row] = jnp.where(in_spare, eb[1 - c, spare_row - 1], eb[c, spare_row])
    for c in range(2):
        eb[c, 0] = jnp.where(lead, eb[1 - c, 1], roll(eb[c, GROUPS], SLOT))
        eb[c, GROUPS + 1] = jnp.where(tail, 1.0, roll(eb[c, 1], -SLOT))

    for load in loads:
        load.wait()
    for c in range(2):
        ea[c, 0, top:top + rows, :] = ea[1 - c, 1, top:top + rows, :]
        ea[c, layers + 1, top:top + rows, :] = ea[1 - c, layers, top:top + rows, :]

    def around(src_a, src_b, other, color, i, t, body_a, body_b):
        r0 = top + 8 * t
        rs = slice(r0, r0 + 8)
        rm = slice(r0 - 1, r0 + 7)
        rp = slice(r0 + 1, r0 + 9)
        up = ~flat if color == 0 else flat
        side = src_b[other, i + 1, rs, :]
        edge = side
        for g in range(GROUPS):
            k = i + GROUPS * g
            here = src_a[other, k + 1, rs, :]
            halo = roll(side, -(SLOT * g + HALO))
            body_a(k, (
                here,
                jnp.where(up, src_a[other, k + 2, rs, :], src_a[other, k, rs, :]),
                src_a[other, k + 1, rm, :],
                src_a[other, k + 1, rp, :],
                jnp.where(at_0, halo, roll(here, 1)),
                jnp.where(at_127, halo, roll(here, -1)),
            ))
            if body_b is not None:
                edge = jnp.where(pick[g], roll(here, SLOT * g + HALO), edge)
        if body_b is not None:
            body_b((
                side,
                jnp.where(up, src_b[other, i, rs, :], src_b[other, i + 2, rs, :]),
                src_b[other, i + 1, rm, :],
                src_b[other, i + 1, rp, :],
                jnp.where(slot_east, edge, roll(side, -1)),
                jnp.where(slot_west, edge, roll(side, 1)),
            ))

    def coefficients(own, charge, sides):
        faces = [0.5 * (own + side) for side in sides]
        total = faces[0] + faces[1] + faces[2] + faces[3] + faces[4] + faces[5]
        scale = OVER_RELAX / total
        return [face * scale for face in faces] + [charge * scale]

    for c in range(2):
        def set_up(i, carry, c=c):
            for t in range(tiles):
                ts = slice(8 * t, 8 * t + 8)
                ps = slice(top + 8 * t, top + 8 * t + 8)

                def body_a(k, sides):
                    values = coefficients(ea[c, k + 1, ps, :], ca[c, k, ts, :], sides)
                    for n, value in enumerate(values):
                        wa[c, n, k, ts, :] = value

                def body_b(sides):
                    values = coefficients(eb[c, i + 1, ps, :], cb[c, i, ts, :], sides)
                    live = in_spare[0:8] & (i + 1 == spare_row)
                    for n, value in enumerate(values):
                        wb[c, n, i, ts, :] = jnp.where(live, 0.0, value)

                around(ea, eb, 1 - c, c, i, t, body_a, body_b)
            return carry

        lax.fori_loop(0, GROUPS, set_up, 0)
        for n in range(7):
            wa[c, n, layers] = jnp.zeros((rows, 128), F32)

    def combine(own, w, sides):
        left = w[0] * sides[0] + w[1] * sides[1]
        mid = w[2] * sides[2] + w[3] * sides[3]
        right = w[4] * sides[4] + w[5] * sides[5]
        return (w[6] - (OVER_RELAX - 1.0) * own) + (left + (mid + right))

    for step in range(2 * SWEEPS):
        c = step % 2
        reach = HALO - 1 - step
        t_low = (FIRST - reach) // 8
        t_high = -(-(FIRST + wide + reach) // 8)

        def half(i, carry, c=c, reach=reach, t_low=t_low, t_high=t_high):
            for t in range(t_low, t_high):
                ts = slice(8 * t, 8 * t + 8)
                ps = slice(top + 8 * t, top + 8 * t + 8)

                def body_a(k, sides):
                    w = [wa[c, n, k, ts, :] for n in range(7)]
                    pa[c, k + 1, ps, :] = combine(pa[c, k + 1, ps, :], w, sides)

                def body_b(sides):
                    w = [wb[c, n, i, ts, :] for n in range(7)]
                    pb[c, i + 1, ps, :] = combine(pb[c, i + 1, ps, :], w, sides)

                around(pa, pb, 1 - c, c, i, t, body_a, body_b if reach else None)
            return carry

        lax.fori_loop(0, GROUPS, half, 0)
        if reach:
            wrap_pot(c)

    press_out[depth] = jnp.zeros((wide, 128), F32)
    core = slice(top + FIRST, top + FIRST + wide)
    core_flat = parity_of((wide, 128))

    def finish(k, carry):
        red, black = pa[0, k + 1, core, :], pa[1, k + 1, core, :]
        e_red, e_black = ea[0, k + 1, core, :], ea[1, k + 1, core, :]
        q_red = 0.5 * e_red * red * red
        q_black = 0.5 * e_black * black * black
        pot_out[2 * k] = jnp.where(core_flat, red, black)
        pot_out[2 * k + 1] = jnp.where(core_flat, black, red)
        press_out[2 * k] = jnp.where(core_flat, q_red, q_black)
        press_out[2 * k + 1] = jnp.where(core_flat, q_black, q_red)
        return carry

    lax.fori_loop(0, layers, finish, 0)


def geometry(direction, offsets, table):
    c0, c1, c2, w = [lane_pick(table[n], direction) for n in range(4)]
    r0, r1, r2 = offsets
    arms = [c0, c1, c2, r1 * c2 - r2 * c1, r2 * c0 - r0 * c2, r0 * c1 - r1 * c0]
    return arms, w


ARM_REACH = 9.0
ARM_BITS = 21
ARM_STEP = 2.0 * ARM_REACH / (2**ARM_BITS - 1)
SPARE_BITS = 32 - ARM_BITS


def pack_arms(rb):
    a, b, c = [jnp.round((rb[n] + ARM_REACH) * (1.0 / ARM_STEP)).astype(jnp.int32) for n in range(3)]
    low = c & ((1 << SPARE_BITS) - 1)
    return (a << SPARE_BITS) | low, (b << SPARE_BITS) | (c >> SPARE_BITS)


def unpack_arms(first, second):
    low = (1 << SPARE_BITS) - 1
    whole = (1 << ARM_BITS) - 1
    a = (first >> SPARE_BITS) & whole
    b = (second >> SPARE_BITS) & whole
    c = ((second & low) << SPARE_BITS) | (first & low)
    return [part.astype(F32) * ARM_STEP - ARM_REACH for part in (a, b, c)]


def store_term(stage, n, value):
    stage[8 * n:8 * n + 8, :] = value


def add_by_slot(stage, slot, width):
    total = stage.shape[0] // 8
    fine = slot & 15
    coarse = slot >> 4
    small = lax.broadcasted_iota(jnp.int32, (16, 128), 0)
    hot, terms = [], []
    for s in range(8):
        match = (jnp.broadcast_to(fine[s:s + 1, :], (16, 128)) == small).astype(F32)
        match = match.astype(jnp.bfloat16)
        part = jnp.broadcast_to(coarse[s:s + 1, :].astype(F32), (16, 128)).astype(jnp.bfloat16)
        none = jnp.zeros((16, 128), jnp.bfloat16)
        hot.append(jnp.concatenate(
            [jnp.where(part == m, match, none) for m in range(width // 16)], axis=0
        ))
        value = stage[pl.ds(s, total, stride=8), :]
        head = value.astype(jnp.bfloat16)
        terms.append(jnp.concatenate(
            [head.astype(F32), value - head.astype(F32)], axis=0
        ).astype(jnp.bfloat16))
    return lax.dot_general(
        jnp.concatenate(terms, axis=1),
        jnp.concatenate(hot, axis=1),
        (((1,), (1,)), ((), ())),
        preferred_element_type=F32,
    )


def add_by_tile(stage, slot, per_tile):
    total = stage.shape[0] // 8
    shift = per_tile.bit_length() - 1
    tile = (slot >> shift).astype(F32)
    fine = (slot & (per_tile - 1)).astype(F32)
    small = lax.broadcasted_iota(jnp.int32, (per_tile, 128), 0).astype(F32).astype(jnp.bfloat16)
    one = jnp.ones((per_tile, 128), jnp.bfloat16)
    none = jnp.zeros((2 * total, 128), jnp.bfloat16)
    hot, terms = [], []
    for s in range(8):
        place = jnp.broadcast_to(fine[s:s + 1, :], (per_tile, 128)).astype(jnp.bfloat16)
        hot.append(jnp.where(place == small, one, jnp.zeros_like(one)))
        owner = jnp.broadcast_to(tile[s:s + 1, :], (2 * total, 128)).astype(jnp.bfloat16)
        value = stage[pl.ds(s, total, stride=8), :]
        head = value.astype(jnp.bfloat16)
        both = jnp.concatenate([head.astype(F32), value - head.astype(F32)], axis=0)
        both = both.astype(jnp.bfloat16)
        terms.append(jnp.concatenate([jnp.where(owner == t, both, none) for t in range(9)], axis=0))
    return lax.dot_general(
        jnp.concatenate(terms, axis=1),
        jnp.concatenate(hot, axis=1),
        (((1,), (1,)), ((), ())),
        preferred_element_type=F32,
    )


def fixed_kernel(slots, dirs, pops, rb, table, out, reach, stage, acc, *, width):
    acc[...] = jnp.zeros_like(acc)
    total = stage.shape[0] // 8
    for n in range(6 + len(PAIRS), total):
        store_term(stage, n, jnp.zeros((8, 128), F32))

    def block(b, carry):
        rs = pl.ds(pl.multiple_of(8 * b, 8), 8)
        arms, w = geometry(dirs[rs, :], [rb[n, rs, :] for n in range(3)], table)
        twice = 2.0 * pops[rs, :]
        weighted = [w * arm for arm in arms]
        for n in range(6):
            reach[n, rs, :] = jnp.where(slots[rs, :] >= 0, 6.0 * weighted[n], 0.0)
        for n in range(6):
            store_term(stage, n, twice * arms[n])
        for n, (a, d) in enumerate(PAIRS):
            store_term(stage, 6 + n, weighted[a] * arms[d])
        acc[...] += add_by_slot(stage, slots[rs, :], width)
        return carry

    lax.fori_loop(0, slots.shape[0] // 8, block, 0)
    out[...] = acc[0:total, :] + acc[total:, :]


BATCH = 8
AHEAD = 4


def press_kernel(
    low, passes, keys, arm0, arm1, table, press, settled, out, stage, acc, sums, *, per_tile
):
    acc[...] = jnp.zeros_like(acc)
    for n in range(6, stage.shape[0] // 8):
        store_term(stage, n, jnp.zeros((8, 128), F32))
    limit = press.shape[0] - AHEAD
    line = lax.broadcasted_iota(jnp.int32, (8, 128), 0)

    def batch(b, carry):
        spots = [pl.ds(pl.multiple_of(8 * (BATCH * b + j), 8), 8) for j in range(BATCH)]
        columns, offsets, starts = [], [], []
        for j in range(BATCH):
            place = (keys[spots[j], :] >> KEY_BITS) + (1 << 18)
            start = [low[8 * (BATCH * b + j) + s] for s in range(8)]
            first = jnp.zeros((8, 128), jnp.int32)
            for s in range(8):
                first = jnp.where(line == s, start[s], first)
            columns.append(place & 127)
            offsets.append((place >> 7) - first)
            starts.append(start)

        def look(m, found):
            found = list(found)
            for j in range(BATCH):
                bases = [jnp.minimum(starts[j][s] + AHEAD * m, limit) for s in range(8)]
                for t in range(AHEAD):
                    window = jnp.zeros((8, 128), F32)
                    for s in range(8):
                        row = press[pl.ds(bases[s] + t, 1), :]
                        window = jnp.where(line == s, jnp.broadcast_to(row, (8, 128)), window)
                    value = lane_pick(window, columns[j])
                    found[j] = jnp.where(offsets[j] == AHEAD * m + t, value, found[j])
            return tuple(found)

        found = lax.fori_loop(
            0, passes[b], look, tuple(jnp.zeros((8, 128), F32) for _ in range(BATCH))
        )
        for j in range(BATCH):
            rs = spots[j]
            code = keys[rs, :] & ((1 << KEY_BITS) - 1)
            slot = jnp.floor((code.astype(F32) + 0.5) * (1.0 / 18.0)).astype(jnp.int32)
            direction = code - 18 * slot
            arms, w = geometry(direction, unpack_arms(arm0[rs, :], arm1[rs, :]), table)
            wq = w * found[j]
            for n in range(6):
                store_term(stage, n, wq * arms[n])
            acc[...] += add_by_tile(stage, slot, per_tile)
        return carry

    lax.fori_loop(0, keys.shape[0] // (8 * BATCH), batch, 0)

    sums[...] = jnp.zeros_like(sums)
    for t in range(9):
        value = acc[16 * t:16 * t + 8, :] + acc[16 * t + 8:16 * t + 16, :]
        sums[:, per_tile * t:per_tile * (t + 1)] = value
    sums[...] += settled[...]
    head, last = sums[:, 0:128], sums[:, 256:384]
    lane = lanes_of((8, 128))
    for n in range(6):
        part = jnp.broadcast_to(last[n:n + 1, :], (8, 128))
        here = (line == 6 + n // 4) & (lane // per_tile == n % 4)
        head = jnp.where(here, roll(part, per_tile * (n % 4)), head)
    tail = sums[:, 128:256]

    def replicate(p, carry):
        out[p, 0:8, :] = head
        out[p, 8:16, :] = tail
        return carry

    lax.fori_loop(0, out.shape[0], replicate, 0)


TOGETHER = 4
AROUND = [(ox, oy) for ox in range(-2, 3) for oy in range(-2, 3)]


def reflect_kernel(
    home, partial_sums, slots, reach, pops, motion, report, out, spread, *, per_tile, counts
):
    lanes = motion.shape[1]
    slot_of_lane = lax.broadcasted_iota(jnp.int32, (8, lanes), 1) // per_tile
    tile_x = slot_of_lane // 3 - 1
    tile_y = slot_of_lane % 3 - 1
    totals = jnp.zeros((8, lanes), F32)
    lane_of = lanes_of((8, 128))
    line = lax.broadcasted_iota(jnp.int32, (8, 128), 0)
    place = lane_of % per_tile + per_tile * (line % 4)

    def unpack(n, carry):
        peer_x = lax.rem(home[0] + n // 5 - 2 + 2 * counts[0], counts[0])
        peer_y = lax.rem(home[1] + n % 5 - 2 + 2 * counts[1], counts[1])
        block = partial_sums[peer_x * counts[1] + peer_y]
        parts = [lane_pick(jnp.broadcast_to(block[r:r + 1, :], (8, 128)), place) for r in (6, 7)]
        spread[n, :, 0:128] = block[0:8, :]
        spread[n, :, 128:256] = block[8:16, :]
        spread[n, :, 256:384] = jnp.where(line < 4, parts[0], parts[1])
        return carry

    lax.fori_loop(0, len(AROUND), unpack, 0)
    for n, (ox, oy) in enumerate(AROUND):
        near = (abs(tile_x - ox) <= 1) & (abs(tile_y - oy) <= 1) & (slot_of_lane < 9)
        shift = per_tile * (3 * ox + oy)
        moved = pltpu.roll(spread[n], shift % lanes, 1)
        totals = totals + jnp.where(near, moved, 0.0)
    mass = 4.0 / 3.0 * math.pi * RADIUS**3
    inertia = 0.4 * mass * RADIUS**2
    is_force = lax.broadcasted_iota(jnp.int32, (8, lanes), 0) < 3
    moved = motion[...] + totals * jnp.where(is_force, 1.0 / mass, 1.0 / inertia)
    stated = totals * jnp.where(is_force, 1.0, 1.0 / RADIUS)
    report[...] = stated[0:6, 4 * per_tile:5 * per_tile]

    table = [
        [jnp.broadcast_to(moved[n:n + 1, 128 * h:128 * h + 128], (8, 128)) for h in range(lanes // 128)]
        for n in range(6)
    ]

    def batch(b, carry):
        for j in range(TOGETHER):
            rs = pl.ds(pl.multiple_of(8 * (TOGETHER * b + j), 8), 8)
            slot = slots[rs, :]
            lane = slot & 127
            part = slot >> 7
            along = jnp.zeros((8, 128), F32)
            for n in range(6):
                value = jnp.zeros((8, 128), F32)
                for h in range(lanes // 128):
                    value = jnp.where(part == h, lane_pick(table[n][h], lane), value)
                along += reach[n, rs, :] * value
            out[rs, :] = pops[rs, :] - along
        return carry

    lax.fori_loop(0, slots.shape[0] // (8 * TOGETHER), batch, 0)


def ring(axis):
    count = lax.axis_size(axis)
    forward = [(i, (i + 1) % count) for i in range(count)]
    return forward, [(b, a) for a, b in forward]


def scales():
    return jnp.array([POT_SCALE, CHARGE_SCALE, 1.0], F32).reshape(3, 1, 1, 1)


def to_half(strips):
    return (strips * scales()).astype(HALF)


def from_half(planes):
    each = (planes.shape[0] - 1) // 3
    back = [1.0 / POT_SCALE] * each + [1.0 / CHARGE_SCALE] * each + [1.0] * (each + 1)
    return planes.astype(F32) * jnp.array(back, F32)[:, None, None]


MOTION_SCALE = 2.0**10
REST_SCALE = 2.0**12


def motion_plane(motions, rows):
    value = motions.reshape(-1, motions.shape[-1]) * MOTION_SCALE
    head = lax.reduce_precision(value, 8, 10)
    both = jnp.concatenate([head, (value - head) * REST_SCALE], axis=0).astype(HALF)
    return jnp.pad(both, ((0, rows - both.shape[0]), (0, 128 - both.shape[1])))[None]


def motion_of(plane, shape):
    count = math.prod(shape[:-1])
    both = plane[:2 * count, :shape[-1]].astype(F32)
    value = both[:count] + both[count:] * (1.0 / REST_SCALE)
    return (value * (1.0 / MOTION_SCALE)).reshape(shape)


def vmem(n):
    return [pl.BlockSpec(memory_space=pltpu.VMEM)] * n


def grant(mib):
    return pltpu.CompilerParams(vmem_limit_bytes=mib * 1024 * 1024)


def shards(
    eps_field, charge, potential_start, colloid_vel, colloid_spin, link_dir, link_colloid,
    link_site, link_depth, link_pop, link_rb,
):
    depth, wide, long = charge.shape
    layers = depth // 2
    rows = wide + 2 * FIRST
    fx, bx = ring("gx")
    fy, by = ring("gy")

    per_tile = colloid_vel.shape[1]
    motion = jnp.concatenate([colloid_vel, colloid_spin], axis=0)
    def edge(part):
        strips = jnp.stack([
            potential_start[:, part] * POT_SCALE,
            charge[:, part] * CHARGE_SCALE,
            eps_field[:, part].astype(F32),
        ])
        strips = strips.transpose(0, 2, 1, 3).astype(HALF).reshape(3 * HALO, depth, 128)
        return jnp.concatenate([strips, motion_plane(motion, depth)], axis=0)

    low = lax.ppermute(edge(slice(wide - HALO, wide)), "gx", fx)
    high = lax.ppermute(edge(slice(0, HALO)), "gx", bx)

    width = 9 * per_tile
    count = link_pop.shape[-1]
    lines = count // 128
    ids = link_colloid.reshape(lines, 128)
    dirs = link_dir.reshape(lines, 128)
    pops = link_pop.reshape(lines, 128)
    rb = link_rb.reshape(3, lines, 128)
    count_x, count_y = lax.axis_size("gx"), lax.axis_size("gy")
    owner = ids // per_tile
    near_x = (owner // count_y - lax.axis_index("gx") + 1) % count_x
    near_y = (owner % count_y - lax.axis_index("gy") + 1) % count_y
    live = ids >= 0
    slots = jnp.where(live, (near_x * 3 + near_y) * per_tile + ids % per_tile, -1)
    place = link_depth.reshape(lines, 128) * (wide * long) + link_site.reshape(lines, 128)
    key = jnp.where(
        live, (place - (1 << 18)) * (1 << KEY_BITS) + slots * 18 + dirs, np.int32(2**31 - 1)
    )
    keys, arm0, arm1 = lax.sort(
        (key.reshape(-1), *(part.reshape(-1) for part in pack_arms(rb))),
        num_keys=1, is_stable=False,
    )
    keys, arm0, arm1, low, high = lax.optimization_barrier((keys, arm0, arm1, low, high))
    keys = keys.reshape(lines, 128)
    table = direction_table()
    table_rows = ((keys >> KEY_BITS) + (1 << 18)) >> 7
    row_low = jnp.minimum(table_rows[:, 0], depth * wide - 1)
    row_high = jnp.max(jnp.where(table_rows < depth * wide, table_rows, 0), axis=1)
    span = jnp.max((row_high - row_low + 1).reshape(-1, 8 * BATCH), axis=1)
    passes = (jnp.maximum(span, 0) + AHEAD - 1) // AHEAD

    low, high = from_half(low), from_half(high)
    split, to_right, to_left = pl.pallas_call(
        pack_kernel,
        out_shape=(
            jax.ShapeDtypeStruct((6, layers + 1, rows, 128), F32),
            jax.ShapeDtypeStruct((3, GROUPS, wide + 2 * HALO, 128), F32),
            jax.ShapeDtypeStruct((3, GROUPS, wide + 2 * HALO, 128), F32),
        ),
        in_specs=vmem(5), out_specs=(pl.BlockSpec(memory_space=pltpu.HBM), *vmem(2)),
        compiler_params=grant(52), name="pack",
        scratch_shapes=[
            pltpu.VMEM((6, layers + 1, rows, 128), F32),
            pltpu.VMEM((2, 3 * GROUPS, wide + 2 * HALO, 128), F32),
            pltpu.SemaphoreType.DMA,
        ],
    )(potential_start, charge, eps_field,
      low.reshape(-1, 128), high.reshape(-1, 128))
    row = jnp.stack([
        motion_of(low[-1], motion.shape), motion, motion_of(high[-1], motion.shape)
    ])
    plane = motion_plane(row, wide + 2 * HALO)

    def strip(part):
        return jnp.concatenate([to_half(part).reshape(-1, *part.shape[2:]), plane], axis=0)

    to_right, dirs_late = lax.optimization_barrier((strip(to_right), dirs))
    from_left = lax.ppermute(to_right, "gy", fy)
    from_right = lax.ppermute(strip(to_left), "gy", by)
    from_left, from_right = from_half(from_left), from_half(from_right)
    near_motion = jnp.stack(
        [motion_of(from_left[-1], row.shape), row, motion_of(from_right[-1], row.shape)], axis=1
    )
    near_motion = near_motion.transpose(2, 0, 1, 3).reshape(6, width)

    terms = 32
    fixed, reach = pl.pallas_call(
        functools.partial(fixed_kernel, width=width),
        out_shape=(
            jax.ShapeDtypeStruct((terms, width), F32), jax.ShapeDtypeStruct((6, lines, 128), F32),
        ),
        in_specs=vmem(5), out_specs=tuple(vmem(2)),
        scratch_shapes=[pltpu.VMEM((8 * terms, 128), F32), pltpu.VMEM((2 * terms, width), F32)],
        compiler_params=grant(8), name="fixed",
        cost_estimate=pl.CostEstimate(flops=10**9, bytes_accessed=2 * 10**7, transcendentals=0),
    )(slots, dirs_late, pops, rb, table)

    tall = rows + 2 * MARGIN
    potential, press = pl.pallas_call(
        relax_kernel,
        out_shape=(
            jax.ShapeDtypeStruct((depth, wide, 128), F32),
            jax.ShapeDtypeStruct((depth + 1, wide, 128), F32),
        ),
        in_specs=[pl.BlockSpec(memory_space=pltpu.HBM)] + vmem(2), out_specs=tuple(vmem(2)),
        scratch_shapes=[
            pltpu.VMEM((2, layers + 3, tall, 128), F32),
            pltpu.VMEM((2, layers + 3, tall, 128), F32),
            pltpu.VMEM((2, layers + 1, rows, 128), F32),
            pltpu.VMEM((2, 7, layers + 1, rows, 128), F32),
            pltpu.VMEM((2, GROUPS + 2, tall, 128), F32),
            pltpu.VMEM((2, GROUPS + 2, tall, 128), F32),
            pltpu.VMEM((2, GROUPS, rows, 128), F32),
            pltpu.VMEM((2, 7, GROUPS, rows, 128), F32),
            pltpu.SemaphoreType.DMA((6,)),
        ],
        compiler_params=grant(48), name="relax",
    )(split, from_left, from_right)

    drag = []
    for a in range(6):
        drag.append(sum(
            fixed[6 + PAIRS.index((min(a, d), max(a, d)))] * near_motion[d] for d in range(6)
        ))
    settled = fixed[0:6] - 6.0 * jnp.stack(drag)
    lanes = -(-width // 128) * 128
    settled, near_motion = [
        jnp.pad(part, ((0, 2), (0, lanes - width))) for part in (settled, near_motion)
    ]
    devices = count_x * count_y
    smem = pl.BlockSpec(memory_space=pltpu.SMEM)
    pressed = pl.pallas_call(
        functools.partial(press_kernel, per_tile=per_tile),
        out_shape=jax.ShapeDtypeStruct((devices, 16, 128), F32),
        in_specs=[smem, smem] + vmem(6), out_specs=vmem(1)[0],
        scratch_shapes=[
            pltpu.VMEM((64, 128), F32), pltpu.VMEM((9 * 16, per_tile), F32),
            pltpu.VMEM((8, lanes), F32),
        ],
        compiler_params=grant(8), name="press",
    )(
        row_low, passes, keys, arm0.reshape(lines, 128), arm1.reshape(lines, 128),
        table, press.reshape(-1, 128), settled,
    )

    partials = lax.all_to_all(pressed, ("gx", "gy"), 0, 0)

    home = jnp.stack([lax.axis_index("gx"), lax.axis_index("gy")])
    report, link_out = pl.pallas_call(
        functools.partial(reflect_kernel, per_tile=per_tile, counts=(count_x, count_y)),
        out_shape=(
            jax.ShapeDtypeStruct((6, per_tile), F32), jax.ShapeDtypeStruct((lines, 128), F32),
        ),
        in_specs=[smem] + vmem(5), out_specs=tuple(vmem(2)), compiler_params=grant(6),
        scratch_shapes=[pltpu.VMEM((len(AROUND), 8, lanes), F32)], name="reflect",
    )(home, partials, slots, reach, pops, near_motion)
    return potential, report, link_out.reshape(link_pop.shape)


def solution(mesh):
    placed = (
        P(None, "gx", "gy"),
        P(None, "gx", "gy"),
        P(None, "gx", "gy"),
        P(None, ("gx", "gy")),
        P(None, ("gx", "gy")),
        P("gx", "gy", None),
        P("gx", "gy", None),
        P("gx", "gy", None),
        P("gx", "gy", None),
        P("gx", "gy", None),
        P(None, "gx", "gy", None),
    )
    return jax.shard_map(
        shards,
        mesh=mesh,
        in_specs=placed,
        out_specs=(P(None, "gx", "gy"), P(None, ("gx", "gy")), P("gx", "gy", None)),
        check_vma=False,
    )
```

```python
import functools
import math

import jax
import jax.numpy as jnp
import numpy as np
from jax import lax
from jax.experimental import pallas as pl
from jax.experimental.pallas import tpu as pltpu
from jax.sharding import PartitionSpec as P

SWEEPS = 6
RADIUS = 8
OVER_RELAX = 1.6
HALO = 2 * SWEEPS
FIRST = 16
MARGIN = 8
GROUPS = 5
SLOT = 2 * HALO
KEY_BITS = 13
F32 = jnp.float32
HALF = jnp.float16
POT_SCALE = 2.0**14
CHARGE_SCALE = 2.0**13

VELOCITY = np.array(
    [
        [1, 0, 0], [-1, 0, 0], [0, 1, 0], [0, -1, 0], [0, 0, 1], [0, 0, -1],
        [1, 1, 0], [1, -1, 0], [-1, 1, 0], [-1, -1, 0], [1, 0, 1], [1, 0, -1],
        [-1, 0, 1], [-1, 0, -1], [0, 1, 1], [0, 1, -1], [0, -1, 1], [0, -1, -1],
    ],
    dtype=np.float32,
)
WEIGHT = np.array([1.0 / 18.0] * 6 + [1.0 / 36.0] * 12, dtype=np.float32)


def direction_table():
    table = np.zeros((4, 8, 128), np.float32)
    table[:3, :, :18] = VELOCITY.T[:, None, :]
    table[3, :, :18] = WEIGHT[None, :]
    return jnp.asarray(table)


PAIRS = [(a, b) for a in range(6) for b in range(a, 6)]


def lane_pick(table, index):
    return jnp.take_along_axis(table, index, axis=1, mode="promise_in_bounds")


def roll(value, shift):
    return pltpu.roll(value, shift % 128, 1)


def lanes_of(shape):
    return lax.broadcasted_iota(jnp.int32, shape, 1)


def parity_of(shape):
    rows = lax.broadcasted_iota(jnp.int32, shape, 0)
    return (rows + lanes_of(shape)) % 2 == 0


def pack_kernel(pot, charge, eps, low, high, kept, to_right, to_left, split, edges, sem):
    depth, wide, _ = pot.shape
    layers = depth // 2
    last = FIRST + wide

    def strip(source, f, z):
        return source[pl.ds(f * HALO * depth + z, HALO, stride=depth), :]

    def build(k, carry):
        for f, field in enumerate((pot, charge, eps)):
            fill = 1.0 if f == 2 else 0.0
            parts = (
                (FIRST, field[2 * k].astype(F32), field[2 * k + 1].astype(F32)),
                (FIRST - HALO, *(strip(low, f, 2 * k + n) for n in range(2))),
                (last, *(strip(high, f, 2 * k + n) for n in range(2))),
            )
            for start, even, odd in parts:
                flat = parity_of(even.shape)
                count = even.shape[0]
                split[2 * f, k, start:start + count, :] = jnp.where(flat, even, odd)
                split[2 * f + 1, k, start:start + count, :] = jnp.where(flat, odd, even)
            spare = FIRST - HALO
            edge = jnp.full((spare, 128), fill, F32)
            for c in range(2):
                split[2 * f + c, k, 0:spare, :] = edge
                split[2 * f + c, k, last + HALO:last + HALO + spare, :] = edge
        return carry

    lax.fori_loop(0, layers, build, 0)
    for f in range(3):
        for c in range(2):
            split[2 * f + c, layers] = jnp.full(
                (split.shape[2], 128), 1.0 if f == 2 else 0.0, F32
            )

    keep = pltpu.make_async_copy(split, kept, sem)
    keep.start()

    rows = slice(FIRST - HALO, last + HALO)
    lane = lanes_of((wide + 2 * HALO, 128))
    early = lane % SLOT < HALO
    slot_of = [(lane >= SLOT * g) & (lane < SLOT * (g + 1)) for g in range(GROUPS)]

    def gather_edges(n, carry):
        f = n // GROUPS
        i = n % GROUPS
        for c in range(2):
            value = jnp.zeros((wide + 2 * HALO, 128), F32)
            for g in range(GROUPS):
                field = split[2 * f + c, i + GROUPS * g, rows, :]
                value = jnp.where(slot_of[g], roll(field, SLOT * g + HALO), value)
            edges[c, n] = value
        return carry

    lax.fori_loop(0, 3 * GROUPS, gather_edges, 0)

    middle = lane - 2 * (lane % SLOT) + SLOT - 1
    near, same, far = [jnp.clip(middle + n * HALO, 0, 127) for n in (-1, 0, 1)]

    def strips(n, carry):
        f = n // GROUPS
        i = n % GROUPS
        red, black = edges[0, n], edges[1, n]
        to_right[f, i] = jnp.where(early, lane_pick(red, near), lane_pick(black, same))
        to_left[f, i] = jnp.where(early, lane_pick(red, same), lane_pick(black, far))
        return carry

    lax.fori_loop(0, 3 * GROUPS, strips, 0)
    keep.wait()


def relax_kernel(
    kept, from_left, from_right, pot_out, press_out, pa, ea, ca, wa, pb, eb, cb, wb, sems
):
    layers = kept.shape[1] - 1
    depth, wide, _ = pot_out.shape
    rows = kept.shape[2]
    tiles = rows // 8
    top = MARGIN
    lane = lanes_of((8, 128))
    flat = parity_of((8, 128))
    at_0 = lane == 0
    at_127 = lane == 127
    in_slot = lane % SLOT
    slot_east = in_slot == HALO - 1
    slot_west = in_slot == HALO
    pick = [(lane == SLOT * g + HALO - 1) | (lane == SLOT * g + HALO) for g in range(GROUPS)]

    zero = jnp.zeros((rows + 2 * MARGIN, 128), F32)
    one = jnp.ones((rows + 2 * MARGIN, 128), F32)
    margin0 = jnp.zeros((MARGIN, 128), F32)
    margin1 = jnp.ones((MARGIN, 128), F32)
    body = pl.ds(top, rows)
    middle = pl.ds(1, layers + 1)
    loads = []
    for c in range(2):
        loads.append(pltpu.make_async_copy(kept.at[4 + c], ea.at[c, middle, body], sems.at[c]))
        loads.append(pltpu.make_async_copy(kept.at[2 + c], ca.at[c], sems.at[2 + c]))
        loads.append(pltpu.make_async_copy(kept.at[c], pa.at[c, middle, body], sems.at[4 + c]))
        for load in loads[-3:]:
            load.start()

    def set_margins(k, carry):
        for c in range(2):
            for start in (0, top + rows):
                pa[c, k + 1, start:start + MARGIN, :] = margin0
                ea[c, k + 1, start:start + MARGIN, :] = margin1
        return carry

    lax.fori_loop(0, layers + 1, set_margins, 0)
    for c in range(2):
        pa[c, 0] = zero
        pa[c, layers + 2] = zero
        for start in (0, top + rows):
            ea[c, 0, start:start + MARGIN, :] = margin1
        ea[c, layers + 2] = one

    first = FIRST - HALO
    high = wide + 2 * HALO
    wide_lane = lanes_of((high, 128))
    wide_first = wide_lane % SLOT < HALO
    wide_used = wide_lane < SLOT * GROUPS
    for c in range(2):
        for i in range(GROUPS + 2):
            pb[c, i] = zero
            eb[c, i] = one
        for i in range(GROUPS):
            cb[c, i] = jnp.zeros((rows, 128), F32)

    for f, target in enumerate((pb, cb, eb)):
        for i in range(GROUPS):
            west = from_left[GROUPS * f + i]
            east = from_right[GROUPS * f + i]
            red = jnp.where(wide_first, east, roll(west, HALO))
            black = jnp.where(wide_first, roll(east, -HALO), west)
            fill = 1.0 if f == 2 else 0.0
            red = jnp.where(wide_used, red, fill)
            black = jnp.where(wide_used, black, fill)
            if f == 1:
                target[0, i, first:first + high, :] = red
                target[1, i, first:first + high, :] = black
            else:
                target[0, i + 1, top + first:top + first + high, :] = red
                target[1, i + 1, top + first:top + first + high, :] = black

    all_lane = lanes_of((rows + 2 * MARGIN, 128))
    lead = all_lane < SLOT
    tail = all_lane >= SLOT * (GROUPS - 1)
    spare_slot = SLOT * (layers // GROUPS)
    in_spare = (all_lane >= spare_slot) & (all_lane < spare_slot + SLOT)

    def wrap_pot(c):
        pb[c, 0] = jnp.where(lead, 0.0, roll(pb[c, GROUPS], SLOT))
        pb[c, GROUPS + 1] = jnp.where(tail, 0.0, roll(pb[c, 1], -SLOT))

    spare_row = layers % GROUPS + 1
    for c in range(2):
        wrap_pot(c)
        eb[c, spare_row] = jnp.where(in_spare, eb[1 - c, spare_row - 1], eb[c, spare_row])
    for c in range(2):
        eb[c, 0] = jnp.where(lead, eb[1 - c, 1], roll(eb[c, GROUPS], SLOT))
        eb[c, GROUPS + 1] = jnp.where(tail, 1.0, roll(eb[c, 1], -SLOT))

    for load in loads:
        load.wait()
    for c in range(2):
        ea[c, 0, top:top + rows, :] = ea[1 - c, 1, top:top + rows, :]
        ea[c, layers + 1, top:top + rows, :] = ea[1 - c, layers, top:top + rows, :]

    def around(src_a, src_b, other, color, i, t, body_a, body_b):
        r0 = top + 8 * t
        rs = slice(r0, r0 + 8)
        rm = slice(r0 - 1, r0 + 7)
        rp = slice(r0 + 1, r0 + 9)
        up = ~flat if color == 0 else flat
        side = src_b[other, i + 1, rs, :]
        edge = side
        for g in range(GROUPS):
            k = i + GROUPS * g
            here = src_a[other, k + 1, rs, :]
            halo = roll(side, -(SLOT * g + HALO))
            body_a(k, (
                here,
                jnp.where(up, src_a[other, k + 2, rs, :], src_a[other, k, rs, :]),
                src_a[other, k + 1, rm, :],
                src_a[other, k + 1, rp, :],
                jnp.where(at_0, halo, roll(here, 1)),
                jnp.where(at_127, halo, roll(here, -1)),
            ))
            if body_b is not None:
                edge = jnp.where(pick[g], roll(here, SLOT * g + HALO), edge)
        if body_b is not None:
            body_b((
                side,
                jnp.where(up, src_b[other, i, rs, :], src_b[other, i + 2, rs, :]),
                src_b[other, i + 1, rm, :],
                src_b[other, i + 1, rp, :],
                jnp.where(slot_east, edge, roll(side, -1)),
                jnp.where(slot_west, edge, roll(side, 1)),
            ))

    def coefficients(own, charge, sides):
        faces = [0.5 * (own + side) for side in sides]
        total = faces[0] + faces[1] + faces[2] + faces[3] + faces[4] + faces[5]
        scale = OVER_RELAX / total
        return [face * scale for face in faces] + [charge * scale]

    for c in range(2):
        def set_up(i, carry, c=c):
            for t in range(tiles):
                ts = slice(8 * t, 8 * t + 8)
                ps = slice(top + 8 * t, top + 8 * t + 8)

                def body_a(k, sides):
                    values = coefficients(ea[c, k + 1, ps, :], ca[c, k, ts, :], sides)
                    for n, value in enumerate(values):
                        wa[c, n, k, ts, :] = value

                def body_b(sides):
                    values = coefficients(eb[c, i + 1, ps, :], cb[c, i, ts, :], sides)
                    live = in_spare[0:8] & (i + 1 == spare_row)
                    for n, value in enumerate(values):
                        wb[c, n, i, ts, :] = jnp.where(live, 0.0, value)

                around(ea, eb, 1 - c, c, i, t, body_a, body_b)
            return carry

        lax.fori_loop(0, GROUPS, set_up, 0)
        for n in range(7):
            wa[c, n, layers] = jnp.zeros((rows, 128), F32)

    def combine(own, w, sides):
        left = w[0] * sides[0] + w[1] * sides[1]
        mid = w[2] * sides[2] + w[3] * sides[3]
        right = w[4] * sides[4] + w[5] * sides[5]
        return (w[6] - (OVER_RELAX - 1.0) * own) + (left + (mid + right))

    for step in range(2 * SWEEPS):
        c = step % 2
        reach = HALO - 1 - step
        t_low = (FIRST - reach) // 8
        t_high = -(-(FIRST + wide + reach) // 8)

        def half(i, carry, c=c, reach=reach, t_low=t_low, t_high=t_high):
            for t in range(t_low, t_high):
                ts = slice(8 * t, 8 * t + 8)
                ps = slice(top + 8 * t, top + 8 * t + 8)

                def body_a(k, sides):
                    w = [wa[c, n, k, ts, :] for n in range(7)]
                    pa[c, k + 1, ps, :] = combine(pa[c, k + 1, ps, :], w, sides)

                def body_b(sides):
                    w = [wb[c, n, i, ts, :] for n in range(7)]
                    pb[c, i + 1, ps, :] = combine(pb[c, i + 1, ps, :], w, sides)

                around(pa, pb, 1 - c, c, i, t, body_a, body_b if reach else None)
            return carry

        lax.fori_loop(0, GROUPS, half, 0)
        if reach:
            wrap_pot(c)

    press_out[depth] = jnp.zeros((wide, 128), F32)
    core = slice(top + FIRST, top + FIRST + wide)
    core_flat = parity_of((wide, 128))

    def finish(k, carry):
        red, black = pa[0, k + 1, core, :], pa[1, k + 1, core, :]
        e_red, e_black = ea[0, k + 1, core, :], ea[1, k + 1, core, :]
        q_red = 0.5 * e_red * red * red
        q_black = 0.5 * e_black * black * black
        pot_out[2 * k] = jnp.where(core_flat, red, black)
        pot_out[2 * k + 1] = jnp.where(core_flat, black, red)
        press_out[2 * k] = jnp.where(core_flat, q_red, q_black)
        press_out[2 * k + 1] = jnp.where(core_flat, q_black, q_red)
        return carry

    lax.fori_loop(0, layers, finish, 0)


def geometry(direction, offsets, table):
    c0, c1, c2, w = [lane_pick(table[n], direction) for n in range(4)]
    r0, r1, r2 = offsets
    arms = [c0, c1, c2, r1 * c2 - r2 * c1, r2 * c0 - r0 * c2, r0 * c1 - r1 * c0]
    return arms, w


ARM_REACH = 9.0
ARM_BITS = 21
ARM_STEP = 2.0 * ARM_REACH / (2**ARM_BITS - 1)
SPARE_BITS = 32 - ARM_BITS


def pack_arms(rb):
    a, b, c = [jnp.round((rb[n] + ARM_REACH) * (1.0 / ARM_STEP)).astype(jnp.int32) for n in range(3)]
    low = c & ((1 << SPARE_BITS) - 1)
    return (a << SPARE_BITS) | low, (b << SPARE_BITS) | (c >> SPARE_BITS)


def unpack_arms(first, second):
    low = (1 << SPARE_BITS) - 1
    whole = (1 << ARM_BITS) - 1
    a = (first >> SPARE_BITS) & whole
    b = (second >> SPARE_BITS) & whole
    c = ((second & low) << SPARE_BITS) | (first & low)
    return [part.astype(F32) * ARM_STEP - ARM_REACH for part in (a, b, c)]


def store_term(stage, n, value):
    stage[8 * n:8 * n + 8, :] = value


def add_by_slot(stage, slot, width):
    total = stage.shape[0] // 8
    fine = slot & 15
    coarse = slot >> 4
    small = lax.broadcasted_iota(jnp.int32, (16, 128), 0)
    hot, terms = [], []
    for s in range(8):
        match = (jnp.broadcast_to(fine[s:s + 1, :], (16, 128)) == small).astype(F32)
        match = match.astype(jnp.bfloat16)
        part = jnp.broadcast_to(coarse[s:s + 1, :].astype(F32), (16, 128)).astype(jnp.bfloat16)
        none = jnp.zeros((16, 128), jnp.bfloat16)
        hot.append(jnp.concatenate(
            [jnp.where(part == m, match, none) for m in range(width // 16)], axis=0
        ))
        value = stage[pl.ds(s, total, stride=8), :]
        head = value.astype(jnp.bfloat16)
        terms.append(jnp.concatenate(
            [head.astype(F32), value - head.astype(F32)], axis=0
        ).astype(jnp.bfloat16))
    return lax.dot_general(
        jnp.concatenate(terms, axis=1),
        jnp.concatenate(hot, axis=1),
        (((1,), (1,)), ((), ())),
        preferred_element_type=F32,
    )


def add_by_tile(stage, slot, per_tile):
    total = stage.shape[0] // 8
    shift = per_tile.bit_length() - 1
    tile = (slot >> shift).astype(F32)
    fine = (slot & (per_tile - 1)).astype(F32)
    small = lax.broadcasted_iota(jnp.int32, (per_tile, 128), 0).astype(F32).astype(jnp.bfloat16)
    one = jnp.ones((per_tile, 128), jnp.bfloat16)
    none = jnp.zeros((2 * total, 128), jnp.bfloat16)
    hot, terms = [], []
    for s in range(8):
        place = jnp.broadcast_to(fine[s:s + 1, :], (per_tile, 128)).astype(jnp.bfloat16)
        hot.append(jnp.where(place == small, one, jnp.zeros_like(one)))
        owner = jnp.broadcast_to(tile[s:s + 1, :], (2 * total, 128)).astype(jnp.bfloat16)
        value = stage[pl.ds(s, total, stride=8), :]
        head = value.astype(jnp.bfloat16)
        both = jnp.concatenate([head.astype(F32), value - head.astype(F32)], axis=0)
        both = both.astype(jnp.bfloat16)
        terms.append(jnp.concatenate([jnp.where(owner == t, both, none) for t in range(9)], axis=0))
    return lax.dot_general(
        jnp.concatenate(terms, axis=1),
        jnp.concatenate(hot, axis=1),
        (((1,), (1,)), ((), ())),
        preferred_element_type=F32,
    )


def fixed_kernel(slots, dirs, pops, rb, table, out, reach, stage, acc, *, width):
    acc[...] = jnp.zeros_like(acc)
    total = stage.shape[0] // 8
    for n in range(6 + len(PAIRS), total):
        store_term(stage, n, jnp.zeros((8, 128), F32))

    def block(b, carry):
        rs = pl.ds(pl.multiple_of(8 * b, 8), 8)
        arms, w = geometry(dirs[rs, :], [rb[n, rs, :] for n in range(3)], table)
        twice = 2.0 * pops[rs, :]
        weighted = [w * arm for arm in arms]
        for n in range(6):
            reach[n, rs, :] = jnp.where(slots[rs, :] >= 0, 6.0 * weighted[n], 0.0)
        for n in range(6):
            store_term(stage, n, twice * arms[n])
        for n, (a, d) in enumerate(PAIRS):
            store_term(stage, 6 + n, weighted[a] * arms[d])
        acc[...] += add_by_slot(stage, slots[rs, :], width)
        return carry

    lax.fori_loop(0, slots.shape[0] // 8, block, 0)
    out[...] = acc[0:total, :] + acc[total:, :]


BATCH = 8
AHEAD = 4


def press_kernel(
    low, passes, keys, arm0, arm1, table, press, fixed, motion, out, stage, acc, sums,
    *, per_tile
):
    acc[...] = jnp.zeros_like(acc)
    for n in range(6, stage.shape[0] // 8):
        store_term(stage, n, jnp.zeros((8, 128), F32))
    limit = press.shape[0] - AHEAD
    line = lax.broadcasted_iota(jnp.int32, (8, 128), 0)

    def batch(b, carry):
        spots = [pl.ds(pl.multiple_of(8 * (BATCH * b + j), 8), 8) for j in range(BATCH)]
        columns, offsets, starts = [], [], []
        for j in range(BATCH):
            place = (keys[spots[j], :] >> KEY_BITS) + (1 << 18)
            start = [low[8 * (BATCH * b + j) + s] for s in range(8)]
            first = jnp.zeros((8, 128), jnp.int32)
            for s in range(8):
                first = jnp.where(line == s, start[s], first)
            columns.append(place & 127)
            offsets.append((place >> 7) - first)
            starts.append(start)

        def look(m, found):
            found = list(found)
            for j in range(BATCH):
                bases = [jnp.minimum(starts[j][s] + AHEAD * m, limit) for s in range(8)]
                for t in range(AHEAD):
                    window = jnp.zeros((8, 128), F32)
                    for s in range(8):
                        row = press[pl.ds(bases[s] + t, 1), :]
                        window = jnp.where(line == s, jnp.broadcast_to(row, (8, 128)), window)
                    value = lane_pick(window, columns[j])
                    found[j] = jnp.where(offsets[j] == AHEAD * m + t, value, found[j])
            return tuple(found)

        found = lax.fori_loop(
            0, passes[b], look, tuple(jnp.zeros((8, 128), F32) for _ in range(BATCH))
        )
        for j in range(BATCH):
            rs = spots[j]
            code = keys[rs, :] & ((1 << KEY_BITS) - 1)
            slot = jnp.floor((code.astype(F32) + 0.5) * (1.0 / 18.0)).astype(jnp.int32)
            direction = code - 18 * slot
            arms, w = geometry(direction, unpack_arms(arm0[rs, :], arm1[rs, :]), table)
            wq = w * found[j]
            for n in range(6):
                store_term(stage, n, wq * arms[n])
            acc[...] += add_by_tile(stage, slot, per_tile)
        return carry

    lax.fori_loop(0, keys.shape[0] // (8 * BATCH), batch, 0)

    sums[...] = jnp.zeros_like(sums)
    for t in range(9):
        value = acc[16 * t:16 * t + 8, :] + acc[16 * t + 8:16 * t + 16, :]
        sums[:, per_tile * t:per_tile * (t + 1)] = value
    for a in range(6):
        drag = jnp.zeros_like(motion[0:1, :])
        for d in range(6):
            n = 6 + PAIRS.index((min(a, d), max(a, d)))
            drag += fixed[n:n + 1, :] * motion[d:d + 1, :]
        sums[a:a + 1, :] += fixed[a:a + 1, :] - 6.0 * drag
    head, last = sums[:, 0:128], sums[:, 256:384]
    lane = lanes_of((8, 128))
    for n in range(6):
        part = jnp.broadcast_to(last[n:n + 1, :], (8, 128))
        here = (line == 6 + n // 4) & (lane // per_tile == n % 4)
        head = jnp.where(here, roll(part, per_tile * (n % 4)), head)
    tail = sums[:, 128:256]

    def replicate(p, carry):
        out[p, 0:8, :] = head
        out[p, 8:16, :] = tail
        return carry

    lax.fori_loop(0, out.shape[0], replicate, 0)


TOGETHER = 4
AROUND = [(ox, oy) for ox in range(-2, 3) for oy in range(-2, 3)]


def reflect_kernel(
    control, partial_sums, slots, reach, pops, motion, report, out, spread, *, per_tile, counts
):
    lanes = motion.shape[1]
    slot_of_lane = lax.broadcasted_iota(jnp.int32, (8, lanes), 1) // per_tile
    tile_x = slot_of_lane // 3 - 1
    tile_y = slot_of_lane % 3 - 1
    totals = jnp.zeros((8, lanes), F32)
    lane_of = lanes_of((8, 128))
    line = lax.broadcasted_iota(jnp.int32, (8, 128), 0)
    place = lane_of % per_tile + per_tile * (line % 4)

    at = control.shape[0] - 2

    def unpack(n, carry):
        peer_x = lax.rem(control[at] + n - 2 + 2 * counts[0], counts[0])
        for m in range(5):
            peer_y = lax.rem(control[at + 1] + m - 2 + 2 * counts[1], counts[1])
            block = partial_sums[peer_x * counts[1] + peer_y]
            parts = [
                lane_pick(jnp.broadcast_to(block[r:r + 1, :], (8, 128)), place) for r in (6, 7)
            ]
            spread[5 * n + m, :, 0:128] = block[0:8, :]
            spread[5 * n + m, :, 128:256] = block[8:16, :]
            spread[5 * n + m, :, 256:384] = jnp.where(line < 4, parts[0], parts[1])
        return carry

    lax.fori_loop(0, 5, unpack, 0)
    for n, (ox, oy) in enumerate(AROUND):
        near = (abs(tile_x - ox) <= 1) & (abs(tile_y - oy) <= 1) & (slot_of_lane < 9)
        shift = per_tile * (3 * ox + oy)
        moved = pltpu.roll(spread[n], shift % lanes, 1)
        totals = totals + jnp.where(near, moved, 0.0)
    mass = 4.0 / 3.0 * math.pi * RADIUS**3
    inertia = 0.4 * mass * RADIUS**2
    is_force = lax.broadcasted_iota(jnp.int32, (8, lanes), 0) < 3
    moved = motion[...] + totals * jnp.where(is_force, 1.0 / mass, 1.0 / inertia)
    stated = totals * jnp.where(is_force, 1.0, 1.0 / RADIUS)
    report[...] = stated[0:6, 4 * per_tile:5 * per_tile]

    table = [
        [jnp.broadcast_to(moved[n:n + 1, 128 * h:128 * h + 128], (8, 128)) for h in range(lanes // 128)]
        for n in range(6)
    ]

    def batch(b, carry):
        for j in range(TOGETHER):
            rs = pl.ds(pl.multiple_of(8 * (TOGETHER * b + j), 8), 8)
            slot = slots[rs, :]
            lane = slot & 127
            part = slot >> 7
            along = jnp.zeros((8, 128), F32)
            for n in range(6):
                value = jnp.zeros((8, 128), F32)
                for h in range(lanes // 128):
                    value = jnp.where(part == h, lane_pick(table[n][h], lane), value)
                along += reach[n, rs, :] * value
            out[rs, :] = pops[rs, :] - along
        return carry

    lax.fori_loop(0, slots.shape[0] // (8 * TOGETHER), batch, 0)


def ring(axis):
    count = lax.axis_size(axis)
    forward = [(i, (i + 1) % count) for i in range(count)]
    return forward, [(b, a) for a, b in forward]


def scales():
    return jnp.array([POT_SCALE, CHARGE_SCALE, 1.0], F32).reshape(3, 1, 1, 1)


def to_half(strips):
    return (strips * scales()).astype(HALF)


def from_half(planes):
    each = (planes.shape[0] - 1) // 3
    back = [1.0 / POT_SCALE] * each + [1.0 / CHARGE_SCALE] * each + [1.0] * (each + 1)
    return planes.astype(F32) * jnp.array(back, F32)[:, None, None]


MOTION_SCALE = 2.0**10
REST_SCALE = 2.0**12


def motion_plane(motions, rows):
    value = motions.reshape(-1, motions.shape[-1]) * MOTION_SCALE
    head = lax.reduce_precision(value, 8, 10)
    both = jnp.concatenate([head, (value - head) * REST_SCALE], axis=0).astype(HALF)
    return jnp.pad(both, ((0, rows - both.shape[0]), (0, 128 - both.shape[1])))[None]


def motion_of(plane, shape):
    count = math.prod(shape[:-1])
    both = plane[:2 * count, :shape[-1]].astype(F32)
    value = both[:count] + both[count:] * (1.0 / REST_SCALE)
    return (value * (1.0 / MOTION_SCALE)).reshape(shape)


def vmem(n):
    return [pl.BlockSpec(memory_space=pltpu.VMEM)] * n


def grant(mib):
    return pltpu.CompilerParams(vmem_limit_bytes=mib * 1024 * 1024)


def shards(
    eps_field, charge, potential_start, colloid_vel, colloid_spin, link_dir, link_colloid,
    link_site, link_depth, link_pop, link_rb,
):
    depth, wide, long = charge.shape
    layers = depth // 2
    rows = wide + 2 * FIRST
    fx, bx = ring("gx")
    fy, by = ring("gy")

    per_tile = colloid_vel.shape[1]
    motion = jnp.concatenate([colloid_vel, colloid_spin], axis=0)
    def edge(part):
        strips = jnp.stack([
            potential_start[:, part] * POT_SCALE,
            charge[:, part] * CHARGE_SCALE,
            eps_field[:, part].astype(F32),
        ])
        strips = strips.transpose(0, 2, 1, 3).astype(HALF).reshape(3 * HALO, depth, 128)
        return jnp.concatenate([strips, motion_plane(motion, depth)], axis=0)

    low = lax.ppermute(edge(slice(wide - HALO, wide)), "gx", fx)
    high = lax.ppermute(edge(slice(0, HALO)), "gx", bx)

    width = 9 * per_tile
    count = link_pop.shape[-1]
    lines = count // 128
    ids = link_colloid.reshape(lines, 128)
    dirs = link_dir.reshape(lines, 128)
    pops = link_pop.reshape(lines, 128)
    rb = link_rb.reshape(3, lines, 128)
    count_x, count_y = lax.axis_size("gx"), lax.axis_size("gy")
    owner = ids // per_tile
    near_x = (owner // count_y - lax.axis_index("gx") + 1) % count_x
    near_y = (owner % count_y - lax.axis_index("gy") + 1) % count_y
    live = ids >= 0
    slots = jnp.where(live, (near_x * 3 + near_y) * per_tile + ids % per_tile, -1)
    place = link_depth.reshape(lines, 128) * (wide * long) + link_site.reshape(lines, 128)
    key = jnp.where(
        live, (place - (1 << 18)) * (1 << KEY_BITS) + slots * 18 + dirs, np.int32(2**31 - 1)
    )
    keys, arm0, arm1 = lax.sort(
        (key.reshape(-1), *(part.reshape(-1) for part in pack_arms(rb))),
        num_keys=1, is_stable=False,
    )
    keys, arm0, arm1, low, high = lax.optimization_barrier((keys, arm0, arm1, low, high))
    keys = keys.reshape(lines, 128)
    table = direction_table()
    table_rows = ((keys >> KEY_BITS) + (1 << 18)) >> 7
    row_low = jnp.minimum(table_rows[:, 0], depth * wide - 1)
    row_high = jnp.max(jnp.where(table_rows < depth * wide, table_rows, 0), axis=1)
    span = jnp.max((row_high - row_low + 1).reshape(-1, 8 * BATCH), axis=1)
    passes = (jnp.maximum(span, 0) + AHEAD - 1) // AHEAD
    home = jnp.stack([lax.axis_index("gx"), lax.axis_index("gy")])
    control = jnp.concatenate([passes, home])

    low, high = from_half(low), from_half(high)
    split, to_right, to_left = pl.pallas_call(
        pack_kernel,
        out_shape=(
            jax.ShapeDtypeStruct((6, layers + 1, rows, 128), F32),
            jax.ShapeDtypeStruct((3, GROUPS, wide + 2 * HALO, 128), F32),
            jax.ShapeDtypeStruct((3, GROUPS, wide + 2 * HALO, 128), F32),
        ),
        in_specs=vmem(5), out_specs=(pl.BlockSpec(memory_space=pltpu.HBM), *vmem(2)),
        compiler_params=grant(52), name="pack",
        scratch_shapes=[
            pltpu.VMEM((6, layers + 1, rows, 128), F32),
            pltpu.VMEM((2, 3 * GROUPS, wide + 2 * HALO, 128), F32),
            pltpu.SemaphoreType.DMA,
        ],
    )(potential_start, charge, eps_field,
      low.reshape(-1, 128), high.reshape(-1, 128))
    row = jnp.stack([
        motion_of(low[-1], motion.shape), motion, motion_of(high[-1], motion.shape)
    ])
    plane = motion_plane(row, wide + 2 * HALO)

    def strip(part):
        return jnp.concatenate([to_half(part).reshape(-1, *part.shape[2:]), plane], axis=0)

    to_right, dirs_late = lax.optimization_barrier((strip(to_right), dirs))
    from_left = lax.ppermute(to_right, "gy", fy)
    from_right = lax.ppermute(strip(to_left), "gy", by)
    from_left, from_right = from_half(from_left), from_half(from_right)
    near_motion = jnp.stack(
        [motion_of(from_left[-1], row.shape), row, motion_of(from_right[-1], row.shape)], axis=1
    )
    near_motion = near_motion.transpose(2, 0, 1, 3).reshape(6, width)

    terms = 32
    fixed, reach = pl.pallas_call(
        functools.partial(fixed_kernel, width=width),
        out_shape=(
            jax.ShapeDtypeStruct((terms, width), F32), jax.ShapeDtypeStruct((6, lines, 128), F32),
        ),
        in_specs=vmem(5), out_specs=tuple(vmem(2)),
        scratch_shapes=[pltpu.VMEM((8 * terms, 128), F32), pltpu.VMEM((2 * terms, width), F32)],
        compiler_params=grant(8), name="fixed",
        cost_estimate=pl.CostEstimate(flops=10**9, bytes_accessed=2 * 10**7, transcendentals=0),
    )(slots, dirs_late, pops, rb, table)

    tall = rows + 2 * MARGIN
    potential, press = pl.pallas_call(
        relax_kernel,
        out_shape=(
            jax.ShapeDtypeStruct((depth, wide, 128), F32),
            jax.ShapeDtypeStruct((depth + 1, wide, 128), F32),
        ),
        in_specs=[pl.BlockSpec(memory_space=pltpu.HBM)] + vmem(2), out_specs=tuple(vmem(2)),
        scratch_shapes=[
            pltpu.VMEM((2, layers + 3, tall, 128), F32),
            pltpu.VMEM((2, layers + 3, tall, 128), F32),
            pltpu.VMEM((2, layers + 1, rows, 128), F32),
            pltpu.VMEM((2, 7, layers + 1, rows, 128), F32),
            pltpu.VMEM((2, GROUPS + 2, tall, 128), F32),
            pltpu.VMEM((2, GROUPS + 2, tall, 128), F32),
            pltpu.VMEM((2, GROUPS, rows, 128), F32),
            pltpu.VMEM((2, 7, GROUPS, rows, 128), F32),
            pltpu.SemaphoreType.DMA((6,)),
        ],
        compiler_params=grant(48), name="relax",
    )(split, from_left, from_right)

    lanes = -(-width // 128) * 128
    fixed, near_motion = [
        jnp.pad(part, ((0, -part.shape[0] % 8), (0, lanes - width))) for part in (fixed, near_motion)
    ]
    devices = count_x * count_y
    smem = pl.BlockSpec(memory_space=pltpu.SMEM)
    pressed = pl.pallas_call(
        functools.partial(press_kernel, per_tile=per_tile),
        out_shape=jax.ShapeDtypeStruct((devices, 16, 128), F32),
        in_specs=[smem, smem] + vmem(7), out_specs=vmem(1)[0],
        scratch_shapes=[
            pltpu.VMEM((64, 128), F32), pltpu.VMEM((9 * 16, per_tile), F32),
            pltpu.VMEM((8, lanes), F32),
        ],
        compiler_params=grant(8), name="press",
    )(
        row_low, control, keys, arm0.reshape(lines, 128), arm1.reshape(lines, 128),
        table, press.reshape(-1, 128), fixed, near_motion,
    )

    partials = lax.all_to_all(pressed, ("gx", "gy"), 0, 0)

    report, link_out = pl.pallas_call(
        functools.partial(reflect_kernel, per_tile=per_tile, counts=(count_x, count_y)),
        out_shape=(
            jax.ShapeDtypeStruct((6, per_tile), F32), jax.ShapeDtypeStruct((lines, 128), F32),
        ),
        in_specs=[smem] + vmem(5), out_specs=tuple(vmem(2)), compiler_params=grant(6),
        scratch_shapes=[pltpu.VMEM((len(AROUND), 8, lanes), F32)], name="reflect",
    )(control, partials, slots, reach, pops, near_motion)
    return potential, report, link_out.reshape(link_pop.shape)


def solution(mesh):
    placed = (
        P(None, "gx", "gy"),
        P(None, "gx", "gy"),
        P(None, "gx", "gy"),
        P(None, ("gx", "gy")),
        P(None, ("gx", "gy")),
        P("gx", "gy", None),
        P("gx", "gy", None),
        P("gx", "gy", None),
        P("gx", "gy", None),
        P("gx", "gy", None),
        P(None, "gx", "gy", None),
    )
    return jax.shard_map(
        shards,
        mesh=mesh,
        in_specs=placed,
        out_specs=(P(None, "gx", "gy"), P(None, ("gx", "gy")), P("gx", "gy", None)),
        check_vma=False,
    )
```

```python
import functools
import math

import jax
import jax.numpy as jnp
import numpy as np
from jax import lax
from jax.experimental import pallas as pl
from jax.experimental.pallas import tpu as pltpu
from jax.sharding import PartitionSpec as P

SWEEPS = 6
RADIUS = 8
OVER_RELAX = 1.6
HALO = 2 * SWEEPS
FIRST = 16
MARGIN = 8
GROUPS = 5
SLOT = 2 * HALO
KEY_BITS = 13
F32 = jnp.float32
HALF = jnp.float16
POT_SCALE = 2.0**14
CHARGE_SCALE = 2.0**13

VELOCITY = np.array(
    [
        [1, 0, 0], [-1, 0, 0], [0, 1, 0], [0, -1, 0], [0, 0, 1], [0, 0, -1],
        [1, 1, 0], [1, -1, 0], [-1, 1, 0], [-1, -1, 0], [1, 0, 1], [1, 0, -1],
        [-1, 0, 1], [-1, 0, -1], [0, 1, 1], [0, 1, -1], [0, -1, 1], [0, -1, -1],
    ],
    dtype=np.float32,
)
WEIGHT = np.array([1.0 / 18.0] * 6 + [1.0 / 36.0] * 12, dtype=np.float32)


def direction_table():
    table = np.zeros((4, 8, 128), np.float32)
    table[:3, :, :18] = VELOCITY.T[:, None, :]
    table[3, :, :18] = WEIGHT[None, :]
    return jnp.asarray(table)


PAIRS = [(a, b) for a in range(6) for b in range(a, 6)]


def lane_pick(table, index):
    return jnp.take_along_axis(table, index, axis=1, mode="promise_in_bounds")


def roll(value, shift):
    return pltpu.roll(value, shift % 128, 1)


def lanes_of(shape):
    return lax.broadcasted_iota(jnp.int32, shape, 1)


def parity_of(shape):
    rows = lax.broadcasted_iota(jnp.int32, shape, 0)
    return (rows + lanes_of(shape)) % 2 == 0


def pack_kernel(pot, charge, eps, low, high, kept, to_right, to_left, split, edges, sem):
    depth, wide, _ = pot.shape
    layers = depth // 2
    last = FIRST + wide

    def strip(source, f, z):
        return source[pl.ds(f * HALO * depth + z, HALO, stride=depth), :]

    def build(k, carry):
        for f, field in enumerate((pot, charge, eps)):
            fill = 1.0 if f == 2 else 0.0
            parts = (
                (FIRST, field[2 * k].astype(F32), field[2 * k + 1].astype(F32)),
                (FIRST - HALO, *(strip(low, f, 2 * k + n) for n in range(2))),
                (last, *(strip(high, f, 2 * k + n) for n in range(2))),
            )
            for start, even, odd in parts:
                flat = parity_of(even.shape)
                count = even.shape[0]
                split[2 * f, k, start:start + count, :] = jnp.where(flat, even, odd)
                split[2 * f + 1, k, start:start + count, :] = jnp.where(flat, odd, even)
            spare = FIRST - HALO
            edge = jnp.full((spare, 128), fill, F32)
            for c in range(2):
                split[2 * f + c, k, 0:spare, :] = edge
                split[2 * f + c, k, last + HALO:last + HALO + spare, :] = edge
        return carry

    lax.fori_loop(0, layers, build, 0)
    for f in range(3):
        for c in range(2):
            split[2 * f + c, layers] = jnp.full(
                (split.shape[2], 128), 1.0 if f == 2 else 0.0, F32
            )

    keep = pltpu.make_async_copy(split, kept, sem)
    keep.start()

    rows = slice(FIRST - HALO, last + HALO)
    lane = lanes_of((wide + 2 * HALO, 128))
    early = lane % SLOT < HALO
    slot_of = [(lane >= SLOT * g) & (lane < SLOT * (g + 1)) for g in range(GROUPS)]

    def gather_edges(n, carry):
        f = n // GROUPS
        i = n % GROUPS
        for c in range(2):
            value = jnp.zeros((wide + 2 * HALO, 128), F32)
            for g in range(GROUPS):
                field = split[2 * f + c, i + GROUPS * g, rows, :]
                value = jnp.where(slot_of[g], roll(field, SLOT * g + HALO), value)
            edges[c, n] = value
        return carry

    lax.fori_loop(0, 3 * GROUPS, gather_edges, 0)

    middle = lane - 2 * (lane % SLOT) + SLOT - 1
    near, same, far = [jnp.clip(middle + n * HALO, 0, 127) for n in (-1, 0, 1)]

    def strips(n, carry):
        f = n // GROUPS
        i = n % GROUPS
        red, black = edges[0, n], edges[1, n]
        to_right[f, i] = jnp.where(early, lane_pick(red, near), lane_pick(black, same))
        to_left[f, i] = jnp.where(early, lane_pick(red, same), lane_pick(black, far))
        return carry

    lax.fori_loop(0, 3 * GROUPS, strips, 0)
    keep.wait()


def relax_kernel(
    kept, from_left, from_right, pot_out, press_out, pa, ea, ca, wa, pb, eb, cb, wb, sems
):
    layers = kept.shape[1] - 1
    depth, wide, _ = pot_out.shape
    rows = kept.shape[2]
    tiles = rows // 8
    top = MARGIN
    lane = lanes_of((8, 128))
    flat = parity_of((8, 128))
    at_0 = lane == 0
    at_127 = lane == 127
    in_slot = lane % SLOT
    slot_east = in_slot == HALO - 1
    slot_west = in_slot == HALO
    pick = [(lane == SLOT * g + HALO - 1) | (lane == SLOT * g + HALO) for g in range(GROUPS)]

    zero = jnp.zeros((rows + 2 * MARGIN, 128), F32)
    one = jnp.ones((rows + 2 * MARGIN, 128), F32)
    margin0 = jnp.zeros((MARGIN, 128), F32)
    margin1 = jnp.ones((MARGIN, 128), F32)
    body = pl.ds(top, rows)
    middle = pl.ds(1, layers + 1)
    loads = []
    for c in range(2):
        loads.append(pltpu.make_async_copy(kept.at[4 + c], ea.at[c, middle, body], sems.at[c]))
        loads.append(pltpu.make_async_copy(kept.at[2 + c], ca.at[c], sems.at[2 + c]))
        loads.append(pltpu.make_async_copy(kept.at[c], pa.at[c, middle, body], sems.at[4 + c]))
        for load in loads[-3:]:
            load.start()

    def set_margins(k, carry):
        for c in range(2):
            for start in (0, top + rows):
                pa[c, k + 1, start:start + MARGIN, :] = margin0
                ea[c, k + 1, start:start + MARGIN, :] = margin1
        return carry

    lax.fori_loop(0, layers + 1, set_margins, 0)
    for c in range(2):
        pa[c, 0] = zero
        pa[c, layers + 2] = zero
        for start in (0, top + rows):
            ea[c, 0, start:start + MARGIN, :] = margin1
        ea[c, layers + 2] = one

    first = FIRST - HALO
    high = wide + 2 * HALO
    wide_lane = lanes_of((high, 128))
    wide_first = wide_lane % SLOT < HALO
    wide_used = wide_lane < SLOT * GROUPS
    for c in range(2):
        for i in range(GROUPS + 2):
            pb[c, i] = zero
            eb[c, i] = one
        for i in range(GROUPS):
            cb[c, i] = jnp.zeros((rows, 128), F32)

    for f, target in enumerate((pb, cb, eb)):
        for i in range(GROUPS):
            west = from_left[GROUPS * f + i]
            east = from_right[GROUPS * f + i]
            red = jnp.where(wide_first, east, roll(west, HALO))
            black = jnp.where(wide_first, roll(east, -HALO), west)
            fill = 1.0 if f == 2 else 0.0
            red = jnp.where(wide_used, red, fill)
            black = jnp.where(wide_used, black, fill)
            if f == 1:
                target[0, i, first:first + high, :] = red
                target[1, i, first:first + high, :] = black
            else:
                target[0, i + 1, top + first:top + first + high, :] = red
                target[1, i + 1, top + first:top + first + high, :] = black

    all_lane = lanes_of((rows + 2 * MARGIN, 128))
    lead = all_lane < SLOT
    tail = all_lane >= SLOT * (GROUPS - 1)
    spare_slot = SLOT * (layers // GROUPS)
    in_spare = (all_lane >= spare_slot) & (all_lane < spare_slot + SLOT)

    def wrap_pot(c):
        pb[c, 0] = jnp.where(lead, 0.0, roll(pb[c, GROUPS], SLOT))
        pb[c, GROUPS + 1] = jnp.where(tail, 0.0, roll(pb[c, 1], -SLOT))

    spare_row = layers % GROUPS + 1
    for c in range(2):
        wrap_pot(c)
        eb[c, spare_row] = jnp.where(in_spare, eb[1 - c, spare_row - 1], eb[c, spare_row])
    for c in range(2):
        eb[c, 0] = jnp.where(lead, eb[1 - c, 1], roll(eb[c, GROUPS], SLOT))
        eb[c, GROUPS + 1] = jnp.where(tail, 1.0, roll(eb[c, 1], -SLOT))

    for load in loads:
        load.wait()
    for c in range(2):
        ea[c, 0, top:top + rows, :] = ea[1 - c, 1, top:top + rows, :]
        ea[c, layers + 1, top:top + rows, :] = ea[1 - c, layers, top:top + rows, :]

    def around(src_a, src_b, other, color, i, t, body_a, body_b):
        r0 = top + 8 * t
        rs = slice(r0, r0 + 8)
        rm = slice(r0 - 1, r0 + 7)
        rp = slice(r0 + 1, r0 + 9)
        up = ~flat if color == 0 else flat
        side = src_b[other, i + 1, rs, :]
        edge = side
        for g in range(GROUPS):
            k = i + GROUPS * g
            here = src_a[other, k + 1, rs, :]
            halo = roll(side, -(SLOT * g + HALO))
            body_a(k, (
                here,
                jnp.where(up, src_a[other, k + 2, rs, :], src_a[other, k, rs, :]),
                src_a[other, k + 1, rm, :],
                src_a[other, k + 1, rp, :],
                jnp.where(at_0, halo, roll(here, 1)),
                jnp.where(at_127, halo, roll(here, -1)),
            ))
            if body_b is not None:
                edge = jnp.where(pick[g], roll(here, SLOT * g + HALO), edge)
        if body_b is not None:
            body_b((
                side,
                jnp.where(up, src_b[other, i, rs, :], src_b[other, i + 2, rs, :]),
                src_b[other, i + 1, rm, :],
                src_b[other, i + 1, rp, :],
                jnp.where(slot_east, edge, roll(side, -1)),
                jnp.where(slot_west, edge, roll(side, 1)),
            ))

    def coefficients(own, charge, sides):
        faces = [0.5 * (own + side) for side in sides]
        total = faces[0] + faces[1] + faces[2] + faces[3] + faces[4] + faces[5]
        scale = OVER_RELAX / total
        return [face * scale for face in faces] + [charge * scale]

    for c in range(2):
        def set_up(i, carry, c=c):
            for t in range(tiles):
                ts = slice(8 * t, 8 * t + 8)
                ps = slice(top + 8 * t, top + 8 * t + 8)

                def body_a(k, sides):
                    values = coefficients(ea[c, k + 1, ps, :], ca[c, k, ts, :], sides)
                    for n, value in enumerate(values):
                        wa[c, n, k, ts, :] = value

                def body_b(sides):
                    values = coefficients(eb[c, i + 1, ps, :], cb[c, i, ts, :], sides)
                    live = in_spare[0:8] & (i + 1 == spare_row)
                    for n, value in enumerate(values):
                        wb[c, n, i, ts, :] = jnp.where(live, 0.0, value)

                around(ea, eb, 1 - c, c, i, t, body_a, body_b)
            return carry

        lax.fori_loop(0, GROUPS, set_up, 0)
        for n in range(7):
            wa[c, n, layers] = jnp.zeros((rows, 128), F32)

    def combine(own, w, sides):
        left = w[0] * sides[0] + w[1] * sides[1]
        mid = w[2] * sides[2] + w[3] * sides[3]
        right = w[4] * sides[4] + w[5] * sides[5]
        return (w[6] - (OVER_RELAX - 1.0) * own) + (left + (mid + right))

    for step in range(2 * SWEEPS):
        c = step % 2
        reach = HALO - 1 - step
        t_low = (FIRST - reach) // 8
        t_high = -(-(FIRST + wide + reach) // 8)

        def half(i, carry, c=c, reach=reach, t_low=t_low, t_high=t_high):
            for t in range(t_low, t_high):
                ts = slice(8 * t, 8 * t + 8)
                ps = slice(top + 8 * t, top + 8 * t + 8)

                def body_a(k, sides):
                    w = [wa[c, n, k, ts, :] for n in range(7)]
                    pa[c, k + 1, ps, :] = combine(pa[c, k + 1, ps, :], w, sides)

                def body_b(sides):
                    w = [wb[c, n, i, ts, :] for n in range(7)]
                    pb[c, i + 1, ps, :] = combine(pb[c, i + 1, ps, :], w, sides)

                around(pa, pb, 1 - c, c, i, t, body_a, body_b if reach else None)
            return carry

        lax.fori_loop(0, GROUPS, half, 0)
        if reach:
            wrap_pot(c)

    press_out[depth] = jnp.zeros((wide, 128), F32)
    core = slice(top + FIRST, top + FIRST + wide)
    core_flat = parity_of((wide, 128))

    def finish(k, carry):
        red, black = pa[0, k + 1, core, :], pa[1, k + 1, core, :]
        e_red, e_black = ea[0, k + 1, core, :], ea[1, k + 1, core, :]
        q_red = 0.5 * e_red * red * red
        q_black = 0.5 * e_black * black * black
        pot_out[2 * k] = jnp.where(core_flat, red, black)
        pot_out[2 * k + 1] = jnp.where(core_flat, black, red)
        press_out[2 * k] = jnp.where(core_flat, q_red, q_black)
        press_out[2 * k + 1] = jnp.where(core_flat, q_black, q_red)
        return carry

    lax.fori_loop(0, layers, finish, 0)


def geometry(direction, offsets, table):
    c0, c1, c2, w = [lane_pick(table[n], direction) for n in range(4)]
    r0, r1, r2 = offsets
    arms = [c0, c1, c2, r1 * c2 - r2 * c1, r2 * c0 - r0 * c2, r0 * c1 - r1 * c0]
    return arms, w


ARM_REACH = 9.0
ARM_BITS = 21
ARM_STEP = 2.0 * ARM_REACH / (2**ARM_BITS - 1)
SPARE_BITS = 32 - ARM_BITS


def pack_arms(rb):
    a, b, c = [jnp.round((rb[n] + ARM_REACH) * (1.0 / ARM_STEP)).astype(jnp.int32) for n in range(3)]
    low = c & ((1 << SPARE_BITS) - 1)
    return (a << SPARE_BITS) | low, (b << SPARE_BITS) | (c >> SPARE_BITS)


def unpack_arms(first, second):
    low = (1 << SPARE_BITS) - 1
    whole = (1 << ARM_BITS) - 1
    a = (first >> SPARE_BITS) & whole
    b = (second >> SPARE_BITS) & whole
    c = ((second & low) << SPARE_BITS) | (first & low)
    return [part.astype(F32) * ARM_STEP - ARM_REACH for part in (a, b, c)]


def store_term(stage, n, value):
    stage[8 * n:8 * n + 8, :] = value


def add_by_slot(stage, slot, width):
    total = stage.shape[0] // 8
    fine = slot & 15
    coarse = slot >> 4
    small = lax.broadcasted_iota(jnp.int32, (16, 128), 0)
    hot, terms = [], []
    for s in range(8):
        match = (jnp.broadcast_to(fine[s:s + 1, :], (16, 128)) == small).astype(F32)
        match = match.astype(jnp.bfloat16)
        part = jnp.broadcast_to(coarse[s:s + 1, :].astype(F32), (16, 128)).astype(jnp.bfloat16)
        none = jnp.zeros((16, 128), jnp.bfloat16)
        hot.append(jnp.concatenate(
            [jnp.where(part == m, match, none) for m in range(width // 16)], axis=0
        ))
        value = stage[pl.ds(s, total, stride=8), :]
        head = value.astype(jnp.bfloat16)
        terms.append(jnp.concatenate(
            [head.astype(F32), value - head.astype(F32)], axis=0
        ).astype(jnp.bfloat16))
    return lax.dot_general(
        jnp.concatenate(terms, axis=1),
        jnp.concatenate(hot, axis=1),
        (((1,), (1,)), ((), ())),
        preferred_element_type=F32,
    )


def add_by_tile(stage, slot, per_tile):
    total = stage.shape[0] // 8
    shift = per_tile.bit_length() - 1
    tile = (slot >> shift).astype(F32)
    fine = (slot & (per_tile - 1)).astype(F32)
    small = lax.broadcasted_iota(jnp.int32, (per_tile, 128), 0).astype(F32).astype(jnp.bfloat16)
    one = jnp.ones((per_tile, 128), jnp.bfloat16)
    none = jnp.zeros((2 * total, 128), jnp.bfloat16)
    hot, terms = [], []
    for s in range(8):
        place = jnp.broadcast_to(fine[s:s + 1, :], (per_tile, 128)).astype(jnp.bfloat16)
        hot.append(jnp.where(place == small, one, jnp.zeros_like(one)))
        owner = jnp.broadcast_to(tile[s:s + 1, :], (2 * total, 128)).astype(jnp.bfloat16)
        value = stage[pl.ds(s, total, stride=8), :]
        head = value.astype(jnp.bfloat16)
        both = jnp.concatenate([head.astype(F32), value - head.astype(F32)], axis=0)
        both = both.astype(jnp.bfloat16)
        terms.append(jnp.concatenate([jnp.where(owner == t, both, none) for t in range(9)], axis=0))
    return lax.dot_general(
        jnp.concatenate(terms, axis=1),
        jnp.concatenate(hot, axis=1),
        (((1,), (1,)), ((), ())),
        preferred_element_type=F32,
    )


def fixed_kernel(slots, dirs, pops, rb, table, out, reach, stage, acc, *, width):
    acc[...] = jnp.zeros_like(acc)
    total = stage.shape[0] // 8
    for n in range(6 + len(PAIRS), total):
        store_term(stage, n, jnp.zeros((8, 128), F32))

    def block(b, carry):
        rs = pl.ds(pl.multiple_of(8 * b, 8), 8)
        arms, w = geometry(dirs[rs, :], [rb[n, rs, :] for n in range(3)], table)
        twice = 2.0 * pops[rs, :]
        weighted = [w * arm for arm in arms]
        for n in range(6):
            reach[n, rs, :] = jnp.where(slots[rs, :] >= 0, 6.0 * weighted[n], 0.0)
        for n in range(6):
            store_term(stage, n, twice * arms[n])
        for n, (a, d) in enumerate(PAIRS):
            store_term(stage, 6 + n, weighted[a] * arms[d])
        acc[...] += add_by_slot(stage, slots[rs, :], width)
        return carry

    lax.fori_loop(0, slots.shape[0] // 8, block, 0)
    out[...] = acc[0:total, :] + acc[total:, :]


BATCH = 8
AHEAD = 8


def press_kernel(
    low, passes, keys, arm0, arm1, table, press, fixed, motion, out, stage, acc, sums,
    *, per_tile
):
    acc[...] = jnp.zeros_like(acc)
    for n in range(6, stage.shape[0] // 8):
        store_term(stage, n, jnp.zeros((8, 128), F32))
    limit = press.shape[0] - AHEAD
    line = lax.broadcasted_iota(jnp.int32, (8, 128), 0)

    def batch(b, carry):
        spots = [pl.ds(pl.multiple_of(8 * (BATCH * b + j), 8), 8) for j in range(BATCH)]
        columns, offsets, starts = [], [], []
        for j in range(BATCH):
            place = (keys[spots[j], :] >> KEY_BITS) + (1 << 18)
            start = [low[8 * (BATCH * b + j) + s] for s in range(8)]
            first = jnp.zeros((8, 128), jnp.int32)
            for s in range(8):
                first = jnp.where(line == s, start[s], first)
            columns.append(place & 127)
            offsets.append((place >> 7) - first)
            starts.append(start)

        def look(m, found):
            found = list(found)
            for j in range(BATCH):
                bases = [jnp.minimum(starts[j][s] + AHEAD * m, limit) for s in range(8)]
                for t in range(AHEAD):
                    window = jnp.zeros((8, 128), F32)
                    for s in range(8):
                        row = press[pl.ds(bases[s] + t, 1), :]
                        window = jnp.where(line == s, jnp.broadcast_to(row, (8, 128)), window)
                    value = lane_pick(window, columns[j])
                    found[j] = jnp.where(offsets[j] == AHEAD * m + t, value, found[j])
            return tuple(found)

        found = lax.fori_loop(
            0, passes[b], look, tuple(jnp.zeros((8, 128), F32) for _ in range(BATCH))
        )
        for j in range(BATCH):
            rs = spots[j]
            code = keys[rs, :] & ((1 << KEY_BITS) - 1)
            slot = jnp.floor((code.astype(F32) + 0.5) * (1.0 / 18.0)).astype(jnp.int32)
            direction = code - 18 * slot
            arms, w = geometry(direction, unpack_arms(arm0[rs, :], arm1[rs, :]), table)
            wq = w * found[j]
            for n in range(6):
                store_term(stage, n, wq * arms[n])
            acc[...] += add_by_tile(stage, slot, per_tile)
        return carry

    lax.fori_loop(0, keys.shape[0] // (8 * BATCH), batch, 0)

    sums[...] = jnp.zeros_like(sums)
    for t in range(9):
        value = acc[16 * t:16 * t + 8, :] + acc[16 * t + 8:16 * t + 16, :]
        sums[:, per_tile * t:per_tile * (t + 1)] = value
    for a in range(6):
        drag = jnp.zeros_like(motion[0:1, :])
        for d in range(6):
            n = 6 + PAIRS.index((min(a, d), max(a, d)))
            drag += fixed[n:n + 1, :] * motion[d:d + 1, :]
        sums[a:a + 1, :] += fixed[a:a + 1, :] - 6.0 * drag
    head, last = sums[:, 0:128], sums[:, 256:384]
    lane = lanes_of((8, 128))
    for n in range(6):
        part = jnp.broadcast_to(last[n:n + 1, :], (8, 128))
        here = (line == 6 + n // 4) & (lane // per_tile == n % 4)
        head = jnp.where(here, roll(part, per_tile * (n % 4)), head)
    tail = sums[:, 128:256]

    def replicate(p, carry):
        out[p, 0:8, :] = head
        out[p, 8:16, :] = tail
        return carry

    lax.fori_loop(0, out.shape[0], replicate, 0)


TOGETHER = 8
AROUND = [(ox, oy) for ox in range(-2, 3) for oy in range(-2, 3)]


def reflect_kernel(
    control, partial_sums, slots, reach, pops, motion, report, out, spread, *, per_tile, counts
):
    lanes = motion.shape[1]
    slot_of_lane = lax.broadcasted_iota(jnp.int32, (8, lanes), 1) // per_tile
    tile_x = slot_of_lane // 3 - 1
    tile_y = slot_of_lane % 3 - 1
    totals = jnp.zeros((8, lanes), F32)
    lane_of = lanes_of((8, 128))
    line = lax.broadcasted_iota(jnp.int32, (8, 128), 0)
    place = lane_of % per_tile + per_tile * (line % 4)

    at = control.shape[0] - 2

    def unpack(n, carry):
        peer_x = lax.rem(control[at] + n - 2 + 2 * counts[0], counts[0])
        for m in range(5):
            peer_y = lax.rem(control[at + 1] + m - 2 + 2 * counts[1], counts[1])
            block = partial_sums[peer_x * counts[1] + peer_y]
            parts = [
                lane_pick(jnp.broadcast_to(block[r:r + 1, :], (8, 128)), place) for r in (6, 7)
            ]
            spread[5 * n + m, :, 0:128] = block[0:8, :]
            spread[5 * n + m, :, 128:256] = block[8:16, :]
            spread[5 * n + m, :, 256:384] = jnp.where(line < 4, parts[0], parts[1])
        return carry

    lax.fori_loop(0, 5, unpack, 0)
    for n, (ox, oy) in enumerate(AROUND):
        near = (abs(tile_x - ox) <= 1) & (abs(tile_y - oy) <= 1) & (slot_of_lane < 9)
        shift = per_tile * (3 * ox + oy)
        moved = pltpu.roll(spread[n], shift % lanes, 1)
        totals = totals + jnp.where(near, moved, 0.0)
    mass = 4.0 / 3.0 * math.pi * RADIUS**3
    inertia = 0.4 * mass * RADIUS**2
    is_force = lax.broadcasted_iota(jnp.int32, (8, lanes), 0) < 3
    moved = motion[...] + totals * jnp.where(is_force, 1.0 / mass, 1.0 / inertia)
    stated = totals * jnp.where(is_force, 1.0, 1.0 / RADIUS)
    report[...] = stated[0:6, 4 * per_tile:5 * per_tile]

    table = [
        [jnp.broadcast_to(moved[n:n + 1, 128 * h:128 * h + 128], (8, 128)) for h in range(lanes // 128)]
        for n in range(6)
    ]

    def batch(b, carry):
        for j in range(TOGETHER):
            rs = pl.ds(pl.multiple_of(8 * (TOGETHER * b + j), 8), 8)
            slot = slots[rs, :]
            lane = slot & 127
            part = slot >> 7
            along = jnp.zeros((8, 128), F32)
            for n in range(6):
                value = jnp.zeros((8, 128), F32)
                for h in range(lanes // 128):
                    value = jnp.where(part == h, lane_pick(table[n][h], lane), value)
                along += reach[n, rs, :] * value
            out[rs, :] = pops[rs, :] - along
        return carry

    lax.fori_loop(0, slots.shape[0] // (8 * TOGETHER), batch, 0)


def ring(axis):
    count = lax.axis_size(axis)
    forward = [(i, (i + 1) % count) for i in range(count)]
    return forward, [(b, a) for a, b in forward]


def scales():
    return jnp.array([POT_SCALE, CHARGE_SCALE, 1.0], F32).reshape(3, 1, 1, 1)


def to_half(strips):
    return (strips * scales()).astype(HALF)


def from_half(planes):
    each = (planes.shape[0] - 1) // 3
    back = [1.0 / POT_SCALE] * each + [1.0 / CHARGE_SCALE] * each + [1.0] * (each + 1)
    return planes.astype(F32) * jnp.array(back, F32)[:, None, None]


MOTION_SCALE = 2.0**10
REST_SCALE = 2.0**12


def motion_plane(motions, rows):
    value = motions.reshape(-1, motions.shape[-1]) * MOTION_SCALE
    head = lax.reduce_precision(value, 8, 10)
    both = jnp.concatenate([head, (value - head) * REST_SCALE], axis=0).astype(HALF)
    return jnp.pad(both, ((0, rows - both.shape[0]), (0, 128 - both.shape[1])))[None]


def motion_of(plane, shape):
    count = math.prod(shape[:-1])
    both = plane[:2 * count, :shape[-1]].astype(F32)
    value = both[:count] + both[count:] * (1.0 / REST_SCALE)
    return (value * (1.0 / MOTION_SCALE)).reshape(shape)


def vmem(n):
    return [pl.BlockSpec(memory_space=pltpu.VMEM)] * n


def grant(mib):
    return pltpu.CompilerParams(vmem_limit_bytes=mib * 1024 * 1024)


def shards(
    eps_field, charge, potential_start, colloid_vel, colloid_spin, link_dir, link_colloid,
    link_site, link_depth, link_pop, link_rb,
):
    depth, wide, long = charge.shape
    layers = depth // 2
    rows = wide + 2 * FIRST
    fx, bx = ring("gx")
    fy, by = ring("gy")

    per_tile = colloid_vel.shape[1]
    motion = jnp.concatenate([colloid_vel, colloid_spin], axis=0)
    def edge(part):
        strips = jnp.stack([
            potential_start[:, part] * POT_SCALE,
            charge[:, part] * CHARGE_SCALE,
            eps_field[:, part].astype(F32),
        ])
        strips = strips.transpose(0, 2, 1, 3).astype(HALF).reshape(3 * HALO, depth, 128)
        return jnp.concatenate([strips, motion_plane(motion, depth)], axis=0)

    low = lax.ppermute(edge(slice(wide - HALO, wide)), "gx", fx)
    high = lax.ppermute(edge(slice(0, HALO)), "gx", bx)

    width = 9 * per_tile
    count = link_pop.shape[-1]
    lines = count // 128
    ids = link_colloid.reshape(lines, 128)
    dirs = link_dir.reshape(lines, 128)
    pops = link_pop.reshape(lines, 128)
    rb = link_rb.reshape(3, lines, 128)
    count_x, count_y = lax.axis_size("gx"), lax.axis_size("gy")
    owner = ids // per_tile
    near_x = (owner // count_y - lax.axis_index("gx") + 1) % count_x
    near_y = (owner % count_y - lax.axis_index("gy") + 1) % count_y
    live = ids >= 0
    slots = jnp.where(live, (near_x * 3 + near_y) * per_tile + ids % per_tile, -1)
    place = link_depth.reshape(lines, 128) * (wide * long) + link_site.reshape(lines, 128)
    key = jnp.where(
        live, (place - (1 << 18)) * (1 << KEY_BITS) + slots * 18 + dirs, np.int32(2**31 - 1)
    )
    keys, arm0, arm1 = lax.sort(
        (key.reshape(-1), *(part.reshape(-1) for part in pack_arms(rb))),
        num_keys=1, is_stable=False,
    )
    keys, arm0, arm1, low, high = lax.optimization_barrier((keys, arm0, arm1, low, high))
    keys = keys.reshape(lines, 128)
    table = direction_table()
    table_rows = ((keys >> KEY_BITS) + (1 << 18)) >> 7
    row_low = jnp.minimum(table_rows[:, 0], depth * wide - 1)
    row_high = jnp.max(jnp.where(table_rows < depth * wide, table_rows, 0), axis=1)
    span = jnp.max((row_high - row_low + 1).reshape(-1, 8 * BATCH), axis=1)
    passes = (jnp.maximum(span, 0) + AHEAD - 1) // AHEAD
    home = jnp.stack([lax.axis_index("gx"), lax.axis_index("gy")])
    control = jnp.concatenate([passes, home])

    low, high = from_half(low), from_half(high)
    split, to_right, to_left = pl.pallas_call(
        pack_kernel,
        out_shape=(
            jax.ShapeDtypeStruct((6, layers + 1, rows, 128), F32),
            jax.ShapeDtypeStruct((3, GROUPS, wide + 2 * HALO, 128), F32),
            jax.ShapeDtypeStruct((3, GROUPS, wide + 2 * HALO, 128), F32),
        ),
        in_specs=vmem(5), out_specs=(pl.BlockSpec(memory_space=pltpu.HBM), *vmem(2)),
        compiler_params=grant(52), name="pack",
        scratch_shapes=[
            pltpu.VMEM((6, layers + 1, rows, 128), F32),
            pltpu.VMEM((2, 3 * GROUPS, wide + 2 * HALO, 128), F32),
            pltpu.SemaphoreType.DMA,
        ],
    )(potential_start, charge, eps_field,
      low.reshape(-1, 128), high.reshape(-1, 128))
    row = jnp.stack([
        motion_of(low[-1], motion.shape), motion, motion_of(high[-1], motion.shape)
    ])
    plane = motion_plane(row, wide + 2 * HALO)

    def strip(part):
        return jnp.concatenate([to_half(part).reshape(-1, *part.shape[2:]), plane], axis=0)

    to_right, dirs_late = lax.optimization_barrier((strip(to_right), dirs))
    from_left = lax.ppermute(to_right, "gy", fy)
    from_right = lax.ppermute(strip(to_left), "gy", by)
    from_left, from_right = from_half(from_left), from_half(from_right)
    near_motion = jnp.stack(
        [motion_of(from_left[-1], row.shape), row, motion_of(from_right[-1], row.shape)], axis=1
    )
    near_motion = near_motion.transpose(2, 0, 1, 3).reshape(6, width)

    terms = 32
    fixed, reach = pl.pallas_call(
        functools.partial(fixed_kernel, width=width),
        out_shape=(
            jax.ShapeDtypeStruct((terms, width), F32), jax.ShapeDtypeStruct((6, lines, 128), F32),
        ),
        in_specs=vmem(5), out_specs=tuple(vmem(2)),
        scratch_shapes=[pltpu.VMEM((8 * terms, 128), F32), pltpu.VMEM((2 * terms, width), F32)],
        compiler_params=grant(8), name="fixed",
        cost_estimate=pl.CostEstimate(flops=10**9, bytes_accessed=2 * 10**7, transcendentals=0),
    )(slots, dirs_late, pops, rb, table)

    tall = rows + 2 * MARGIN
    potential, press = pl.pallas_call(
        relax_kernel,
        out_shape=(
            jax.ShapeDtypeStruct((depth, wide, 128), F32),
            jax.ShapeDtypeStruct((depth + 1, wide, 128), F32),
        ),
        in_specs=[pl.BlockSpec(memory_space=pltpu.HBM)] + vmem(2), out_specs=tuple(vmem(2)),
        scratch_shapes=[
            pltpu.VMEM((2, layers + 3, tall, 128), F32),
            pltpu.VMEM((2, layers + 3, tall, 128), F32),
            pltpu.VMEM((2, layers + 1, rows, 128), F32),
            pltpu.VMEM((2, 7, layers + 1, rows, 128), F32),
            pltpu.VMEM((2, GROUPS + 2, tall, 128), F32),
            pltpu.VMEM((2, GROUPS + 2, tall, 128), F32),
            pltpu.VMEM((2, GROUPS, rows, 128), F32),
            pltpu.VMEM((2, 7, GROUPS, rows, 128), F32),
            pltpu.SemaphoreType.DMA((6,)),
        ],
        compiler_params=grant(48), name="relax",
    )(split, from_left, from_right)

    lanes = -(-width // 128) * 128
    fixed, near_motion = [
        jnp.pad(part, ((0, -part.shape[0] % 8), (0, lanes - width))) for part in (fixed, near_motion)
    ]
    devices = count_x * count_y
    smem = pl.BlockSpec(memory_space=pltpu.SMEM)
    pressed = pl.pallas_call(
        functools.partial(press_kernel, per_tile=per_tile),
        out_shape=jax.ShapeDtypeStruct((devices, 16, 128), F32),
        in_specs=[smem, smem] + vmem(7), out_specs=vmem(1)[0],
        scratch_shapes=[
            pltpu.VMEM((64, 128), F32), pltpu.VMEM((9 * 16, per_tile), F32),
            pltpu.VMEM((8, lanes), F32),
        ],
        compiler_params=grant(8), name="press",
    )(
        row_low, control, keys, arm0.reshape(lines, 128), arm1.reshape(lines, 128),
        table, press.reshape(-1, 128), fixed, near_motion,
    )

    partials = lax.all_to_all(pressed, ("gx", "gy"), 0, 0)

    report, link_out = pl.pallas_call(
        functools.partial(reflect_kernel, per_tile=per_tile, counts=(count_x, count_y)),
        out_shape=(
            jax.ShapeDtypeStruct((6, per_tile), F32), jax.ShapeDtypeStruct((lines, 128), F32),
        ),
        in_specs=[smem] + vmem(5), out_specs=tuple(vmem(2)), compiler_params=grant(6),
        scratch_shapes=[pltpu.VMEM((len(AROUND), 8, lanes), F32)], name="reflect",
    )(control, partials, slots, reach, pops, near_motion)
    return potential, report, link_out.reshape(link_pop.shape)


def solution(mesh):
    placed = (
        P(None, "gx", "gy"),
        P(None, "gx", "gy"),
        P(None, "gx", "gy"),
        P(None, ("gx", "gy")),
        P(None, ("gx", "gy")),
        P("gx", "gy", None),
        P("gx", "gy", None),
        P("gx", "gy", None),
        P("gx", "gy", None),
        P("gx", "gy", None),
        P(None, "gx", "gy", None),
    )
    return jax.shard_map(
        shards,
        mesh=mesh,
        in_specs=placed,
        out_specs=(P(None, "gx", "gy"), P(None, ("gx", "gy")), P("gx", "gy", None)),
        check_vma=False,
    )
```
